32 devices in a mesh: ctx: 2 (over y), head: 4 (over x, core), video: 4 (over z).
Axes of the slice: x: 2, y: 2, z: 4, core: 2. Of those that a mesh axis runs over, the one named last changes fastest.
Arguments:
- attention_qkv: bfloat16 [3, 4, 256, 3072], P(None, 'video', 'ctx', 'head'), may hold values from -8 to 8
- inner_qkv: bfloat16 [3, 4, 256, 3072], P(None, 'video', 'ctx', 'head'), may hold values from -3 to 3
- learn_rate: float32 [4, 48, 256], P('video', 'head', 'ctx'), may hold values from 0.001 to 0.01
- segment_id: int32 [4, 256], P('video'), may hold values from 0 to 3, never falling along the last dimension, each value on 1 to 128 neighbouring positions
- video_length: int32 [4], P('video'), may hold values from 128 to 256, as said below
- gate_alpha: float32 [3072], P('head'), may hold values from -1.5 to 1.5
- inner_gain: float32 [48, 64], P('head'), may hold values from 0.5 to 1.5
- inner_shift: float32 [48, 64], P('head'), may hold values from -3 to 3
- first_weight: bfloat16 [48, 64, 256], P('head'), may hold values from -0.75 to 0.75
- first_bias: float32 [48, 256], P('head'), may hold values from -3 to 3
- second_weight: bfloat16 [48, 256, 64], P('head'), may hold values from -0.375 to 0.375
- second_bias: float32 [48, 64], P('head'), may hold values from -3 to 3
- out_weight: bfloat16 [3072, 3072], P('head', 'video'), may hold values from -0.109375 to 0.109375
Outputs:
- mixed: bfloat16 [4, 256, 3072], P('video', 'ctx', 'head')
The draws below stay inside these ranges and needn't reach their ends.
Inputs may be any that keep to these rules, and one draw needn't show every extreme that they name: `segment_id`: segment numbers never fall along a video; each segment holds 1 to 128 positions and some segment exactly 128. `video_length`: some video is live in all 256 positions.
All inputs are finite; a program needn't handle non-finite values.
Results may differ from the reference program's by a relative error of at most 0.017.
Values may be sent and summed in bfloat16 or wider, within the bound.
A program may use at most 64 MiB of HBM per device.

```python
import math
import jax
import jax.numpy as jnp
import numpy as np
from jax import lax

HEADS = 48
HD = 64
D = 3072
INNER = 256
MB = 64
TOK_DEV = 128
SEQ = 256
VIDEOS = 4
N_CTX = 2
N_HEAD = 4


def draw_attention_qkv(key, part):
    base_draw = jnp.clip(jax.random.normal(key, (3, VIDEOS, SEQ, D), jnp.float32), -4.0, 4.0)
    return base_draw.astype(jnp.bfloat16)


def draw_video_length(key, part):
    drawn_len = jax.random.randint(key, (VIDEOS,), SEQ // 2, SEQ + 1)
    longest = jax.random.randint(jax.random.fold_in(key, 5), (), 0, VIDEOS)
    return jnp.where(jnp.arange(VIDEOS) == longest, SEQ, drawn_len).astype(jnp.int32)


def level_of(rng, extent, shards, low, largest):
    factor_of, own = 1.0, jax.random.fold_in(rng, 6)
    for axis_at, parts in shards:
        heights = jnp.exp(jax.random.uniform(jax.random.fold_in(own, axis_at), (parts,), jnp.float32, low / len(shards), largest / len(shards)))
        factor_of = factor_of * jnp.repeat(heights, extent[axis_at] // parts).reshape([-1 if axis == axis_at else 1 for axis in range(len(extent))])
    return factor_of


def profile(count, total, bound, slope):
    loads = [(1 << 20) // math.isqrt(rank ** slope) + 1 for rank in range(2, count + 1)]
    surplus, counts = total - bound - (count - 1), [1] * (count - 1)
    while surplus > 0:
        candidates = [i for i in range(count - 1) if counts[i] < bound]
        mass, remaining = sum([loads[i] for i in candidates]), surplus
        for i in candidates:
            extra = min(bound - counts[i], max(1, remaining * loads[i] // mass), surplus)
            counts[i] = counts[i] + extra
            surplus = surplus - extra
    return np.array([bound] + counts)


def ragged(stream_key, count, total, limit, lean):
    if count == 2:
        one = jax.random.randint(stream_key, (), max(1, total - limit), min(limit, total - 1) + 1)
        return jnp.stack([one, total - one])
    lengths = jnp.asarray(profile(count, total, limit, lean), jnp.int32)
    twos = (count - 1) // 2
    donor, taker = lengths[1:1 + 2 * twos:2], lengths[2:2 + 2 * twos:2]
    slack = jnp.minimum(donor - 1, limit - taker)
    passed = jax.random.randint(jax.random.fold_in(stream_key, 1), (twos,), 0, 1 << 20) % (slack + 1)
    lengths = lengths.at[1:1 + 2 * twos:2].set(donor - passed).at[2:2 + 2 * twos:2].set(taker + passed)
    return lengths[jax.random.permutation(jax.random.fold_in(stream_key, 2), count)]


def noise(key, extent, scale, limit, shards=(), kind=jnp.bfloat16):
    level = level_of(key, extent, shards, -0.22, 0.18) if shards else 1.0
    values = jax.random.normal(key, extent, jnp.float32) * scale * level
    return jnp.minimum(jnp.maximum(values, -limit), limit).astype(kind)


def setup_inputs(seed: int = 0) -> dict:
    streams_of = jax.random.split(jax.random.key(seed), 14)
    attention_qkv = draw_attention_qkv(jax.random.fold_in(streams_of[13], 71), 0)
    inner_qkv = noise(streams_of[1], (3, VIDEOS, SEQ, D), 0.5, 3.0, ((1, 4), (2, 2), (3, 4)))
    learn_rate = jnp.clip(jnp.exp(math.log(0.01) - 2.30258502 * jax.random.uniform(streams_of[2], (VIDEOS, HEADS, SEQ), jnp.float32) ** level_of(streams_of[2], (VIDEOS, HEADS, SEQ), ((0, 4), (1, 4), (2, 2)), -0.2, 0.2)), 0.001, 0.01)
    segment_id = jax.vmap(lambda own: jnp.searchsorted(jnp.cumsum(ragged(own, 2 * N_CTX, SEQ, TOK_DEV, 0)), jnp.arange(SEQ), side="right"))(jax.random.split(streams_of[3], VIDEOS)).reshape((VIDEOS, SEQ)).astype(jnp.int32)
    video_length = draw_video_length(jax.random.fold_in(streams_of[13], 71), 0)
    gate_alpha = jnp.clip(jax.random.uniform(streams_of[5], (D,), jnp.float32, -1.5, 1.5) * level_of(streams_of[5], (D,), ((0, 4),), -0.4, 0.0), -1.5, 1.5)
    inner_gain = jnp.clip(1.0 + 0.1 * jax.random.normal(streams_of[6], (HEADS, HD), jnp.float32), 0.5, 1.5)
    inner_shift = noise(streams_of[7], (HEADS, HD), 0.5, 3.0, ((0, 4),), jnp.float32)
    first_weight = noise(streams_of[8], (HEADS, HD, INNER), HD ** -0.5, 0.75, ((0, 4),))
    first_bias = noise(streams_of[9], (HEADS, INNER), 0.5, 3.0, ((0, 4),), jnp.float32)
    second_weight = noise(streams_of[10], (HEADS, INNER, HD), INNER ** -0.5, 0.375, ((0, 4),))
    second_bias = noise(streams_of[11], (HEADS, HD), 0.5, 3.0, ((0, 4),), jnp.float32)
    out_weight = noise(streams_of[12], (D, D), D ** -0.5, 0.109375, ((0, 4), (1, 4)))
    return dict(attention_qkv=attention_qkv, inner_qkv=inner_qkv, learn_rate=learn_rate, segment_id=segment_id, video_length=video_length, gate_alpha=gate_alpha, inner_gain=inner_gain, inner_shift=inner_shift, first_weight=first_weight, first_bias=first_bias, second_weight=second_weight, second_bias=second_bias, out_weight=out_weight)


gelu_scale = 0.7978845608028654
gelu_cubic = 0.044715

def matmul_high(first_op, second_op):
    return jnp.matmul(first_op, second_op, precision=lax.Precision.HIGHEST)

def gelu_pair(entries):
    inner_arg = gelu_scale * (entries + gelu_cubic * entries * entries * entries)
    tanh_val = jnp.tanh(inner_arg)
    act_val = 0.5 * entries * (1.0 + tanh_val)
    slope_val = 0.5 * (1.0 + tanh_val) + 0.5 * entries * (1.0 - tanh_val * tanh_val) * gelu_scale * (1.0 + 3.0 * gelu_cubic * entries * entries)
    return (act_val, slope_val)

def layer_stats(summed):
    center = summed - lax.optimization_barrier(jnp.mean(summed, axis=-1, keepdims=True))
    variance = lax.optimization_barrier(jnp.mean(center * center, axis=-1, keepdims=True))
    inv_std = lax.rsqrt(variance + 1e-06)
    return (center * inv_std, inv_std)

def lower_mask(row_count):
    row_ids = lax.broadcasted_iota(jnp.int32, (row_count, row_count), 0)
    col_ids = lax.broadcasted_iota(jnp.int32, (row_count, row_count), 1)
    return (row_ids >= col_ids).astype(jnp.float32)

def inner_update(inner_state, key_mb, value_mb, rate_mb, norm_gain, norm_shift):
    weight_one, bias_one, weight_two, bias_two = inner_state
    hidden_pre = matmul_high(key_mb, weight_one) + bias_one
    hidden_act, hidden_slope = gelu_pair(hidden_pre)
    output_pre = matmul_high(hidden_act, weight_two) + bias_two
    normed, inv_std = layer_stats(output_pre)
    residual_err = norm_gain * normed + norm_shift - (value_mb - key_mb)
    scaled_err = residual_err * norm_gain
    grad_two = inv_std * (scaled_err - lax.optimization_barrier(jnp.mean(scaled_err, axis=-1, keepdims=True)) - normed * lax.optimization_barrier(jnp.mean(scaled_err * normed, axis=-1, keepdims=True)))
    grad_one = matmul_high(grad_two, weight_two.T) * hidden_slope
    grad_one = grad_one * rate_mb[:, None]
    grad_two = grad_two * rate_mb[:, None]
    new_state = (weight_one - matmul_high(key_mb.T, grad_one), bias_one - lax.optimization_barrier(jnp.sum(grad_one, axis=0)), weight_two - matmul_high(hidden_act.T, grad_two), bias_two - lax.optimization_barrier(jnp.sum(grad_two, axis=0)))
    return ((grad_one, hidden_act, grad_two), new_state)

def query_side(inner_state, query_mb, key_mb, grad_pack, norm_gain, norm_shift):
    weight_one, bias_one, weight_two, bias_two = inner_state
    grad_one, hidden_act, grad_two = grad_pack
    causal = lower_mask(query_mb.shape[0])
    first_kernel = (matmul_high(query_mb, key_mb.T) + 1.0) * causal
    query_pre = matmul_high(query_mb, weight_one) + bias_one - matmul_high(first_kernel, grad_one)
    query_act, unused_slope = gelu_pair(query_pre)
    second_kernel = (matmul_high(query_act, hidden_act.T) + 1.0) * causal
    query_out = matmul_high(query_act, weight_two) + bias_two - matmul_high(second_kernel, grad_two)
    normed, unused_inv = layer_stats(query_out)
    return query_mb + norm_gain * normed + norm_shift

def head_chain(inner_state, queries, key_rows, values, rate_vals, norm_gain, norm_shift):

    def stepper(loop_state, inputs):
        query_mb, key_mb, value_mb, rate_mb = inputs
        grad_pack, new_state = inner_update(loop_state, key_mb, value_mb, rate_mb, norm_gain, norm_shift)
        return (new_state, query_side(loop_state, query_mb, key_mb, grad_pack, norm_gain, norm_shift))
    final_state, outputs = lax.scan(stepper, inner_state, (queries, key_rows, values, rate_vals))
    return outputs

def attend_block(query_blk, key_ext, value_ext, allowed):
    query_float = query_blk.astype(jnp.float32)
    key_float = key_ext.astype(jnp.float32)
    value_float = value_ext.astype(jnp.float32)
    scores = jnp.einsum('qhd,khd->hqk', query_float, key_float) * HD ** (-0.5)
    scores = jnp.where(allowed[None], scores, -1e+30)
    row_max = lax.optimization_barrier(jnp.max(scores, axis=-1, keepdims=True))
    exp_scores = jnp.exp(scores - row_max)
    soft_weights = (exp_scores / lax.optimization_barrier(jnp.sum(exp_scores, axis=-1, keepdims=True))).astype(jnp.bfloat16)
    soft_float = lax.optimization_barrier(soft_weights).astype(jnp.float32)
    return jnp.einsum('hqk,khd->qhd', soft_float, value_float)

def video_attention(attention_video, segment_row, length_val):
    pad_rows = jnp.zeros((TOK_DEV, D), attention_video.dtype)
    key_pad = jnp.concatenate([pad_rows, attention_video[1], pad_rows], axis=0)
    value_pad = jnp.concatenate([pad_rows, attention_video[2], pad_rows], axis=0)
    fill_ids = jnp.full((TOK_DEV,), -1, jnp.int32)
    seg_pad = jnp.concatenate([fill_ids, segment_row.astype(jnp.int32), fill_ids])

    def one_block(block_index):
        start_row = (block_index * TOK_DEV).astype(jnp.int32)
        query_blk = lax.dynamic_slice_in_dim(attention_video[0], start_row, TOK_DEV, 0).reshape(TOK_DEV, HEADS, HD)
        key_ext = lax.dynamic_slice_in_dim(key_pad, start_row, 3 * TOK_DEV, 0).reshape(3 * TOK_DEV, HEADS, HD)
        value_ext = lax.dynamic_slice_in_dim(value_pad, start_row, 3 * TOK_DEV, 0).reshape(3 * TOK_DEV, HEADS, HD)
        key_seg = lax.dynamic_slice_in_dim(seg_pad, start_row, 3 * TOK_DEV, 0)
        query_seg = lax.dynamic_slice_in_dim(segment_row.astype(jnp.int32), start_row, TOK_DEV, 0)
        query_pos = start_row + jnp.arange(TOK_DEV, dtype=jnp.int32)
        key_pos = start_row - TOK_DEV + jnp.arange(3 * TOK_DEV, dtype=jnp.int32)
        allowed = (key_seg[None, :] == query_seg[:, None]) & ((key_pos[None, :] < length_val) | (key_pos[None, :] == query_pos[:, None]))
        return attend_block(query_blk, key_ext, value_ext, allowed).reshape(TOK_DEV, D)
    blocks = lax.map(one_block, jnp.arange(N_CTX, dtype=jnp.int32))
    return blocks.reshape(SEQ, D)

def reference(attention_qkv, inner_qkv, learn_rate, segment_id, video_length, gate_alpha, inner_gain, inner_shift, first_weight, first_bias, second_weight, second_bias, out_weight):
    positions = jnp.arange(SEQ, dtype=jnp.int32)
    live_rows = (positions[None, :] < video_length[:, None]).astype(jnp.float32)
    attended = jnp.stack([video_attention(attention_qkv[:, video_idx], segment_id[video_idx], video_length[video_idx]) for video_idx in range(VIDEOS)])
    qkv_heads = inner_qkv.astype(jnp.float32).reshape(3, VIDEOS, SEQ, HEADS, HD).transpose(0, 1, 3, 2, 4).reshape(3, VIDEOS, HEADS, SEQ // MB, MB, HD)
    rate_vals = (learn_rate * live_rows[:, None, :]).reshape(VIDEOS, HEADS, SEQ // MB, MB)
    init_state = (first_weight.astype(jnp.float32), first_bias, second_weight.astype(jnp.float32), second_bias)
    per_head = jax.vmap(head_chain)
    per_video = jax.vmap(per_head, in_axes=(None, 0, 0, 0, 0, None, None))
    inner_out = per_video(init_state, qkv_heads[0], qkv_heads[1], qkv_heads[2], rate_vals, inner_gain, inner_shift)
    inner_flat = inner_out.reshape(VIDEOS, HEADS, SEQ, HD).transpose(0, 2, 1, 3).reshape(VIDEOS, SEQ, D)
    combined = ((attended + jnp.tanh(gate_alpha) * inner_flat) * live_rows[:, :, None]).astype(jnp.bfloat16)
    flat_rows = combined.reshape(VIDEOS * SEQ, D)
    block_width = D // N_HEAD
    mixed_sum = jnp.zeros((VIDEOS * SEQ, D), jnp.float32)
    for block_idx in range(N_HEAD):
        lower_col = block_idx * block_width
        partial_prod = jnp.dot(flat_rows[:, lower_col:lower_col + block_width], out_weight[lower_col:lower_col + block_width], preferred_element_type=jnp.float32)
        rounded_part = lax.optimization_barrier(partial_prod.astype(jnp.bfloat16)).astype(jnp.float32)
        mixed_sum = mixed_sum + rounded_part
    return mixed_sum.astype(jnp.bfloat16).reshape(VIDEOS, SEQ, D)
```

```python
from functools import partial

import jax
import jax.numpy as jnp
import numpy as np
from jax import lax
from jax.experimental import pallas as pl
from jax.experimental.pallas import tpu as pltpu
from jax.sharding import PartitionSpec as P

HD = 64
MB = 64


gelu_scale = 0.7978845608028654
gelu_cubic = 0.044715


def with_halo(cells, sides, width):
    for axis, dim in sides:
        count = lax.axis_size(axis)
        ends = count - 1
        head = lax.slice_in_dim(cells, 0, width, axis=dim)
        tail = lax.slice_in_dim(cells, cells.shape[dim] - width, cells.shape[dim], axis=dim)
        cells = jnp.concatenate(
            [
                lax.ppermute(tail, axis, [(i, (i + 1) % count) for i in range(ends)]),
                cells,
                lax.ppermute(head, axis, [((i + 1) % count, i) for i in range(ends)]),
            ],
            axis=dim,
        )
    return cells


def matmul_high(first_op, second_op):
    return jnp.matmul(first_op, second_op, precision=lax.Precision.HIGHEST)


def gelu_pair(entries):
    inner_arg = gelu_scale * (entries + gelu_cubic * entries * entries * entries)
    tanh_val = jnp.tanh(inner_arg)
    act_val = 0.5 * entries * (1.0 + tanh_val)
    slope_val = 0.5 * (1.0 + tanh_val) + 0.5 * entries * (
        1.0 - tanh_val * tanh_val
    ) * gelu_scale * (1.0 + 3.0 * gelu_cubic * entries * entries)
    return (act_val, slope_val)


def layer_stats(summed):
    center = summed - jnp.mean(summed, axis=-1, keepdims=True)
    variance = jnp.mean(center * center, axis=-1, keepdims=True)
    inv_std = lax.rsqrt(variance + 1e-06)
    return (center * inv_std, inv_std)


def lower_mask(row_count):
    row_ids = lax.broadcasted_iota(jnp.int32, (row_count, row_count), 0)
    col_ids = lax.broadcasted_iota(jnp.int32, (row_count, row_count), 1)
    return (row_ids >= col_ids).astype(jnp.float32)


def inner_update(inner_state, key_mb, value_mb, rate_mb, norm_gain, norm_shift):
    weight_one, bias_one, weight_two, bias_two = inner_state
    hidden_pre = matmul_high(key_mb, weight_one) + bias_one
    hidden_act, hidden_slope = gelu_pair(hidden_pre)
    output_pre = matmul_high(hidden_act, weight_two) + bias_two
    normed, inv_std = layer_stats(output_pre)
    residual_err = norm_gain * normed + norm_shift - (value_mb - key_mb)
    scaled_err = residual_err * norm_gain
    grad_two = inv_std * (
        scaled_err
        - jnp.mean(scaled_err, axis=-1, keepdims=True)
        - normed * jnp.mean(scaled_err * normed, axis=-1, keepdims=True)
    )
    grad_one = matmul_high(grad_two, weight_two.T) * hidden_slope
    grad_one = grad_one * rate_mb[:, None]
    grad_two = grad_two * rate_mb[:, None]
    new_state = (
        weight_one - matmul_high(key_mb.T, grad_one),
        bias_one - jnp.sum(grad_one, axis=0),
        weight_two - matmul_high(hidden_act.T, grad_two),
        bias_two - jnp.sum(grad_two, axis=0),
    )
    return ((grad_one, hidden_act, grad_two), new_state)


def query_side(inner_state, query_mb, key_mb, grad_pack, norm_gain, norm_shift):
    weight_one, bias_one, weight_two, bias_two = inner_state
    grad_one, hidden_act, grad_two = grad_pack
    causal = lower_mask(query_mb.shape[0])
    first_kernel = (matmul_high(query_mb, key_mb.T) + 1.0) * causal
    query_pre = matmul_high(query_mb, weight_one) + bias_one - matmul_high(first_kernel, grad_one)
    query_act, unused_slope = gelu_pair(query_pre)
    second_kernel = (matmul_high(query_act, hidden_act.T) + 1.0) * causal
    query_out = matmul_high(query_act, weight_two) + bias_two - matmul_high(second_kernel, grad_two)
    normed, unused_inv = layer_stats(query_out)
    return query_mb + norm_gain * normed + norm_shift


def chain_scan(
    keep_queries, inner_state, queries, key_rows, values, rate_vals, norm_gain, norm_shift
):

    def stepper(loop_state, inputs):
        query_mb, key_mb, value_mb, rate_mb = inputs
        grad_pack, new_state = inner_update(
            loop_state, key_mb, value_mb, rate_mb, norm_gain, norm_shift
        )
        return (
            new_state,
            query_side(loop_state, query_mb, key_mb, grad_pack, norm_gain, norm_shift),
        )

    return lax.scan(stepper, inner_state, (queries, key_rows, values, rate_vals))


def pad_heads(array_in, total_heads, fill_value):
    extra = total_heads - array_in.shape[0]
    filler = jnp.full((extra,) + array_in.shape[1:], fill_value, array_in.dtype)
    return jnp.concatenate([array_in, filler], axis=0)


LANE = 128
MESH_ID = pl.DeviceIdType.MESH


def dot_nn(left, right):
    return lax.dot_general(
        left, right, (((1,), (0,)), ((), ())), preferred_element_type=jnp.float32
    )


def dot_nt(left, right):
    return lax.dot_general(
        left, right, (((1,), (1,)), ((), ())), preferred_element_type=jnp.float32
    )


def dot_tn(left, right):
    return lax.dot_general(
        left, right, (((0,), (0,)), ((), ())), preferred_element_type=jnp.float32
    )


def gelu_parts(entries):
    square = entries * entries
    inner_arg = entries * (gelu_scale + gelu_scale * gelu_cubic * square)
    half = 0.5 + 0.5 * jnp.tanh(inner_arg)
    return (square, half, entries * half)


def gelu_only(entries):
    return gelu_parts(entries)[2]


def gelu_and_slope(entries):
    square, half, act_val = gelu_parts(entries)
    ramp = 2.0 * gelu_scale + 6.0 * gelu_scale * gelu_cubic * square
    return (act_val, half + act_val * (1.0 - half) * ramp)


def half_mean(cells, left):
    first = jnp.sum(jnp.where(left, cells, 0.0), axis=-1, keepdims=True)
    second = jnp.sum(jnp.where(left, 0.0, cells), axis=-1, keepdims=True)
    return jnp.where(left, first, second) * (1.0 / HD)


def split_heads(cells, left):
    wide = cells.astype(jnp.float32)
    return jnp.concatenate(
        [jnp.where(left, wide, 0.0), jnp.where(left, 0.0, wide)], axis=0
    ).astype(cells.dtype)


def fused_kernel(
    aqkv,
    iqkv,
    rate,
    first_w,
    second_w,
    out_w,
    seg,
    length,
    gate,
    gain,
    shift,
    first_b,
    second_b,
    out,
    a_rows,
    i_rows,
    rates,
    fw,
    sw,
    ow,
    lefts,
    rights,
    w2m,
    w2b,
    b1,
    b2,
    gate_s,
    gain_s,
    shift_s,
    rate_s,
    averager,
    pickers,
    tri_pair,
    bias,
    inner,
    comb,
    gathered,
    parts,
    arrived,
    total,
    landed,
    load_sem,
    y_send,
    y_recv,
    back_send,
    back_recv,
    z_send,
    z_recv,
    own_sem,
    r_send,
    r_recv,
    t_send,
    t_recv,
    low_sem,
    high_sem,
):
    slabs, _, seq, _ = a_rows.shape
    tok = aqkv.shape[2]
    hidden = first_b.shape[1]
    count = lax.axis_size("head")
    c = lax.axis_index("ctx")
    h = lax.axis_index("head")
    v = lax.axis_index("video")
    other = 1 - c
    mine = pl.multiple_of(c * tok, tok)
    theirs = pl.multiple_of(other * tok, tok)
    pairs_heads = 2 * slabs

    def columns(owner, slab):
        return pl.ds(pl.multiple_of((owner * slabs + slab) * LANE, LANE), LANE)

    loads = []
    for slab in range(slabs):
        loads.append(
            pltpu.make_async_copy(
                iqkv.at[:, 0, :, columns(c, slab)],
                i_rows.at[slab, :, pl.ds(mine, tok), :],
                load_sem.at[slab],
            )
        )
    loads.append(pltpu.make_async_copy(rate, rates.at[c], load_sem.at[2 * slabs]))
    loads.append(
        pltpu.make_async_copy(
            first_w.at[pl.ds(c * pairs_heads, pairs_heads)], fw, load_sem.at[2 * slabs + 1]
        )
    )
    loads.append(
        pltpu.make_async_copy(
            second_w.at[pl.ds(c * pairs_heads, pairs_heads)], sw, load_sem.at[2 * slabs + 2]
        )
    )
    a_loads = [
        pltpu.make_async_copy(
            aqkv.at[:, 0, :, columns(c, slab)],
            a_rows.at[slab, :, pl.ds(mine, tok), :],
            load_sem.at[slabs + slab],
        )
        for slab in range(slabs)
    ]
    ow_load = pltpu.make_async_copy(out_w, ow, load_sem.at[2 * slabs + 3])
    for copy in loads + a_loads + [ow_load]:
        copy.start()

    barrier = pltpu.get_barrier_semaphore()
    pl.semaphore_signal(
        barrier, inc=1, device_id={"ctx": other}, device_id_type=MESH_ID
    )
    below, above = v > 0, v < count - 1
    for step in range(1, count):
        pl.semaphore_signal(
            barrier,
            inc=1,
            device_id={"head": lax.rem(h + step, count)},
            device_id_type=MESH_ID,
        )

    def tell(semaphore, inside, video):
        @pl.when(inside)
        def _():
            pl.semaphore_signal(
                semaphore, inc=1, device_id={"video": video}, device_id_type=MESH_ID
            )

    tell(barrier, below, v - 1)
    tell(barrier, above, v + 1)
    pl.semaphore_wait(barrier, count + (v + count - 1) // count + (2 * count - 2 - v) // count)

    def to_partner(src, dst, send, recv):
        return pltpu.make_async_remote_copy(
            src_ref=src,
            dst_ref=dst,
            send_sem=send,
            recv_sem=recv,
            device_id={"ctx": other},
            device_id_type=MESH_ID,
        )

    rate_out = to_partner(
        rate, rates.at[c], y_send.at[2 * slabs], y_recv.at[2 * slabs]
    )
    rate_out.start()
    i_out = [
        to_partner(
            iqkv.at[:, 0, :, columns(other, slab)],
            i_rows.at[slab, :, pl.ds(mine, tok), :],
            y_send.at[slab],
            y_recv.at[slab],
        )
        for slab in range(slabs)
    ]
    a_out = [
        to_partner(
            aqkv.at[:, 0, :, columns(other, slab)],
            a_rows.at[slab, :, pl.ds(mine, tok), :],
            y_send.at[slabs + slab],
            y_recv.at[slabs + slab],
        )
        for slab in range(slabs)
    ]
    for first, second in zip(i_out, a_out):
        first.start()
        second.start()

    tell(low_sem, v == 0, v + 1)
    tell(high_sem, v == count - 1, v - 1)

    def pass_on(stage):
        for semaphore, here, video, last in (
            (low_sem, v == stage, v + 1, above),
            (high_sem, v == count - 1 - stage, v - 1, below),
        ):

            @pl.when(here)
            def _(semaphore=semaphore):
                pl.semaphore_wait(semaphore, 1)

            tell(semaphore, jnp.logical_and(here, last), video)

    seq_ids = lax.broadcasted_iota(jnp.int32, (seq, seq), 1)
    row_ids = lax.broadcasted_iota(jnp.int32, (seq, seq), 0)
    len_val = length[0]
    segs = jnp.broadcast_to(seg[...].astype(jnp.float32), (seq, seq))
    allowed = (segs == segs.T) & ((seq_ids < len_val) | (seq_ids == row_ids))
    bias[...] = jnp.where(allowed, 0.0, -1e30)
    live = (lax.broadcasted_iota(jnp.int32, (seq, LANE), 0) < len_val).astype(jnp.float32)
    left = lax.broadcasted_iota(jnp.int32, (MB, LANE), 1) < HD
    left_seq = lax.broadcasted_iota(jnp.int32, (seq, LANE), 1) < HD
    pair_row_ids = lax.broadcasted_iota(jnp.int32, (LANE, LANE), 0)
    pair_col_ids = lax.broadcasted_iota(jnp.int32, (LANE, LANE), 1)
    same = (pair_row_ids < HD) == (pair_col_ids < HD)
    tri_pair[...] = jnp.where(same & (pair_row_ids >= pair_col_ids), 1.0, 0.0)
    averager[...] = jnp.where(same, 1.0 / HD, 0.0).astype(jnp.bfloat16)
    pickers[...] = jnp.where(pair_row_ids == pair_col_ids, 1.0, 0.0).astype(jnp.bfloat16)
    batches = seq // MB
    before = seq - MB
    lane_ids = lax.broadcasted_iota(jnp.int32, (MB, LANE), 1)
    batch_row_ids = lax.broadcasted_iota(jnp.int32, (MB, LANE), 0)

    gate_s[...] = jnp.tanh(gate[...].reshape(1, gate.shape[0]))

    for copy in loads:
        copy.wait()
    pass_on(1)

    def pair_row(ref, head):
        return jnp.concatenate([ref[pl.ds(head, 1), :], ref[pl.ds(head + 1, 1), :]], axis=1)

    for slab in range(slabs):
        head = c * pairs_heads + 2 * slab
        gain_s[slab] = pair_row(gain, head)
        shift_s[slab] = pair_row(shift, head)
        bias_two = pair_row(second_b, head)
        b2[slab, 0] = bias_two - half_mean(bias_two, left[:1])
        for half in range(2):
            b1[slab, half] = first_b[pl.ds(head + half, 1), :]
            rights[slab, half, 0:before] = jnp.zeros((before, hidden), jnp.bfloat16)
            rights[slab, half, before:seq] = fw[2 * slab + half]
            whole = sw[2 * slab + half].astype(jnp.float32)
            whole = whole - jnp.mean(whole, axis=0, keepdims=True)
            w2m[slab, half * HD : (half + 1) * HD] = whole
            w2b[slab, 0, half * HD : (half + 1) * HD] = whole.astype(jnp.bfloat16)

    rate_out.wait_recv()
    for slab in range(slabs):
        head = c * pairs_heads + 2 * slab
        for part in range(seq // tok):
            rows = slice(part * tok, (part + 1) * tok)
            row_a, row_b = rates[part, head], rates[part, head + 1]
            upright = jnp.concatenate(
                [jnp.broadcast_to(row_a, (HD, tok)), jnp.broadcast_to(row_b, (HD, tok))], axis=0
            )
            rate_s[slab, rows] = -(upright.T * live[rows])

    def average(cells):
        return dot_nn(cells.astype(jnp.bfloat16), averager[...])

    def parted(cells):
        return jnp.concatenate(
            [jnp.where(left, cells, 0.0), jnp.where(left, 0.0, cells)], axis=0
        ).astype(jnp.bfloat16)

    def joined(cells):
        return jnp.where(left, cells[:MB], cells[MB:])

    def masked_tile(cells, base, limit, causal):
        cols = np.arange(LANE)[None, :] + base
        reach = limit + (np.arange(MB)[:, None] if causal else -1)
        allowed = np.broadcast_to((cols <= reach) & (cols < before), (MB, LANE))
        kept = allowed | (cols >= before)
        if not kept.any():
            return jnp.zeros((MB, LANE), jnp.bfloat16)
        col_ids = lane_ids + base
        if allowed.all():
            cells = cells + 1.0
        elif allowed.any():
            inside = col_ids <= (limit + batch_row_ids if causal else limit - 1)
            inside = inside & (col_ids < before)
            cells = cells + jnp.where(inside, 1.0, 0.0)
            if not kept.all():
                cells = jnp.where(inside | (col_ids >= before), cells, 0.0)
        elif not kept.all():
            cells = jnp.where(col_ids >= before, cells, 0.0)
        return cells.astype(jnp.bfloat16)

    def inner_setup(slab):
        query, key, value = (i_rows[slab, kind] for kind in range(3))
        key_f = key.astype(jnp.float32)
        key_parts = (
            jnp.where(left_seq, key_f, 0.0).astype(jnp.bfloat16),
            jnp.where(left_seq, 0.0, key_f).astype(jnp.bfloat16),
        )
        both = jnp.concatenate([key, query], axis=0)
        for half in range(2):
            against = jnp.concatenate(
                [key_parts[half][:before], pickers[half * HD : (half + 1) * HD]], axis=0
            )
            product = dot_nt(both, against)
            for block in range(2 * batches):
                rows = slice(block * MB, (block + 1) * MB)
                for base in range(0, seq, LANE):
                    lefts[slab, half, rows, base : base + LANE] = masked_tile(
                        product[rows, base : base + LANE],
                        base,
                        (block % batches) * MB,
                        block >= batches,
                    )
        norm_gain = gain_s[slab]
        pull = norm_gain * (shift_s[slab] - (value.astype(jnp.float32) - key_f))
        last = slice(before, seq)
        own = dot_nt(query[last], jnp.concatenate([part[last] for part in key_parts], axis=0))
        own = ((jnp.concatenate([own, own], axis=0) + 1.0) * tri_pair[...]).astype(jnp.bfloat16)
        return pull, average(pull), own

    def query_step(slab, batch, pre, hidden_b, pair_two):
        rows = slice(batch * MB, (batch + 1) * MB)
        query_act = gelu_only(pre).astype(jnp.bfloat16)
        second_kernel = (dot_nt(query_act, hidden_b) + 1.0) * tri_pair[...]
        query_out = dot_nt(query_act, w2b[slab, batch]) + dot_nn(
            second_kernel.astype(jnp.bfloat16), pair_two
        )
        query_out = joined(query_out) + b2[slab, batch]
        inv_std = lax.rsqrt(average(query_out * query_out) + 1e-06)
        query = i_rows[slab, 0, rows, :].astype(jnp.float32)
        inner[slab, rows, :] = query + gain_s[slab] * (query_out * inv_std) + shift_s[slab]

    def inner_step(slab, batch, prepared, waiting):
        pull, pull_mean, own = prepared
        rows = slice(batch * MB, (batch + 1) * MB)
        final = batch == batches - 1
        blocks = [batch] + ([batches + batch - 1] if batch else []) + (
            [batches + batch] if final else []
        )
        pres = []
        for half in range(2):
            used = jnp.concatenate(
                [lefts[slab, half, at * MB : (at + 1) * MB] for at in blocks], axis=0
            )
            pres.append(dot_nn(used, rights[slab, half]) + b1[slab, half])

        def picked(at):
            return jnp.concatenate([pre[at * MB : (at + 1) * MB] for pre in pres], axis=0)

        hidden_act, slope = gelu_and_slope(picked(0))
        hidden_b = hidden_act.astype(jnp.bfloat16)
        norm_gain = gain_s[slab]
        squared_gain = norm_gain * norm_gain
        bias_two = b2[slab, batch]
        center = joined(dot_nt(hidden_b, w2b[slab, batch])) + bias_two
        square = center * center
        pulled = pull[rows]
        means = average(
            jnp.concatenate(
                [square, squared_gain * center, squared_gain * square, pulled * center], axis=0
            )
        )
        var, lin, quad, cross = (means[at * MB : (at + 1) * MB] for at in range(4))
        inv_std = lax.rsqrt(var + 1e-06)
        normed = center * inv_std
        scaled = squared_gain * normed + pulled
        along = inv_std * (inv_std * quad + cross)
        grad_two = inv_std * (scaled - (inv_std * lin + pull_mean[rows]) - normed * along)
        two = grad_two * rate_s[slab, rows]
        pair_two = parted(two)
        one = (dot_nn(pair_two, w2b[slab, batch]) * slope).astype(jnp.bfloat16)
        if not final:
            for half in range(2):
                rights[slab, half, rows] = one[half * MB : (half + 1) * MB]
            updated = w2m[slab] + dot_tn(pair_two, hidden_b)
            w2m[slab] = updated
            w2b[slab, batch + 1] = updated.astype(jnp.bfloat16)
            b2[slab, batch + 1] = bias_two + jnp.sum(two, axis=0, keepdims=True)
        if waiting is not None:
            query_step(slab, batch - 1, picked(1), *waiting)
        if final:
            pre = picked(len(blocks) - 1) + dot_nn(own, one)
            query_step(slab, batch, pre, hidden_b, pair_two)
        return (hidden_b, pair_two)

    def to_video(src, video, spot, step):
        return pltpu.make_async_remote_copy(
            src_ref=src,
            dst_ref=gathered.at[v, spot],
            send_sem=z_send.at[spot, step - 1],
            recv_sem=z_recv.at[spot, step - 1],
            device_id={"video": video},
            device_id_type=MESH_ID,
        )

    def spread(src, spot):
        copies = []
        for step in range(count - 1, 0, -1):
            copy = to_video(src, lax.rem(v + step, count), spot, step)
            copy.start()
            copies.append(copy)
        return copies

    z_out = []
    backs = []
    owns = []
    for slab in range(slabs):
        i_out[slab].wait_recv()
        if slab == 0:
            for stage in range(2, count - 1):
                pass_on(stage)

        prepared = inner_setup(slab)
        waiting = None
        for batch in range(batches // 2):
            waiting = inner_step(slab, batch, prepared, waiting)
        if slab == 0 and count > 2:
            pass_on(count - 1)
        a_loads[slab].wait()
        a_out[slab].wait_recv()
        for batch in range(batches // 2, batches):
            waiting = inner_step(slab, batch, prepared, waiting)
        query, key, value = (a_rows[slab, kind] for kind in range(3))
        scores = dot_nt(split_heads(query, left_seq), key) * HD ** (-0.5)
        halves = []
        for part in range(2):
            mine_scores = scores[part * seq : (part + 1) * seq] + bias[...]
            top = jnp.max(mine_scores, axis=-1, keepdims=True)
            weights = jnp.exp(mine_scores - top)
            mass = jnp.sum(weights, axis=-1, keepdims=True)
            halves.append(dot_nn(weights.astype(jnp.bfloat16), value) / mass)
        attended = jnp.where(left_seq, halves[0], halves[1])
        gate_row = gate_s[:, columns(c, slab)]
        comb[slab] = ((attended + gate_row * inner[slab]) * live).astype(jnp.bfloat16)
        spot = c * slabs + slab
        back = to_partner(
            comb.at[slab, pl.ds(theirs, tok), :],
            gathered.at[v, spot],
            back_send.at[slab],
            back_recv.at[slab],
        )
        back.start()
        backs.append(back)
        own = pltpu.make_async_copy(
            comb.at[slab, pl.ds(mine, tok), :], gathered.at[v, spot], own_sem.at[slab]
        )
        own.start()
        owns.append(own)
        z_out += spread(comb.at[slab, pl.ds(mine, tok), :], spot)
        if slab:
            backs[slab - 1].wait_recv()
            far = other * slabs + slab - 1
            z_out += spread(gathered.at[v, far], far)
    backs[slabs - 1].wait_recv()
    far = other * slabs + slabs - 1
    z_out += spread(gathered.at[v, far], far)
    for own in owns:
        own.wait()
    ow_load.wait()

    def owner_of(video):
        return lax.rem(video, 2) * (count // 2) + video // 2

    def video_of(head):
        return lax.rem(head, count // 2) * 2 + head // (count // 2)

    chunks, _, _, chunk = parts.shape
    toward = 1 - 2 * (v // (count // 2))

    def part_copy(video, at):
        head = owner_of(video)
        ahead = lax.rem(head - h + count, count)
        slot = lax.rem(ahead + count - 1, count)
        return head, pltpu.make_async_remote_copy(
            src_ref=parts.at[at, video],
            dst_ref=arrived.at[at, slot],
            send_sem=r_send.at[at, slot],
            recv_sem=r_recv.at[at, slot],
            device_id={"head": head},
            device_id_type=MESH_ID,
        )

    videos = []
    for near in range(count):
        video = lax.rem(v + toward * near + count, count)
        videos.append(video)
        if near:
            step = lax.rem(v - video + count, count)
            for spot in range(2 * slabs):
                pltpu.make_async_remote_copy(
                    src_ref=gathered.at[video, spot],
                    dst_ref=gathered.at[video, spot],
                    send_sem=z_send.at[spot, step - 1],
                    recv_sem=z_recv.at[spot, step - 1],
                    device_id={"video": video},
                    device_id_type=MESH_ID,
                ).wait_recv()
        rows_video = jnp.concatenate(
            [gathered[video, spot] for spot in range(2 * slabs)], axis=1
        )
        for at in range(chunks):
            piece = dot_nn(rows_video, ow[:, at * chunk : (at + 1) * chunk])
            parts[at, video] = piece.astype(jnp.bfloat16)
            head, copy = part_copy(video, at)

            @pl.when(head != h)
            def _(copy=copy):
                copy.start()

    to_head, to_v = v, video_of(h)
    stays = (to_head == h) & (to_v == v)
    finals = []
    for at in range(chunks):
        for step in range(1, count):
            pltpu.make_async_remote_copy(
                src_ref=arrived.at[at, step - 1],
                dst_ref=arrived.at[at, step - 1],
                send_sem=r_send.at[at, step - 1],
                recv_sem=r_recv.at[at, step - 1],
                device_id={"head": lax.rem(h + step, count)},
                device_id_type=MESH_ID,
            ).wait_recv()
        summed = parts[at, video_of(h)].astype(jnp.float32)
        for step in range(count - 1):
            summed = summed + arrived[at, step].astype(jnp.float32)
        total[at] = summed.astype(jnp.bfloat16)
        final = pltpu.make_async_remote_copy(
            src_ref=total.at[at],
            dst_ref=landed.at[at],
            send_sem=t_send.at[at],
            recv_sem=t_recv.at[at],
            device_id={"head": to_head, "video": to_v},
            device_id_type=MESH_ID,
        )

        @pl.when(stays)
        def _(at=at):
            landed[at] = total[at]

        @pl.when(jnp.logical_not(stays))
        def _(final=final):
            final.start()

        finals.append(final)

    @pl.when(jnp.logical_not(stays))
    def _():
        for final in finals:
            final.wait()

    for at in range(chunks):
        out[0, :, at * chunk : (at + 1) * chunk] = landed[at]

    for copy in [rate_out] + i_out + a_out + backs + z_out:
        copy.wait_send()
    for video in videos:
        for at in range(chunks):
            head, copy = part_copy(video, at)

            @pl.when(head != h)
            def _(copy=copy):
                copy.wait_send()


def fused_on_device(
    attention_qkv,
    inner_qkv,
    learn_rate,
    segment_id,
    video_length,
    gate_alpha,
    inner_gain,
    inner_shift,
    first_weight,
    first_bias,
    second_weight,
    second_bias,
    out_weight,
):
    tok = attention_qkv.shape[2]
    width_dev = attention_qkv.shape[3]
    count = lax.axis_size("head")
    ctx_count = lax.axis_size("ctx")
    seq = tok * ctx_count
    slabs = width_dev // LANE // ctx_count
    heads = width_dev // HD
    hidden = first_weight.shape[2]
    columns = out_weight.shape[1]
    chunk = 2 * LANE if columns % (2 * LANE) == 0 else columns
    chunks = columns // chunk
    half = jnp.bfloat16
    full = jnp.float32
    hbm = pl.BlockSpec(memory_space=pl.ANY)
    vmem = pl.BlockSpec(memory_space=pltpu.VMEM)
    smem = pl.BlockSpec(memory_space=pltpu.SMEM)
    dma = pltpu.SemaphoreType.DMA
    return pl.pallas_call(
        fused_kernel,
        out_shape=jax.ShapeDtypeStruct((1, tok, columns), half),
        in_specs=[hbm] * 6 + [vmem, smem] + [vmem] * 5,
        out_specs=vmem,
        scratch_shapes=[
            pltpu.VMEM((slabs, 3, seq, LANE), half),
            pltpu.VMEM((slabs, 3, seq, LANE), half),
            pltpu.VMEM((ctx_count, heads, 1, tok), full),
            pltpu.VMEM((2 * slabs,) + first_weight.shape[1:], half),
            pltpu.VMEM((2 * slabs,) + second_weight.shape[:0:-1], half),
            pltpu.VMEM(out_weight.shape, half),
            pltpu.VMEM((slabs, 2, 2 * seq, seq), half),
            pltpu.VMEM((slabs, 2, seq, hidden), half),
            pltpu.VMEM((slabs, LANE, hidden), full),
            pltpu.VMEM((slabs, seq // MB, LANE, hidden), half),
            pltpu.VMEM((slabs, 2, 1, hidden), full),
            pltpu.VMEM((slabs, seq // MB, 1, LANE), full),
            pltpu.VMEM((1, width_dev), full),
            pltpu.VMEM((slabs, 1, LANE), full),
            pltpu.VMEM((slabs, 1, LANE), full),
            pltpu.VMEM((slabs, seq, LANE), full),
            pltpu.VMEM((LANE, LANE), half),
            pltpu.VMEM((LANE, LANE), half),
            pltpu.VMEM((LANE, LANE), full),
            pltpu.VMEM((seq, seq), full),
            pltpu.VMEM((slabs, seq, LANE), full),
            pltpu.VMEM((slabs, seq, LANE), half),
            pltpu.VMEM((count, 2 * slabs, tok, LANE), half),
            pltpu.VMEM((chunks, count, tok, chunk), half),
            pltpu.VMEM((chunks, count - 1, tok, chunk), half),
            pltpu.VMEM((chunks, tok, chunk), half),
            pltpu.VMEM((chunks, tok, chunk), half),
            dma((2 * slabs + 4,)),
            dma((2 * slabs + 1,)),
            dma((2 * slabs + 1,)),
            dma((slabs,)),
            dma((slabs,)),
            dma((2 * slabs, count - 1)),
            dma((2 * slabs, count - 1)),
            dma((slabs,)),
            dma((chunks, count - 1)),
            dma((chunks, count - 1)),
            dma((chunks,)),
            dma((chunks,)),
            pltpu.SemaphoreType.REGULAR,
            pltpu.SemaphoreType.REGULAR,
        ],
        compiler_params=pltpu.CompilerParams(
            collective_id=0, has_side_effects=True, vmem_limit_bytes=60 * 1024 * 1024
        ),
    )(
        attention_qkv,
        inner_qkv,
        learn_rate.transpose(1, 0, 2),
        first_weight,
        second_weight.transpose(0, 2, 1),
        out_weight,
        segment_id,
        video_length,
        gate_alpha,
        inner_gain,
        inner_shift,
        first_bias,
        second_bias,
    )


def general_on_device(
    attention_qkv,
    inner_qkv,
    learn_rate,
    segment_id,
    video_length,
    gate_alpha,
    inner_gain,
    inner_shift,
    first_weight,
    first_bias,
    second_weight,
    second_bias,
    out_weight,
):
    tok_count = attention_qkv.shape[2]
    width_dev = attention_qkv.shape[3]
    heads_dev = width_dev // HD
    ctx_index = lax.axis_index("ctx")
    ctx_count = lax.axis_size("ctx")
    positions = ctx_index * tok_count + jnp.arange(tok_count, dtype=jnp.int32)
    length_val = video_length[0]
    live_rows = (positions < length_val).astype(jnp.float32)
    kv_pair = attention_qkv[1:, 0]
    kv_wide = with_halo(kv_pair, (("ctx", 1),), tok_count)
    key_pos = (ctx_index - 1) * tok_count + jnp.arange(3 * tok_count, dtype=jnp.int32)
    seg_row = segment_id[0]
    fill_ids = jnp.full((tok_count,), -1, jnp.int32)
    seg_pad = jnp.concatenate([fill_ids, seg_row, fill_ids])
    key_seg = lax.dynamic_slice_in_dim(seg_pad, ctx_index * tok_count, 3 * tok_count, 0)
    query_seg = lax.dynamic_slice_in_dim(seg_row, ctx_index * tok_count, tok_count, 0)
    allowed = (key_seg[None, :] == query_seg[:, None]) & (
        (key_pos[None, :] < length_val) | (key_pos[None, :] == positions[:, None])
    )
    query_heads = attention_qkv[0, 0].reshape(tok_count, heads_dev, HD)
    key_heads = kv_wide[0].reshape(3 * tok_count, heads_dev, HD)
    value_heads = kv_wide[1].reshape(3 * tok_count, heads_dev, HD)
    scores = jnp.einsum(
        "qhd,khd->hqk", query_heads, key_heads, preferred_element_type=jnp.float32
    ) * HD ** (-0.5)
    scores = jnp.where(allowed[None], scores, -1e30)
    row_max = jnp.max(scores, axis=-1, keepdims=True)
    exp_scores = jnp.exp(scores - row_max)
    soft_weights = (exp_scores / jnp.sum(exp_scores, axis=-1, keepdims=True)).astype(jnp.bfloat16)
    attended = jnp.einsum(
        "hqk,khd->qhd", soft_weights, value_heads, preferred_element_type=jnp.float32
    ).reshape(tok_count, width_dev)
    init_state = (
        first_weight.astype(jnp.float32),
        first_bias,
        second_weight.astype(jnp.float32),
        second_bias,
    )
    rate_rows = learn_rate[0] * live_rows[None, :]
    heads_each = -(-heads_dev // ctx_count)
    heads_padded = heads_each * ctx_count
    rows_heads = inner_qkv[:, 0].reshape(3, tok_count, heads_dev, HD)
    rows_padded = jnp.concatenate(
        [rows_heads, jnp.zeros((3, tok_count, heads_padded - heads_dev, HD), rows_heads.dtype)],
        axis=2,
    )
    rates_padded = pad_heads(rate_rows, heads_padded, 0.0)
    whole_rows = lax.all_to_all(rows_padded, "ctx", split_axis=2, concat_axis=1, tiled=True)
    whole_rates = lax.all_to_all(rates_padded, "ctx", split_axis=0, concat_axis=1, tiled=True)
    seq_count = whole_rows.shape[1]
    full_batches = seq_count // MB
    local_qkv = (
        whole_rows.astype(jnp.float32)
        .transpose(0, 2, 1, 3)
        .reshape(3, heads_each, full_batches, MB, HD)
    )
    local_rates = whole_rates.reshape(heads_each, full_batches, MB)
    first_head = ctx_index * heads_each
    local_gain = lax.dynamic_slice_in_dim(
        pad_heads(inner_gain, heads_padded, 1.0), first_head, heads_each, 0
    )
    local_shift = lax.dynamic_slice_in_dim(
        pad_heads(inner_shift, heads_padded, 0.0), first_head, heads_each, 0
    )
    local_state = tuple(
        (
            lax.dynamic_slice_in_dim(
                pad_heads(piece_arr, heads_padded, 0.0), first_head, heads_each, 0
            )
            for piece_arr in init_state
        )
    )
    unused_final, saved_local = jax.vmap(partial(chain_scan, True))(
        local_state, local_qkv[0], local_qkv[1], local_qkv[2], local_rates, local_gain, local_shift
    )
    out_rows = saved_local.reshape(heads_each, seq_count, HD).transpose(1, 0, 2)
    back_rows = lax.all_to_all(
        out_rows.astype(jnp.bfloat16), "ctx", split_axis=0, concat_axis=1, tiled=True
    ).astype(out_rows.dtype)
    inner_flat = back_rows[:, :heads_dev].reshape(tok_count, width_dev)
    combined = ((attended + jnp.tanh(gate_alpha) * inner_flat) * live_rows[:, None]).astype(
        jnp.bfloat16
    )
    terms = jnp.dot(
        combined,
        lax.all_gather(out_weight, "video", axis=1, tiled=True),
        preferred_element_type=jnp.float32,
    )
    mixed = lax.psum_scatter(terms.astype(jnp.bfloat16), "head", scatter_dimension=1, tiled=True)
    return mixed[None]


def solution(mesh):
    placed = (
        P(None, "video", "ctx", "head"),
        P(None, "video", "ctx", "head"),
        P("video", "head", "ctx"),
        P("video", None),
        P("video"),
        P("head"),
        P("head", None),
        P("head", None),
        P("head", None, None),
        P("head", None),
        P("head", None, None),
        P("head", None),
        P("head", "video"),
    )
    shape = mesh.shape
    fused = shape["ctx"] == 2 and shape["head"] == shape["video"] and shape["head"] % 2 == 0

    def on_device(*args):
        heads_dev = args[0].shape[3] // HD
        if fused and heads_dev % (2 * shape["ctx"]) == 0 and args[0].shape[2] % 128 == 0:
            return fused_on_device(*args)
        return general_on_device(*args)

    return jax.shard_map(
        on_device, mesh=mesh, in_specs=placed, out_specs=P("video", "ctx", "head"), check_vma=False
    )
```

```python
from functools import partial

import jax
import jax.numpy as jnp
import numpy as np
from jax import lax
from jax.experimental import pallas as pl
from jax.experimental.pallas import tpu as pltpu
from jax.sharding import PartitionSpec as P

HD = 64
MB = 64


gelu_scale = 0.7978845608028654
gelu_cubic = 0.044715


def with_halo(cells, sides, width):
    for axis, dim in sides:
        count = lax.axis_size(axis)
        ends = count - 1
        head = lax.slice_in_dim(cells, 0, width, axis=dim)
        tail = lax.slice_in_dim(cells, cells.shape[dim] - width, cells.shape[dim], axis=dim)
        cells = jnp.concatenate(
            [
                lax.ppermute(tail, axis, [(i, (i + 1) % count) for i in range(ends)]),
                cells,
                lax.ppermute(head, axis, [((i + 1) % count, i) for i in range(ends)]),
            ],
            axis=dim,
        )
    return cells


def matmul_high(first_op, second_op):
    return jnp.matmul(first_op, second_op, precision=lax.Precision.HIGHEST)


def gelu_pair(entries):
    inner_arg = gelu_scale * (entries + gelu_cubic * entries * entries * entries)
    tanh_val = jnp.tanh(inner_arg)
    act_val = 0.5 * entries * (1.0 + tanh_val)
    slope_val = 0.5 * (1.0 + tanh_val) + 0.5 * entries * (
        1.0 - tanh_val * tanh_val
    ) * gelu_scale * (1.0 + 3.0 * gelu_cubic * entries * entries)
    return (act_val, slope_val)


def layer_stats(summed):
    center = summed - jnp.mean(summed, axis=-1, keepdims=True)
    variance = jnp.mean(center * center, axis=-1, keepdims=True)
    inv_std = lax.rsqrt(variance + 1e-06)
    return (center * inv_std, inv_std)


def lower_mask(row_count):
    row_ids = lax.broadcasted_iota(jnp.int32, (row_count, row_count), 0)
    col_ids = lax.broadcasted_iota(jnp.int32, (row_count, row_count), 1)
    return (row_ids >= col_ids).astype(jnp.float32)


def inner_update(inner_state, key_mb, value_mb, rate_mb, norm_gain, norm_shift):
    weight_one, bias_one, weight_two, bias_two = inner_state
    hidden_pre = matmul_high(key_mb, weight_one) + bias_one
    hidden_act, hidden_slope = gelu_pair(hidden_pre)
    output_pre = matmul_high(hidden_act, weight_two) + bias_two
    normed, inv_std = layer_stats(output_pre)
    residual_err = norm_gain * normed + norm_shift - (value_mb - key_mb)
    scaled_err = residual_err * norm_gain
    grad_two = inv_std * (
        scaled_err
        - jnp.mean(scaled_err, axis=-1, keepdims=True)
        - normed * jnp.mean(scaled_err * normed, axis=-1, keepdims=True)
    )
    grad_one = matmul_high(grad_two, weight_two.T) * hidden_slope
    grad_one = grad_one * rate_mb[:, None]
    grad_two = grad_two * rate_mb[:, None]
    new_state = (
        weight_one - matmul_high(key_mb.T, grad_one),
        bias_one - jnp.sum(grad_one, axis=0),
        weight_two - matmul_high(hidden_act.T, grad_two),
        bias_two - jnp.sum(grad_two, axis=0),
    )
    return ((grad_one, hidden_act, grad_two), new_state)


def query_side(inner_state, query_mb, key_mb, grad_pack, norm_gain, norm_shift):
    weight_one, bias_one, weight_two, bias_two = inner_state
    grad_one, hidden_act, grad_two = grad_pack
    causal = lower_mask(query_mb.shape[0])
    first_kernel = (matmul_high(query_mb, key_mb.T) + 1.0) * causal
    query_pre = matmul_high(query_mb, weight_one) + bias_one - matmul_high(first_kernel, grad_one)
    query_act, unused_slope = gelu_pair(query_pre)
    second_kernel = (matmul_high(query_act, hidden_act.T) + 1.0) * causal
    query_out = matmul_high(query_act, weight_two) + bias_two - matmul_high(second_kernel, grad_two)
    normed, unused_inv = layer_stats(query_out)
    return query_mb + norm_gain * normed + norm_shift


def chain_scan(
    keep_queries, inner_state, queries, key_rows, values, rate_vals, norm_gain, norm_shift
):

    def stepper(loop_state, inputs):
        query_mb, key_mb, value_mb, rate_mb = inputs
        grad_pack, new_state = inner_update(
            loop_state, key_mb, value_mb, rate_mb, norm_gain, norm_shift
        )
        return (
            new_state,
            query_side(loop_state, query_mb, key_mb, grad_pack, norm_gain, norm_shift),
        )

    return lax.scan(stepper, inner_state, (queries, key_rows, values, rate_vals))


def pad_heads(array_in, total_heads, fill_value):
    extra = total_heads - array_in.shape[0]
    filler = jnp.full((extra,) + array_in.shape[1:], fill_value, array_in.dtype)
    return jnp.concatenate([array_in, filler], axis=0)


LANE = 128
MESH_ID = pl.DeviceIdType.MESH


def dot_nn(left, right):
    return lax.dot_general(
        left, right, (((1,), (0,)), ((), ())), preferred_element_type=jnp.float32
    )


def dot_nt(left, right):
    return lax.dot_general(
        left, right, (((1,), (1,)), ((), ())), preferred_element_type=jnp.float32
    )


def dot_tn(left, right):
    return lax.dot_general(
        left, right, (((0,), (0,)), ((), ())), preferred_element_type=jnp.float32
    )


def gelu_parts(entries):
    square = entries * entries
    inner_arg = entries * (gelu_scale + gelu_scale * gelu_cubic * square)
    half = 0.5 + 0.5 * jnp.tanh(inner_arg)
    return (square, half, entries * half)


def gelu_only(entries):
    return gelu_parts(entries)[2]


def gelu_and_slope(entries):
    square, half, act_val = gelu_parts(entries)
    ramp = 2.0 * gelu_scale + 6.0 * gelu_scale * gelu_cubic * square
    return (act_val, half + act_val * (1.0 - half) * ramp)


def half_mean(cells, left):
    first = jnp.sum(jnp.where(left, cells, 0.0), axis=-1, keepdims=True)
    second = jnp.sum(jnp.where(left, 0.0, cells), axis=-1, keepdims=True)
    return jnp.where(left, first, second) * (1.0 / HD)


def split_heads(cells, left):
    wide = cells.astype(jnp.float32)
    return jnp.concatenate(
        [jnp.where(left, wide, 0.0), jnp.where(left, 0.0, wide)], axis=0
    ).astype(cells.dtype)


def fused_kernel(
    aqkv,
    iqkv,
    rate,
    first_w,
    second_w,
    out_w,
    seg,
    length,
    gate,
    gain,
    shift,
    first_b,
    second_b,
    out,
    a_rows,
    i_rows,
    rates,
    fw,
    sw,
    ow,
    lefts,
    rights,
    w2m,
    w2b,
    b1,
    b2,
    gate_s,
    gain_s,
    shift_s,
    rate_s,
    averager,
    pickers,
    tri_pair,
    bias,
    inner,
    comb,
    gathered,
    sums,
    parts,
    beside,
    crossing,
    arrived,
    total,
    landed,
    load_sem,
    y_send,
    y_recv,
    back_send,
    back_recv,
    z_send,
    z_recv,
    own_sem,
    s_send,
    s_recv,
    r_send,
    r_recv,
    t_send,
    t_recv,
    low_sem,
    high_sem,
):
    slabs, _, seq, _ = a_rows.shape
    tok = aqkv.shape[2]
    hidden = first_b.shape[1]
    count = lax.axis_size("head")
    c = lax.axis_index("ctx")
    h = lax.axis_index("head")
    v = lax.axis_index("video")
    other = 1 - c
    mine = pl.multiple_of(c * tok, tok)
    theirs = pl.multiple_of(other * tok, tok)
    pairs_heads = 2 * slabs

    def columns(owner, slab):
        return pl.ds(pl.multiple_of((owner * slabs + slab) * LANE, LANE), LANE)

    loads = []
    for slab in range(slabs):
        loads.append(
            pltpu.make_async_copy(
                iqkv.at[:, 0, :, columns(c, slab)],
                i_rows.at[slab, :, pl.ds(mine, tok), :],
                load_sem.at[slab],
            )
        )
    loads.append(pltpu.make_async_copy(rate, rates.at[c], load_sem.at[2 * slabs]))
    loads.append(
        pltpu.make_async_copy(
            first_w.at[pl.ds(c * pairs_heads, pairs_heads)], fw, load_sem.at[2 * slabs + 1]
        )
    )
    loads.append(
        pltpu.make_async_copy(
            second_w.at[pl.ds(c * pairs_heads, pairs_heads)], sw, load_sem.at[2 * slabs + 2]
        )
    )
    a_loads = [
        pltpu.make_async_copy(
            aqkv.at[:, 0, :, columns(c, slab)],
            a_rows.at[slab, :, pl.ds(mine, tok), :],
            load_sem.at[slabs + slab],
        )
        for slab in range(slabs)
    ]
    ow_load = pltpu.make_async_copy(out_w, ow, load_sem.at[2 * slabs + 3])
    for copy in loads + a_loads + [ow_load]:
        copy.start()

    barrier = pltpu.get_barrier_semaphore()
    pl.semaphore_signal(
        barrier, inc=1, device_id={"ctx": other}, device_id_type=MESH_ID
    )
    below, above = v > 0, v < count - 1
    for step in range(1, count):
        pl.semaphore_signal(
            barrier,
            inc=1,
            device_id={"head": lax.rem(h + step, count)},
            device_id_type=MESH_ID,
        )

    def tell(semaphore, inside, video):
        @pl.when(inside)
        def _():
            pl.semaphore_signal(
                semaphore, inc=1, device_id={"video": video}, device_id_type=MESH_ID
            )

    tell(barrier, below, v - 1)
    tell(barrier, above, v + 1)
    pl.semaphore_wait(barrier, count + (v + count - 1) // count + (2 * count - 2 - v) // count)

    def to_partner(src, dst, send, recv):
        return pltpu.make_async_remote_copy(
            src_ref=src,
            dst_ref=dst,
            send_sem=send,
            recv_sem=recv,
            device_id={"ctx": other},
            device_id_type=MESH_ID,
        )

    rate_out = to_partner(
        rate, rates.at[c], y_send.at[6 * slabs], y_recv.at[6 * slabs]
    )
    rate_out.start()

    def rows_out(source, target, slab, base):
        return [
            to_partner(
                source.at[kind, 0, :, columns(other, slab)],
                target.at[slab, kind, pl.ds(mine, tok), :],
                y_send.at[base + 3 * slab + kind],
                y_recv.at[base + 3 * slab + kind],
            )
            for kind in range(3)
        ]

    i_out = [rows_out(iqkv, i_rows, slab, 0) for slab in range(slabs)]
    a_out = [rows_out(aqkv, a_rows, slab, 3 * slabs) for slab in range(slabs)]
    early = max(slabs - 1, 1)

    def start_rows(part):
        for copies in zip(i_out[part], a_out[part]):
            for copy in copies[0] + copies[1]:
                copy.start()

    start_rows(slice(0, early))

    tell(low_sem, v == 0, v + 1)
    tell(high_sem, v == count - 1, v - 1)

    def pass_on(stage):
        for semaphore, here, video, last in (
            (low_sem, v == stage, v + 1, above),
            (high_sem, v == count - 1 - stage, v - 1, below),
        ):

            @pl.when(here)
            def _(semaphore=semaphore):
                pl.semaphore_wait(semaphore, 1)

            tell(semaphore, jnp.logical_and(here, last), video)

    seq_ids = lax.broadcasted_iota(jnp.int32, (seq, seq), 1)
    row_ids = lax.broadcasted_iota(jnp.int32, (seq, seq), 0)
    len_val = length[0]
    segs = jnp.broadcast_to(seg[...].astype(jnp.float32), (seq, seq))
    allowed = (segs == segs.T) & ((seq_ids < len_val) | (seq_ids == row_ids))
    bias[...] = jnp.where(allowed, 0.0, -1e30)
    live = (lax.broadcasted_iota(jnp.int32, (seq, LANE), 0) < len_val).astype(jnp.float32)
    left = lax.broadcasted_iota(jnp.int32, (MB, LANE), 1) < HD
    left_seq = lax.broadcasted_iota(jnp.int32, (seq, LANE), 1) < HD
    pair_row_ids = lax.broadcasted_iota(jnp.int32, (LANE, LANE), 0)
    pair_col_ids = lax.broadcasted_iota(jnp.int32, (LANE, LANE), 1)
    same = (pair_row_ids < HD) == (pair_col_ids < HD)
    tri_pair[...] = jnp.where(same & (pair_row_ids >= pair_col_ids), 1.0, 0.0)
    averager[...] = jnp.where(same, 1.0 / HD, 0.0).astype(jnp.bfloat16)
    pickers[...] = jnp.where(pair_row_ids == pair_col_ids, 1.0, 0.0).astype(jnp.bfloat16)
    batches = seq // MB
    before = seq - MB
    lane_ids = lax.broadcasted_iota(jnp.int32, (MB, LANE), 1)
    batch_row_ids = lax.broadcasted_iota(jnp.int32, (MB, LANE), 0)

    gate_s[...] = jnp.tanh(gate[...].reshape(1, gate.shape[0]))

    for copy in loads:
        copy.wait()
    pass_on(1)

    def pair_row(ref, head):
        return jnp.concatenate([ref[pl.ds(head, 1), :], ref[pl.ds(head + 1, 1), :]], axis=1)

    for slab in range(slabs):
        head = c * pairs_heads + 2 * slab
        gain_s[slab] = pair_row(gain, head)
        shift_s[slab] = pair_row(shift, head)
        bias_two = pair_row(second_b, head)
        b2[slab, 0] = bias_two - half_mean(bias_two, left[:1])
        for half in range(2):
            b1[slab, half] = first_b[pl.ds(head + half, 1), :]
            rights[slab, half, 0:before] = jnp.zeros((before, hidden), jnp.bfloat16)
            rights[slab, half, before:seq] = fw[2 * slab + half]
            whole = sw[2 * slab + half].astype(jnp.float32)
            whole = whole - jnp.mean(whole, axis=0, keepdims=True)
            w2m[slab, half * HD : (half + 1) * HD] = whole
            w2b[slab, 0, half * HD : (half + 1) * HD] = whole.astype(jnp.bfloat16)

    rate_out.wait_recv()
    for slab in range(slabs):
        head = c * pairs_heads + 2 * slab
        for part in range(seq // tok):
            rows = slice(part * tok, (part + 1) * tok)
            row_a, row_b = rates[part, head], rates[part, head + 1]
            upright = jnp.concatenate(
                [jnp.broadcast_to(row_a, (HD, tok)), jnp.broadcast_to(row_b, (HD, tok))], axis=0
            )
            rate_s[slab, rows] = -(upright.T * live[rows])

    def average(cells):
        return dot_nn(cells.astype(jnp.bfloat16), averager[...])

    def parted(cells):
        return jnp.concatenate(
            [jnp.where(left, cells, 0.0), jnp.where(left, 0.0, cells)], axis=0
        ).astype(jnp.bfloat16)

    def joined(cells):
        return jnp.where(left, cells[:MB], cells[MB:])

    def masked_tile(cells, base, limit, causal):
        cols = np.arange(LANE)[None, :] + base
        reach = limit + (np.arange(MB)[:, None] if causal else -1)
        allowed = np.broadcast_to((cols <= reach) & (cols < before), (MB, LANE))
        kept = allowed | (cols >= before)
        if not kept.any():
            return jnp.zeros((MB, LANE), jnp.bfloat16)
        col_ids = lane_ids + base
        if allowed.all():
            cells = cells + 1.0
        elif allowed.any():
            inside = col_ids <= (limit + batch_row_ids if causal else limit - 1)
            inside = inside & (col_ids < before)
            cells = cells + jnp.where(inside, 1.0, 0.0)
            if not kept.all():
                cells = jnp.where(inside | (col_ids >= before), cells, 0.0)
        elif not kept.all():
            cells = jnp.where(col_ids >= before, cells, 0.0)
        return cells.astype(jnp.bfloat16)

    def inner_setup(slab):
        query, key, value = (i_rows[slab, kind] for kind in range(3))
        key_f = key.astype(jnp.float32)
        key_parts = (
            jnp.where(left_seq, key_f, 0.0).astype(jnp.bfloat16),
            jnp.where(left_seq, 0.0, key_f).astype(jnp.bfloat16),
        )
        both = jnp.concatenate([key, query], axis=0)
        for half in range(2):
            against = jnp.concatenate(
                [key_parts[half][:before], pickers[half * HD : (half + 1) * HD]], axis=0
            )
            product = dot_nt(both, against)
            for block in range(2 * batches):
                rows = slice(block * MB, (block + 1) * MB)
                for base in range(0, seq, LANE):
                    lefts[slab, half, rows, base : base + LANE] = masked_tile(
                        product[rows, base : base + LANE],
                        base,
                        (block % batches) * MB,
                        block >= batches,
                    )
        norm_gain = gain_s[slab]
        pull = norm_gain * (shift_s[slab] - (value.astype(jnp.float32) - key_f))
        last = slice(before, seq)
        own = dot_nt(query[last], jnp.concatenate([part[last] for part in key_parts], axis=0))
        own = ((jnp.concatenate([own, own], axis=0) + 1.0) * tri_pair[...]).astype(jnp.bfloat16)
        return pull, average(pull), own

    def query_step(slab, batch, pre, hidden_b, pair_two):
        rows = slice(batch * MB, (batch + 1) * MB)
        query_act = gelu_only(pre).astype(jnp.bfloat16)
        second_kernel = (dot_nt(query_act, hidden_b) + 1.0) * tri_pair[...]
        query_out = dot_nt(query_act, w2b[slab, batch]) + dot_nn(
            second_kernel.astype(jnp.bfloat16), pair_two
        )
        query_out = joined(query_out) + b2[slab, batch]
        inv_std = lax.rsqrt(average(query_out * query_out) + 1e-06)
        query = i_rows[slab, 0, rows, :].astype(jnp.float32)
        inner[slab, rows, :] = query + gain_s[slab] * (query_out * inv_std) + shift_s[slab]

    def inner_step(slab, batch, prepared, waiting):
        pull, pull_mean, own = prepared
        rows = slice(batch * MB, (batch + 1) * MB)
        final = batch == batches - 1
        blocks = [batch] + ([batches + batch - 1] if batch else []) + (
            [batches + batch] if final else []
        )
        pres = []
        for half in range(2):
            used = jnp.concatenate(
                [lefts[slab, half, at * MB : (at + 1) * MB] for at in blocks], axis=0
            )
            pres.append(dot_nn(used, rights[slab, half]) + b1[slab, half])

        def picked(at):
            return jnp.concatenate([pre[at * MB : (at + 1) * MB] for pre in pres], axis=0)

        hidden_act, slope = gelu_and_slope(picked(0))
        hidden_b = hidden_act.astype(jnp.bfloat16)
        norm_gain = gain_s[slab]
        squared_gain = norm_gain * norm_gain
        bias_two = b2[slab, batch]
        center = joined(dot_nt(hidden_b, w2b[slab, batch])) + bias_two
        square = center * center
        pulled = pull[rows]
        means = average(
            jnp.concatenate(
                [square, squared_gain * center, squared_gain * square, pulled * center], axis=0
            )
        )
        var, lin, quad, cross = (means[at * MB : (at + 1) * MB] for at in range(4))
        inv_std = lax.rsqrt(var + 1e-06)
        normed = center * inv_std
        scaled = squared_gain * normed + pulled
        along = inv_std * (inv_std * quad + cross)
        grad_two = inv_std * (scaled - (inv_std * lin + pull_mean[rows]) - normed * along)
        two = grad_two * rate_s[slab, rows]
        pair_two = parted(two)
        one = (dot_nn(pair_two, w2b[slab, batch]) * slope).astype(jnp.bfloat16)
        if not final:
            for half in range(2):
                rights[slab, half, rows] = one[half * MB : (half + 1) * MB]
            updated = w2m[slab] + dot_tn(pair_two, hidden_b)
            w2m[slab] = updated
            w2b[slab, batch + 1] = updated.astype(jnp.bfloat16)
            b2[slab, batch + 1] = bias_two + jnp.sum(two, axis=0, keepdims=True)
        if waiting is not None:
            query_step(slab, batch - 1, picked(1), *waiting)
        if final:
            pre = picked(len(blocks) - 1) + dot_nn(own, one)
            query_step(slab, batch, pre, hidden_b, pair_two)
        return (hidden_b, pair_two)

    def to_video(src, video, spot, step):
        return pltpu.make_async_remote_copy(
            src_ref=src,
            dst_ref=gathered.at[v, spot],
            send_sem=z_send.at[spot, step - 1],
            recv_sem=z_recv.at[spot, step - 1],
            device_id={"video": video},
            device_id_type=MESH_ID,
        )

    def spread(src, spot):
        copies = []
        for step in range(1, count):
            copy = to_video(src, lax.rem(v + step, count), spot, step)
            copy.start()
            copies.append(copy)
        return copies

    z_out = []
    backs = []
    owns = []
    for slab in range(slabs):
        for copy in i_out[slab]:
            copy.wait_recv()
        if slab == 0:
            for stage in range(2, count - 1):
                pass_on(stage)
        prepared = inner_setup(slab)
        waiting = None
        for batch in range(batches // 2):
            waiting = inner_step(slab, batch, prepared, waiting)
        if slab == 0 and count > 2:
            pass_on(count - 1)
        a_loads[slab].wait()
        for copy in a_out[slab]:
            copy.wait_recv()
        query, key, value = (a_rows[slab, kind] for kind in range(3))
        scores = dot_nt(split_heads(query, left_seq), key) * HD ** (-0.5)
        halves = []
        for part in range(2):
            mine_scores = scores[part * seq : (part + 1) * seq] + bias[...]
            top = jnp.max(mine_scores, axis=-1, keepdims=True)
            weights = jnp.exp(mine_scores - top)
            mass = jnp.sum(weights, axis=-1, keepdims=True)
            halves.append(dot_nn(weights.astype(jnp.bfloat16), value) / mass)
        attended = jnp.where(left_seq, halves[0], halves[1])
        for batch in range(batches // 2, batches):
            if slab and batch == batches // 2:
                backs[slab - 1].wait_recv()
                far = other * slabs + slab - 1
                z_out += spread(gathered.at[v, far], far)
            waiting = inner_step(slab, batch, prepared, waiting)
        gate_row = gate_s[:, columns(c, slab)]
        comb[slab] = ((attended + gate_row * inner[slab]) * live).astype(jnp.bfloat16)
        spot = c * slabs + slab
        back = to_partner(
            comb.at[slab, pl.ds(theirs, tok), :],
            gathered.at[v, spot],
            back_send.at[slab],
            back_recv.at[slab],
        )
        back.start()
        backs.append(back)
        if slab == 0:
            start_rows(slice(early, slabs))
        own = pltpu.make_async_copy(
            comb.at[slab, pl.ds(mine, tok), :], gathered.at[v, spot], own_sem.at[slab]
        )
        own.start()
        owns.append(own)
        z_out += spread(comb.at[slab, pl.ds(mine, tok), :], spot)
    ow_load.wait()
    for own in owns[:-1]:
        own.wait()

    chunks, _, _, chunk = parts.shape
    toward = 1 - 2 * (v // (count // 2))
    videos = [lax.rem(v + toward * near + count, count) for near in range(count)]

    def z_wait(video, spots):
        step = lax.rem(v - video + count, count)
        for spot in spots:
            pltpu.make_async_remote_copy(
                src_ref=gathered.at[video, spot],
                dst_ref=gathered.at[video, spot],
                send_sem=z_send.at[spot, step - 1],
                recv_sem=z_recv.at[spot, step - 1],
                device_id={"video": video},
                device_id_type=MESH_ID,
            ).wait_recv()

    def rows_of(video, spots):
        return jnp.concatenate([gathered[video, spot] for spot in spots], axis=1)

    first_half = list(range(slabs - 1))
    second_half = list(range(slabs, 2 * slabs - 1))
    last_spots = [slabs - 1, 2 * slabs - 1]

    def begin(near):
        if slabs == 1:
            return
        video = videos[near]
        if near:
            z_wait(video, first_half + second_half)
        sums[near] = dot_nn(
            rows_of(video, first_half), ow[0 : (slabs - 1) * LANE]
        ) + dot_nn(
            rows_of(video, second_half), ow[slabs * LANE : (2 * slabs - 1) * LANE]
        )

    lane_of, core_of = h // 2, lax.rem(h, 2)
    sibling = 2 * lane_of + 1 - core_of
    across = 2 * (1 - lane_of) + core_of

    def owner_lane(video):
        return lax.rem(video + v, 2)

    def owner_core(video):
        return lax.rem(video // 2 + v // 2, 2)

    def owned(lane, core):
        return 2 * lax.rem(core + v // 2, 2) + lax.rem(lane + v, 2)

    def to_head_copy(src, dst, send, recv, head):
        return pltpu.make_async_remote_copy(
            src_ref=src,
            dst_ref=dst,
            send_sem=send,
            recv_sem=recv,
            device_id={"head": head},
            device_id_type=MESH_ID,
        )

    def part_copy(video, at):
        slot = lax.rem(owner_lane(video) + lane_of, 2)
        return to_head_copy(
            parts.at[at, video],
            beside.at[at, slot],
            s_send.at[at, slot],
            s_recv.at[at, slot],
            sibling,
        )

    def finish(near):
        video = videos[near]
        if near:
            z_wait(video, last_spots)
        rows_video = rows_of(video, last_spots)
        for at in range(chunks):
            cols = slice(at * chunk, (at + 1) * chunk)
            piece = dot_nn(
                rows_video,
                jnp.concatenate(
                    [ow[spot * LANE : (spot + 1) * LANE, cols] for spot in last_spots], axis=0
                ),
            )
            if slabs > 1:
                piece = piece + sums[near, :, cols]
            parts[at, video] = piece.astype(jnp.bfloat16)
            copy = part_copy(video, at)

            @pl.when(owner_core(video) != core_of)
            def _(copy=copy):
                copy.start()

    begin(0)
    backs[slabs - 1].wait_recv()
    far = other * slabs + slabs - 1
    z_out += spread(gathered.at[v, far], far)
    owns[-1].wait()
    finish(0)
    for near in range(1, count):
        begin(near)
    for near in range(1, count):
        finish(near)

    home, away = owned(lane_of, core_of), owned(1 - lane_of, core_of)
    x_out = []
    for at in range(chunks):
        part_copy(away, at).wait_recv()
        crossing[at] = (
            parts[at, away].astype(jnp.float32) + beside[at, 1].astype(jnp.float32)
        ).astype(jnp.bfloat16)
        copy = to_head_copy(
            crossing.at[at], arrived.at[at], r_send.at[at], r_recv.at[at], across
        )
        copy.start()
        x_out.append(copy)

    to_head, to_v = v, home
    stays = (to_head == h) & (to_v == v)
    finals = []
    for at in range(chunks):
        part_copy(home, at).wait_recv()
        summed = parts[at, home].astype(jnp.float32) + beside[at, 0].astype(jnp.float32)
        x_out[at].wait_recv()
        summed = summed + arrived[at].astype(jnp.float32)
        total[at] = summed.astype(jnp.bfloat16)
        final = pltpu.make_async_remote_copy(
            src_ref=total.at[at],
            dst_ref=landed.at[at],
            send_sem=t_send.at[at],
            recv_sem=t_recv.at[at],
            device_id={"head": to_head, "video": to_v},
            device_id_type=MESH_ID,
        )

        @pl.when(stays)
        def _(at=at):
            landed[at] = total[at]

        @pl.when(jnp.logical_not(stays))
        def _(final=final):
            final.start()

        finals.append(final)

    @pl.when(jnp.logical_not(stays))
    def _():
        for final in finals:
            final.wait()

    for at in range(chunks):
        out[0, :, at * chunk : (at + 1) * chunk] = landed[at]

    rows_sent = [copy for copies in i_out + a_out for copy in copies]
    for copy in [rate_out] + rows_sent + backs + z_out + x_out:
        copy.wait_send()
    for lane in range(2):
        for at in range(chunks):
            part_copy(owned(lane, 1 - core_of), at).wait_send()


def fused_on_device(
    attention_qkv,
    inner_qkv,
    learn_rate,
    segment_id,
    video_length,
    gate_alpha,
    inner_gain,
    inner_shift,
    first_weight,
    first_bias,
    second_weight,
    second_bias,
    out_weight,
):
    tok = attention_qkv.shape[2]
    width_dev = attention_qkv.shape[3]
    count = lax.axis_size("head")
    ctx_count = lax.axis_size("ctx")
    seq = tok * ctx_count
    slabs = width_dev // LANE // ctx_count
    heads = width_dev // HD
    hidden = first_weight.shape[2]
    columns = out_weight.shape[1]
    chunk = 2 * LANE if columns % (2 * LANE) == 0 else columns
    chunks = columns // chunk
    half = jnp.bfloat16
    full = jnp.float32
    hbm = pl.BlockSpec(memory_space=pl.ANY)
    vmem = pl.BlockSpec(memory_space=pltpu.VMEM)
    smem = pl.BlockSpec(memory_space=pltpu.SMEM)
    dma = pltpu.SemaphoreType.DMA
    return pl.pallas_call(
        fused_kernel,
        out_shape=jax.ShapeDtypeStruct((1, tok, columns), half),
        in_specs=[hbm] * 6 + [vmem, smem] + [vmem] * 5,
        out_specs=vmem,
        scratch_shapes=[
            pltpu.VMEM((slabs, 3, seq, LANE), half),
            pltpu.VMEM((slabs, 3, seq, LANE), half),
            pltpu.VMEM((ctx_count, heads, 1, tok), full),
            pltpu.VMEM((2 * slabs,) + first_weight.shape[1:], half),
            pltpu.VMEM((2 * slabs,) + second_weight.shape[:0:-1], half),
            pltpu.VMEM(out_weight.shape, half),
            pltpu.VMEM((slabs, 2, 2 * seq, seq), half),
            pltpu.VMEM((slabs, 2, seq, hidden), half),
            pltpu.VMEM((slabs, LANE, hidden), full),
            pltpu.VMEM((slabs, seq // MB, LANE, hidden), half),
            pltpu.VMEM((slabs, 2, 1, hidden), full),
            pltpu.VMEM((slabs, seq // MB, 1, LANE), full),
            pltpu.VMEM((1, width_dev), full),
            pltpu.VMEM((slabs, 1, LANE), full),
            pltpu.VMEM((slabs, 1, LANE), full),
            pltpu.VMEM((slabs, seq, LANE), full),
            pltpu.VMEM((LANE, LANE), half),
            pltpu.VMEM((LANE, LANE), half),
            pltpu.VMEM((LANE, LANE), full),
            pltpu.VMEM((seq, seq), full),
            pltpu.VMEM((slabs, seq, LANE), full),
            pltpu.VMEM((slabs, seq, LANE), half),
            pltpu.VMEM((count, 2 * slabs, tok, LANE), half),
            pltpu.VMEM((count, tok, columns), full),
            pltpu.VMEM((chunks, count, tok, chunk), half),
            pltpu.VMEM((chunks, 2, tok, chunk), half),
            pltpu.VMEM((chunks, tok, chunk), half),
            pltpu.VMEM((chunks, tok, chunk), half),
            pltpu.VMEM((chunks, tok, chunk), half),
            pltpu.VMEM((chunks, tok, chunk), half),
            dma((2 * slabs + 4,)),
            dma((6 * slabs + 1,)),
            dma((6 * slabs + 1,)),
            dma((slabs,)),
            dma((slabs,)),
            dma((2 * slabs, count - 1)),
            dma((2 * slabs, count - 1)),
            dma((slabs,)),
            dma((chunks, 2)),
            dma((chunks, 2)),
            dma((chunks,)),
            dma((chunks,)),
            dma((chunks,)),
            dma((chunks,)),
            pltpu.SemaphoreType.REGULAR,
            pltpu.SemaphoreType.REGULAR,
        ],
        compiler_params=pltpu.CompilerParams(
            collective_id=0, has_side_effects=True, vmem_limit_bytes=60 * 1024 * 1024
        ),
    )(
        attention_qkv,
        inner_qkv,
        learn_rate.transpose(1, 0, 2),
        first_weight,
        second_weight.transpose(0, 2, 1),
        out_weight,
        segment_id,
        video_length,
        gate_alpha,
        inner_gain,
        inner_shift,
        first_bias,
        second_bias,
    )


def general_on_device(
    attention_qkv,
    inner_qkv,
    learn_rate,
    segment_id,
    video_length,
    gate_alpha,
    inner_gain,
    inner_shift,
    first_weight,
    first_bias,
    second_weight,
    second_bias,
    out_weight,
):
    tok_count = attention_qkv.shape[2]
    width_dev = attention_qkv.shape[3]
    heads_dev = width_dev // HD
    ctx_index = lax.axis_index("ctx")
    ctx_count = lax.axis_size("ctx")
    positions = ctx_index * tok_count + jnp.arange(tok_count, dtype=jnp.int32)
    length_val = video_length[0]
    live_rows = (positions < length_val).astype(jnp.float32)
    kv_pair = attention_qkv[1:, 0]
    kv_wide = with_halo(kv_pair, (("ctx", 1),), tok_count)
    key_pos = (ctx_index - 1) * tok_count + jnp.arange(3 * tok_count, dtype=jnp.int32)
    seg_row = segment_id[0]
    fill_ids = jnp.full((tok_count,), -1, jnp.int32)
    seg_pad = jnp.concatenate([fill_ids, seg_row, fill_ids])
    key_seg = lax.dynamic_slice_in_dim(seg_pad, ctx_index * tok_count, 3 * tok_count, 0)
    query_seg = lax.dynamic_slice_in_dim(seg_row, ctx_index * tok_count, tok_count, 0)
    allowed = (key_seg[None, :] == query_seg[:, None]) & (
        (key_pos[None, :] < length_val) | (key_pos[None, :] == positions[:, None])
    )
    query_heads = attention_qkv[0, 0].reshape(tok_count, heads_dev, HD)
    key_heads = kv_wide[0].reshape(3 * tok_count, heads_dev, HD)
    value_heads = kv_wide[1].reshape(3 * tok_count, heads_dev, HD)
    scores = jnp.einsum(
        "qhd,khd->hqk", query_heads, key_heads, preferred_element_type=jnp.float32
    ) * HD ** (-0.5)
    scores = jnp.where(allowed[None], scores, -1e30)
    row_max = jnp.max(scores, axis=-1, keepdims=True)
    exp_scores = jnp.exp(scores - row_max)
    soft_weights = (exp_scores / jnp.sum(exp_scores, axis=-1, keepdims=True)).astype(jnp.bfloat16)
    attended = jnp.einsum(
        "hqk,khd->qhd", soft_weights, value_heads, preferred_element_type=jnp.float32
    ).reshape(tok_count, width_dev)
    init_state = (
        first_weight.astype(jnp.float32),
        first_bias,
        second_weight.astype(jnp.float32),
        second_bias,
    )
    rate_rows = learn_rate[0] * live_rows[None, :]
    heads_each = -(-heads_dev // ctx_count)
    heads_padded = heads_each * ctx_count
    rows_heads = inner_qkv[:, 0].reshape(3, tok_count, heads_dev, HD)
    rows_padded = jnp.concatenate(
        [rows_heads, jnp.zeros((3, tok_count, heads_padded - heads_dev, HD), rows_heads.dtype)],
        axis=2,
    )
    rates_padded = pad_heads(rate_rows, heads_padded, 0.0)
    whole_rows = lax.all_to_all(rows_padded, "ctx", split_axis=2, concat_axis=1, tiled=True)
    whole_rates = lax.all_to_all(rates_padded, "ctx", split_axis=0, concat_axis=1, tiled=True)
    seq_count = whole_rows.shape[1]
    full_batches = seq_count // MB
    local_qkv = (
        whole_rows.astype(jnp.float32)
        .transpose(0, 2, 1, 3)
        .reshape(3, heads_each, full_batches, MB, HD)
    )
    local_rates = whole_rates.reshape(heads_each, full_batches, MB)
    first_head = ctx_index * heads_each
    local_gain = lax.dynamic_slice_in_dim(
        pad_heads(inner_gain, heads_padded, 1.0), first_head, heads_each, 0
    )
    local_shift = lax.dynamic_slice_in_dim(
        pad_heads(inner_shift, heads_padded, 0.0), first_head, heads_each, 0
    )
    local_state = tuple(
        (
            lax.dynamic_slice_in_dim(
                pad_heads(piece_arr, heads_padded, 0.0), first_head, heads_each, 0
            )
            for piece_arr in init_state
        )
    )
    unused_final, saved_local = jax.vmap(partial(chain_scan, True))(
        local_state, local_qkv[0], local_qkv[1], local_qkv[2], local_rates, local_gain, local_shift
    )
    out_rows = saved_local.reshape(heads_each, seq_count, HD).transpose(1, 0, 2)
    back_rows = lax.all_to_all(
        out_rows.astype(jnp.bfloat16), "ctx", split_axis=0, concat_axis=1, tiled=True
    ).astype(out_rows.dtype)
    inner_flat = back_rows[:, :heads_dev].reshape(tok_count, width_dev)
    combined = ((attended + jnp.tanh(gate_alpha) * inner_flat) * live_rows[:, None]).astype(
        jnp.bfloat16
    )
    terms = jnp.dot(
        combined,
        lax.all_gather(out_weight, "video", axis=1, tiled=True),
        preferred_element_type=jnp.float32,
    )
    mixed = lax.psum_scatter(terms.astype(jnp.bfloat16), "head", scatter_dimension=1, tiled=True)
    return mixed[None]


def solution(mesh):
    placed = (
        P(None, "video", "ctx", "head"),
        P(None, "video", "ctx", "head"),
        P("video", "head", "ctx"),
        P("video", None),
        P("video"),
        P("head"),
        P("head", None),
        P("head", None),
        P("head", None, None),
        P("head", None),
        P("head", None, None),
        P("head", None),
        P("head", "video"),
    )
    shape = mesh.shape
    fused = shape["ctx"] == 2 and shape["head"] == shape["video"] == 4

    def on_device(*args):
        heads_dev = args[0].shape[3] // HD
        if fused and heads_dev % (2 * shape["ctx"]) == 0 and args[0].shape[2] % 128 == 0:
            return fused_on_device(*args)
        return general_on_device(*args)

    return jax.shard_map(
        on_device, mesh=mesh, in_specs=placed, out_specs=P("video", "ctx", "head"), check_vma=False
    )
```

```python
from functools import partial

import jax
import jax.numpy as jnp
import numpy as np
from jax import lax
from jax.experimental import pallas as pl
from jax.experimental.pallas import tpu as pltpu
from jax.sharding import PartitionSpec as P

HD = 64
MB = 64


gelu_scale = 0.7978845608028654
gelu_cubic = 0.044715


def with_halo(cells, sides, width):
    for axis, dim in sides:
        count = lax.axis_size(axis)
        ends = count - 1
        head = lax.slice_in_dim(cells, 0, width, axis=dim)
        tail = lax.slice_in_dim(cells, cells.shape[dim] - width, cells.shape[dim], axis=dim)
        cells = jnp.concatenate(
            [
                lax.ppermute(tail, axis, [(i, (i + 1) % count) for i in range(ends)]),
                cells,
                lax.ppermute(head, axis, [((i + 1) % count, i) for i in range(ends)]),
            ],
            axis=dim,
        )
    return cells


def matmul_high(first_op, second_op):
    return jnp.matmul(first_op, second_op, precision=lax.Precision.HIGHEST)


def gelu_pair(entries):
    inner_arg = gelu_scale * (entries + gelu_cubic * entries * entries * entries)
    tanh_val = jnp.tanh(inner_arg)
    act_val = 0.5 * entries * (1.0 + tanh_val)
    slope_val = 0.5 * (1.0 + tanh_val) + 0.5 * entries * (
        1.0 - tanh_val * tanh_val
    ) * gelu_scale * (1.0 + 3.0 * gelu_cubic * entries * entries)
    return (act_val, slope_val)


def layer_stats(summed):
    center = summed - jnp.mean(summed, axis=-1, keepdims=True)
    variance = jnp.mean(center * center, axis=-1, keepdims=True)
    inv_std = lax.rsqrt(variance + 1e-06)
    return (center * inv_std, inv_std)


def lower_mask(row_count):
    row_ids = lax.broadcasted_iota(jnp.int32, (row_count, row_count), 0)
    col_ids = lax.broadcasted_iota(jnp.int32, (row_count, row_count), 1)
    return (row_ids >= col_ids).astype(jnp.float32)


def inner_update(inner_state, key_mb, value_mb, rate_mb, norm_gain, norm_shift):
    weight_one, bias_one, weight_two, bias_two = inner_state
    hidden_pre = matmul_high(key_mb, weight_one) + bias_one
    hidden_act, hidden_slope = gelu_pair(hidden_pre)
    output_pre = matmul_high(hidden_act, weight_two) + bias_two
    normed, inv_std = layer_stats(output_pre)
    residual_err = norm_gain * normed + norm_shift - (value_mb - key_mb)
    scaled_err = residual_err * norm_gain
    grad_two = inv_std * (
        scaled_err
        - jnp.mean(scaled_err, axis=-1, keepdims=True)
        - normed * jnp.mean(scaled_err * normed, axis=-1, keepdims=True)
    )
    grad_one = matmul_high(grad_two, weight_two.T) * hidden_slope
    grad_one = grad_one * rate_mb[:, None]
    grad_two = grad_two * rate_mb[:, None]
    new_state = (
        weight_one - matmul_high(key_mb.T, grad_one),
        bias_one - jnp.sum(grad_one, axis=0),
        weight_two - matmul_high(hidden_act.T, grad_two),
        bias_two - jnp.sum(grad_two, axis=0),
    )
    return ((grad_one, hidden_act, grad_two), new_state)


def query_side(inner_state, query_mb, key_mb, grad_pack, norm_gain, norm_shift):
    weight_one, bias_one, weight_two, bias_two = inner_state
    grad_one, hidden_act, grad_two = grad_pack
    causal = lower_mask(query_mb.shape[0])
    first_kernel = (matmul_high(query_mb, key_mb.T) + 1.0) * causal
    query_pre = matmul_high(query_mb, weight_one) + bias_one - matmul_high(first_kernel, grad_one)
    query_act, unused_slope = gelu_pair(query_pre)
    second_kernel = (matmul_high(query_act, hidden_act.T) + 1.0) * causal
    query_out = matmul_high(query_act, weight_two) + bias_two - matmul_high(second_kernel, grad_two)
    normed, unused_inv = layer_stats(query_out)
    return query_mb + norm_gain * normed + norm_shift


def chain_scan(
    keep_queries, inner_state, queries, key_rows, values, rate_vals, norm_gain, norm_shift
):

    def stepper(loop_state, inputs):
        query_mb, key_mb, value_mb, rate_mb = inputs
        grad_pack, new_state = inner_update(
            loop_state, key_mb, value_mb, rate_mb, norm_gain, norm_shift
        )
        return (
            new_state,
            query_side(loop_state, query_mb, key_mb, grad_pack, norm_gain, norm_shift),
        )

    return lax.scan(stepper, inner_state, (queries, key_rows, values, rate_vals))


def pad_heads(array_in, total_heads, fill_value):
    extra = total_heads - array_in.shape[0]
    filler = jnp.full((extra,) + array_in.shape[1:], fill_value, array_in.dtype)
    return jnp.concatenate([array_in, filler], axis=0)


LANE = 128
MESH_ID = pl.DeviceIdType.MESH


def dot_nn(left, right):
    return lax.dot_general(
        left, right, (((1,), (0,)), ((), ())), preferred_element_type=jnp.float32
    )


def dot_nt(left, right):
    return lax.dot_general(
        left, right, (((1,), (1,)), ((), ())), preferred_element_type=jnp.float32
    )


def dot_tn(left, right):
    return lax.dot_general(
        left, right, (((0,), (0,)), ((), ())), preferred_element_type=jnp.float32
    )


def gelu_parts(entries):
    square = entries * entries
    inner_arg = entries * (gelu_scale + gelu_scale * gelu_cubic * square)
    half = 0.5 + 0.5 * jnp.tanh(inner_arg)
    return (square, half, entries * half)


def gelu_only(entries):
    return gelu_parts(entries)[2]


def gelu_and_slope(entries):
    square, half, act_val = gelu_parts(entries)
    ramp = 2.0 * gelu_scale + 6.0 * gelu_scale * gelu_cubic * square
    return (act_val, half + act_val * (1.0 - half) * ramp)


def half_mean(cells, left):
    first = jnp.sum(jnp.where(left, cells, 0.0), axis=-1, keepdims=True)
    second = jnp.sum(jnp.where(left, 0.0, cells), axis=-1, keepdims=True)
    return jnp.where(left, first, second) * (1.0 / HD)


def split_heads(cells, left):
    wide = cells.astype(jnp.float32)
    return jnp.concatenate(
        [jnp.where(left, wide, 0.0), jnp.where(left, 0.0, wide)], axis=0
    ).astype(cells.dtype)


def fused_kernel(
    aqkv,
    iqkv,
    rate,
    first_w,
    second_w,
    out_w,
    seg_in,
    length_in,
    gate_in,
    gain_in,
    shift_in,
    first_b_in,
    second_b_in,
    out,
    seg,
    length,
    gate,
    gain,
    shift,
    first_b,
    second_b,
    small_sem,
    a_rows,
    i_rows,
    rates,
    fw,
    sw,
    ow,
    lefts,
    rights,
    w2m,
    w2b,
    b1,
    b2,
    gate_s,
    gain_s,
    shift_s,
    rate_s,
    averager,
    pickers,
    tri_pair,
    bias,
    pulls,
    pull_means,
    own_s,
    hiddens,
    twos,
    inner,
    comb,
    gathered,
    sums,
    parts,
    beside,
    crossing,
    arrived,
    total,
    load_sem,
    y_send,
    y_recv,
    back_send,
    back_recv,
    z_send,
    z_recv,
    relay_send,
    own_sem,
    s_send,
    s_recv,
    r_send,
    r_recv,
    t_send,
    t_recv,
    low_sem,
    high_sem,
):
    slabs, _, seq, _ = a_rows.shape
    tok = aqkv.shape[2]
    hidden = first_b.shape[1]
    count = lax.axis_size("head")
    c = lax.axis_index("ctx")
    h = lax.axis_index("head")
    v = lax.axis_index("video")
    other = 1 - c
    mine = pl.multiple_of(c * tok, tok)
    theirs = pl.multiple_of(other * tok, tok)
    pairs_heads = 2 * slabs

    def columns(owner, slab):
        return pl.ds(pl.multiple_of((owner * slabs + slab) * LANE, LANE), LANE)

    barrier = pltpu.get_barrier_semaphore()
    pl.semaphore_signal(
        barrier, inc=1, device_id={"ctx": other}, device_id_type=MESH_ID
    )
    below, above = v > 0, v < count - 1
    for step in range(1, count):
        pl.semaphore_signal(
            barrier,
            inc=1,
            device_id={"head": lax.rem(h + step, count)},
            device_id_type=MESH_ID,
        )

    def tell(semaphore, inside, video):
        @pl.when(inside)
        def _():
            pl.semaphore_signal(
                semaphore, inc=1, device_id={"video": video}, device_id_type=MESH_ID
            )

    tell(barrier, below, v - 1)
    tell(barrier, above, v + 1)
    loads = []
    for slab in range(slabs):
        loads.append(
            pltpu.make_async_copy(
                iqkv.at[:, 0, :, columns(c, slab)],
                i_rows.at[slab, :, pl.ds(mine, tok), :],
                load_sem.at[slab],
            )
        )
    loads.append(pltpu.make_async_copy(rate, rates.at[c], load_sem.at[2 * slabs]))
    loads.append(
        pltpu.make_async_copy(
            first_w.at[pl.ds(c * pairs_heads, pairs_heads)], fw, load_sem.at[2 * slabs + 1]
        )
    )
    loads.append(
        pltpu.make_async_copy(
            second_w.at[pl.ds(c * pairs_heads, pairs_heads)], sw, load_sem.at[2 * slabs + 2]
        )
    )
    a_loads = [
        pltpu.make_async_copy(
            aqkv.at[:, 0, :, columns(c, slab)],
            a_rows.at[slab, :, pl.ds(mine, tok), :],
            load_sem.at[slabs + slab],
        )
        for slab in range(slabs)
    ]
    ow_load = pltpu.make_async_copy(out_w, ow, load_sem.at[2 * slabs + 3])
    for copy in loads + a_loads + [ow_load]:
        copy.start()

    small_loads = [
        pltpu.make_async_copy(source, kept_in, small_sem.at[at])
        for at, (source, kept_in) in enumerate(
            (
                (seg_in, seg),
                (length_in, length),
                (gate_in, gate),
                (gain_in, gain),
                (shift_in, shift),
                (first_b_in, first_b),
                (second_b_in, second_b),
            )
        )
    ]
    for copy in small_loads:
        copy.start()
    pl.semaphore_wait(barrier, count + (v + count - 1) // count + (2 * count - 2 - v) // count)

    def to_partner(src, dst, send, recv):
        return pltpu.make_async_remote_copy(
            src_ref=src,
            dst_ref=dst,
            send_sem=send,
            recv_sem=recv,
            device_id={"ctx": other},
            device_id_type=MESH_ID,
        )

    rate_out = to_partner(
        rate, rates.at[c], y_send.at[6 * slabs], y_recv.at[6 * slabs]
    )
    rate_out.start()

    def rows_out(source, target, slab, base):
        return [
            to_partner(
                source.at[kind, 0, :, columns(other, slab)],
                target.at[slab, kind, pl.ds(mine, tok), :],
                y_send.at[base + 3 * slab + kind],
                y_recv.at[base + 3 * slab + kind],
            )
            for kind in range(3)
        ]

    i_out = [rows_out(iqkv, i_rows, slab, 0) for slab in range(slabs)]
    a_out = [rows_out(aqkv, a_rows, slab, 3 * slabs) for slab in range(slabs)]
    early = max(slabs - 1, 1)

    def start_rows(part):
        for copies in zip(i_out[part], a_out[part]):
            for copy in copies[0] + copies[1]:
                copy.start()

    start_rows(slice(0, early))

    tell(low_sem, v == 0, v + 1)
    tell(high_sem, v == count - 1, v - 1)

    def pass_on(stage):
        for semaphore, here, video, last in (
            (low_sem, v == stage, v + 1, above),
            (high_sem, v == count - 1 - stage, v - 1, below),
        ):

            @pl.when(here)
            def _(semaphore=semaphore):
                pl.semaphore_wait(semaphore, 1)

            tell(semaphore, jnp.logical_and(here, last), video)

    for copy in small_loads:
        copy.wait()
    seq_ids = lax.broadcasted_iota(jnp.int32, (seq, seq), 1)
    row_ids = lax.broadcasted_iota(jnp.int32, (seq, seq), 0)
    len_val = length[0]
    segs = jnp.broadcast_to(seg[...].astype(jnp.float32), (seq, seq))
    allowed = (segs == segs.T) & ((seq_ids < len_val) | (seq_ids == row_ids))
    bias[...] = jnp.where(allowed, 0.0, -1e30)
    live = (lax.broadcasted_iota(jnp.int32, (seq, LANE), 0) < len_val).astype(jnp.float32)
    left = lax.broadcasted_iota(jnp.int32, (MB, LANE), 1) < HD
    left_seq = lax.broadcasted_iota(jnp.int32, (seq, LANE), 1) < HD
    pair_row_ids = lax.broadcasted_iota(jnp.int32, (LANE, LANE), 0)
    pair_col_ids = lax.broadcasted_iota(jnp.int32, (LANE, LANE), 1)
    same = (pair_row_ids < HD) == (pair_col_ids < HD)
    tri_pair[...] = jnp.where(same & (pair_row_ids >= pair_col_ids), 1.0, 0.0)
    averager[...] = jnp.where(same, 1.0 / HD, 0.0).astype(jnp.bfloat16)
    pickers[...] = jnp.where(pair_row_ids == pair_col_ids, 1.0, 0.0).astype(jnp.bfloat16)
    batches = seq // MB
    before = seq - MB
    lane_ids = lax.broadcasted_iota(jnp.int32, (MB, LANE), 1)
    batch_row_ids = lax.broadcasted_iota(jnp.int32, (MB, LANE), 0)

    gate_s[...] = jnp.tanh(gate[...].reshape(1, gate.shape[0]))

    for copy in loads:
        copy.wait()

    def pair_row(ref, head):
        return jnp.concatenate([ref[pl.ds(head, 1), :], ref[pl.ds(head + 1, 1), :]], axis=1)

    for slab in range(slabs):
        head = c * pairs_heads + 2 * slab
        gain_s[slab] = pair_row(gain, head)
        shift_s[slab] = pair_row(shift, head)
        bias_two = pair_row(second_b, head)
        b2[slab, 0] = bias_two - half_mean(bias_two, left[:1])
        for half in range(2):
            b1[slab, half] = first_b[pl.ds(head + half, 1), :]
            rights[slab, half, 0:before] = jnp.zeros((before, hidden), jnp.bfloat16)
            rights[slab, half, before:seq] = fw[2 * slab + half]
            whole = sw[2 * slab + half].astype(jnp.float32)
            whole = whole - jnp.mean(whole, axis=0, keepdims=True)
            w2m[slab, half * HD : (half + 1) * HD] = whole
            w2b[slab, 0, half * HD : (half + 1) * HD] = whole.astype(jnp.bfloat16)

    def average(cells):
        return dot_nn(cells.astype(jnp.bfloat16), averager[...])

    def parted(cells):
        return jnp.concatenate(
            [jnp.where(left, cells, 0.0), jnp.where(left, 0.0, cells)], axis=0
        ).astype(jnp.bfloat16)

    def joined(cells):
        return jnp.where(left, cells[:MB], cells[MB:])

    def masked_tile(cells, base, limit, causal):
        cols = np.arange(LANE)[None, :] + base
        reach = limit + (np.arange(MB)[:, None] if causal else -1)
        allowed = np.broadcast_to((cols <= reach) & (cols < before), (MB, LANE))
        kept = allowed | (cols >= before)
        if not kept.any():
            return jnp.zeros((MB, LANE), jnp.bfloat16)
        col_ids = lane_ids + base
        if allowed.all():
            cells = cells + 1.0
        elif allowed.any():
            inside = col_ids <= (limit + batch_row_ids if causal else limit - 1)
            inside = inside & (col_ids < before)
            cells = cells + jnp.where(inside, 1.0, 0.0)
            if not kept.all():
                cells = jnp.where(inside | (col_ids >= before), cells, 0.0)
        elif not kept.all():
            cells = jnp.where(col_ids >= before, cells, 0.0)
        return cells.astype(jnp.bfloat16)

    def inner_setup(slab, part):
        rows = slice(part * tok, (part + 1) * tok)
        head = c * pairs_heads + 2 * slab
        upright = jnp.concatenate(
            [jnp.broadcast_to(rates[part, head + half], (HD, tok)) for half in range(2)], axis=0
        )
        rate_s[slab, rows] = -(upright.T * live[rows])
        known = min((part + 1) * tok, before)
        query, key, value = (i_rows[slab, kind, rows] for kind in range(3))
        both = jnp.concatenate([key, query], axis=0)
        keys = i_rows[slab, 1, 0 : (part + 1) * tok].astype(jnp.float32)
        left_keys = left_seq[0 : (part + 1) * tok]
        key_parts = (
            jnp.where(left_keys, keys, 0.0).astype(jnp.bfloat16),
            jnp.where(left_keys, 0.0, keys).astype(jnp.bfloat16),
        )
        spare = [jnp.zeros((before - known, LANE), jnp.bfloat16)] if known < before else []
        blocks = tok // MB
        for half in range(2):
            against = jnp.concatenate(
                [key_parts[half][:known]] + spare + [pickers[half * HD : (half + 1) * HD]], axis=0
            )
            product = dot_nt(both, against)
            for block in range(2 * blocks):
                batch = part * blocks + block % blocks
                causal = block >= blocks
                target = causal * seq + batch * MB
                for base in range(0, seq, LANE):
                    lefts[slab, half, target : target + MB, base : base + LANE] = masked_tile(
                        product[block * MB : (block + 1) * MB, base : base + LANE],
                        base,
                        batch * MB,
                        causal,
                    )
        key_f = key.astype(jnp.float32)
        pull = gain_s[slab] * (shift_s[slab] - (value.astype(jnp.float32) - key_f))
        pulls[slab, rows] = pull
        pull_means[slab, rows] = average(pull)
        if (part + 1) * tok == seq:
            last = slice(before, seq)
            own = dot_nt(
                query[before - part * tok :],
                jnp.concatenate([cells[last] for cells in key_parts], axis=0),
            )
            own = (jnp.concatenate([own, own], axis=0) + 1.0) * tri_pair[...]
            own_s[slab] = own.astype(jnp.bfloat16)

    def query_step(slab, batch, pre):
        hidden_b = hiddens[slab, batch]
        pair_two = twos[slab, batch]
        rows = slice(batch * MB, (batch + 1) * MB)
        query_act = gelu_only(pre).astype(jnp.bfloat16)
        second_kernel = (dot_nt(query_act, hidden_b) + 1.0) * tri_pair[...]
        query_out = dot_nt(query_act, w2b[slab, batch]) + dot_nn(
            second_kernel.astype(jnp.bfloat16), pair_two
        )
        query_out = joined(query_out) + b2[slab, batch]
        inv_std = lax.rsqrt(average(query_out * query_out) + 1e-06)
        query = i_rows[slab, 0, rows, :].astype(jnp.float32)
        inner[slab, rows, :] = query + gain_s[slab] * (query_out * inv_std) + shift_s[slab]

    def inner_step(slab, batch):
        rows = slice(batch * MB, (batch + 1) * MB)
        final = batch == batches - 1
        blocks = [batch] + ([batches + batch - 1] if batch else []) + (
            [batches + batch] if final else []
        )
        pres = []
        for half in range(2):
            used = jnp.concatenate(
                [lefts[slab, half, at * MB : (at + 1) * MB] for at in blocks], axis=0
            )
            pres.append(dot_nn(used, rights[slab, half]) + b1[slab, half])

        def picked(at):
            return jnp.concatenate([pre[at * MB : (at + 1) * MB] for pre in pres], axis=0)

        hidden_act, slope = gelu_and_slope(picked(0))
        hidden_b = hidden_act.astype(jnp.bfloat16)
        hiddens[slab, batch] = hidden_b
        norm_gain = gain_s[slab]
        squared_gain = norm_gain * norm_gain
        bias_two = b2[slab, batch]
        center = joined(dot_nt(hidden_b, w2b[slab, batch])) + bias_two
        square = center * center
        pulled = pulls[slab, rows]
        means = average(
            jnp.concatenate(
                [square, squared_gain * center, squared_gain * square, pulled * center], axis=0
            )
        )
        var, lin, quad, cross = (means[at * MB : (at + 1) * MB] for at in range(4))
        inv_std = lax.rsqrt(var + 1e-06)
        normed = center * inv_std
        scaled = squared_gain * normed + pulled
        along = inv_std * (inv_std * quad + cross)
        grad_two = inv_std * (scaled - (inv_std * lin + pull_means[slab, rows]) - normed * along)
        two = grad_two * rate_s[slab, rows]
        pair_two = parted(two)
        twos[slab, batch] = pair_two
        one = (dot_nn(pair_two, w2b[slab, batch]) * slope).astype(jnp.bfloat16)
        if not final:
            for half in range(2):
                rights[slab, half, rows] = one[half * MB : (half + 1) * MB]
            updated = w2m[slab] + dot_tn(pair_two, hidden_b)
            w2m[slab] = updated
            w2b[slab, batch + 1] = updated.astype(jnp.bfloat16)
            b2[slab, batch + 1] = bias_two + jnp.sum(two, axis=0, keepdims=True)
        if batch:
            query_step(slab, batch - 1, picked(1))
        if final:
            query_step(slab, batch, picked(len(blocks) - 1) + dot_nn(own_s[slab], one))

    def to_video(src, video, spot, step):
        return pltpu.make_async_remote_copy(
            src_ref=src,
            dst_ref=gathered.at[v, spot],
            send_sem=z_send.at[spot, step - 1],
            recv_sem=z_recv.at[spot, step - 1],
            device_id={"video": video},
            device_id_type=MESH_ID,
        )

    def reached(step):
        target = lax.rem(v + step, count)
        return jnp.abs(target - v) < count - 1

    def spread(src, spot):
        copies = []
        for step in (2, 1, 3):
            copy = to_video(src, lax.rem(v + step, count), spot, step)

            copies.append((step, copy))
        return copies

    def launch(copies):
        for step, copy in copies:

            @pl.when(reached(step))
            def _(copy=copy):
                copy.start()


    def relays(spot):
        found = []
        for place, origin in ((1, count - 1), (count - 2, 0)):
            end = count - 1 - origin
            step = (end - origin) % count
            found.append(
                (
                    place,
                    origin,
                    pltpu.make_async_remote_copy(
                        src_ref=gathered.at[origin, spot],
                        dst_ref=gathered.at[origin, spot],
                        send_sem=relay_send.at[spot],
                        recv_sem=z_recv.at[spot, step - 1],
                        device_id={"video": end},
                        device_id_type=MESH_ID,
                    ),
                )
            )
        return found

    def z_arrival(video, spot, step):
        return pltpu.make_async_remote_copy(
            src_ref=gathered.at[video, spot],
            dst_ref=gathered.at[video, spot],
            send_sem=z_send.at[spot, step - 1],
            recv_sem=z_recv.at[spot, step - 1],
            device_id={"video": video},
            device_id_type=MESH_ID,
        )

    def relay(spot):
        for place, origin, copy in relays(spot):

            @pl.when(v == place)
            def _(copy=copy, origin=origin, place=place):
                z_arrival(origin, spot, (place - origin) % count).wait_recv()
                copy.start()

    z_out = []
    backs = []
    owns = []
    half_batches = batches // 2

    def attend(slab):
        query, key, value = (a_rows[slab, kind] for kind in range(3))
        scores = dot_nt(split_heads(query, left_seq), key) * HD ** (-0.5)
        halves = []
        for part in range(2):
            mine_scores = scores[part * seq : (part + 1) * seq] + bias[...]
            top = jnp.max(mine_scores, axis=-1, keepdims=True)
            weights = jnp.exp(mine_scores - top)
            mass = jnp.sum(weights, axis=-1, keepdims=True)
            halves.append(dot_nn(weights.astype(jnp.bfloat16), value) / mass)
        return jnp.where(left_seq, halves[0], halves[1])

    def combine(slab, attended):
        gate_row = gate_s[:, columns(c, slab)]
        comb[slab] = ((attended + gate_row * inner[slab]) * live).astype(jnp.bfloat16)

    @pl.when(c == 0)
    def _():
        for slab in range(slabs):
            inner_setup(slab, 0)
        for batch in range(half_batches):
            for slab in range(slabs):
                inner_step(slab, batch)

    pass_on(1)
    rate_out.wait_recv()
    for slab in range(slabs):
        for copy in i_out[slab]:
            copy.wait_recv()

        @pl.when(c == 1)
        def _(slab=slab):
            inner_setup(slab, 0)
            for batch in range(half_batches):
                inner_step(slab, batch)
            inner_setup(slab, 1)
            inner_step(slab, half_batches)

        @pl.when(c == 0)
        def _(slab=slab):
            inner_setup(slab, 1)
            for batch in range(half_batches, batches):
                inner_step(slab, batch)

        if slab == 0:
            pass_on(2)
        if slab:
            far = other * slabs + slab - 1
            far_out = spread(gathered.at[v, far], far)
            z_out += far_out

            def send_far(far_out=far_out, slab=slab):
                backs[slab - 1].wait_recv()
                launch(far_out)

            pl.when(c == 1)(send_far)
        a_loads[slab].wait()
        for copy in a_out[slab]:
            copy.wait_recv()
        @pl.when(c == 1)
        def _(slab=slab):
            attended = attend(slab)
            for batch in range(half_batches + 1, batches):
                inner_step(slab, batch)
            combine(slab, attended)

        @pl.when(c == 0)
        def _(slab=slab):
            combine(slab, attend(slab))

        if slab:
            pl.when(c == 0)(send_far)
        spot = c * slabs + slab
        back = to_partner(
            comb.at[slab, pl.ds(theirs, tok), :],
            gathered.at[v, spot],
            back_send.at[slab],
            back_recv.at[slab],
        )
        back.start()
        backs.append(back)
        if slab == 0:
            start_rows(slice(early, slabs))
        own = pltpu.make_async_copy(
            comb.at[slab, pl.ds(mine, tok), :], gathered.at[v, spot], own_sem.at[slab]
        )
        own.start()
        owns.append(own)
        if slab == 0:
            pass_on(3)
        near_out = spread(comb.at[slab, pl.ds(mine, tok), :], spot)
        launch(near_out)
        z_out += near_out
        if slab:
            relay(spot - 1)
        if slab > 1:
            relay(other * slabs + slab - 2)
    ow_load.wait()
    for own in owns[:-1]:
        own.wait()

    chunks, _, _, chunk = parts.shape
    toward = 1 - 2 * (v // (count // 2))
    videos = [lax.rem(v + toward * near + count, count) for near in range(count)]

    def z_wait(video, spots):
        step = lax.rem(v - video + count, count)
        passed = ((v == 1) & (video == count - 1)) | ((v == count - 2) & (video == 0))

        @pl.when(jnp.logical_not(passed))
        def _():
            for spot in spots:
                z_arrival(video, spot, step).wait_recv()

    def rows_of(video, spots):
        return jnp.concatenate([gathered[video, spot] for spot in spots], axis=1)

    first_half = list(range(slabs - 1))
    second_half = list(range(slabs, 2 * slabs - 1))
    last_spots = [slabs - 1, 2 * slabs - 1]

    def begin(near):
        if slabs == 1:
            return
        video = videos[near]
        if near:
            z_wait(video, first_half + second_half)
        sums[near] = dot_nn(
            rows_of(video, first_half), ow[0 : (slabs - 1) * LANE]
        ) + dot_nn(
            rows_of(video, second_half), ow[slabs * LANE : (2 * slabs - 1) * LANE]
        )

    lane_of, core_of = h // 2, lax.rem(h, 2)
    sibling = 2 * lane_of + 1 - core_of
    across = 2 * (1 - lane_of) + core_of

    def owner_lane(video):
        return lax.rem(video + v, 2)

    def owner_core(video):
        return lax.rem(video // 2 + v // 2, 2)

    def owned(lane, core):
        return 2 * lax.rem(core + v // 2, 2) + lax.rem(lane + v, 2)

    def to_head_copy(src, dst, send, recv, head):
        return pltpu.make_async_remote_copy(
            src_ref=src,
            dst_ref=dst,
            send_sem=send,
            recv_sem=recv,
            device_id={"head": head},
            device_id_type=MESH_ID,
        )

    def part_copy(video, at):
        slot = lax.rem(owner_lane(video) + lane_of, 2)
        return to_head_copy(
            parts.at[at, video],
            beside.at[at, slot],
            s_send.at[at, slot],
            s_recv.at[at, slot],
            sibling,
        )

    def finish(near):
        video = videos[near]
        if near:
            z_wait(video, last_spots)
        rest = jnp.concatenate(
            [ow[spot * LANE : (spot + 1) * LANE] for spot in last_spots], axis=0
        )
        piece = dot_nn(rows_of(video, last_spots), rest)
        if slabs > 1:
            piece = piece + sums[near]
        piece = piece.astype(jnp.bfloat16)
        for at in range(chunks):
            parts[at, video] = piece[:, at * chunk : (at + 1) * chunk]
            copy = part_copy(video, at)

            @pl.when(owner_core(video) != core_of)
            def _(copy=copy):
                copy.start()

    home, away = owned(lane_of, core_of), owned(1 - lane_of, core_of)
    to_head, to_v = v, home
    stays = (to_head == h) & (to_v == v)
    x_out = [
        to_head_copy(crossing.at[at], arrived.at[at], r_send.at[at], r_recv.at[at], across)
        for at in range(chunks)
    ]
    finals = [
        pltpu.make_async_remote_copy(
            src_ref=total.at[at],
            dst_ref=out.at[0, :, at * chunk : (at + 1) * chunk],
            send_sem=t_send.at[at],
            recv_sem=t_recv.at[at],
            device_id={"head": to_head, "video": to_v},
            device_id_type=MESH_ID,
        )
        for at in range(chunks)
    ]

    kept = [
        pltpu.make_async_copy(
            total.at[at], out.at[0, :, at * chunk : (at + 1) * chunk], t_send.at[at]
        )
        for at in range(chunks)
    ]

    def cross(near):
        @pl.when(videos[near] == away)
        def _():
            for at in range(chunks):
                part_copy(away, at).wait_recv()
                crossing[at] = (
                    parts[at, away].astype(jnp.float32) + beside[at, 1].astype(jnp.float32)
                ).astype(jnp.bfloat16)
                x_out[at].start()

    def arrive(near):
        @pl.when(videos[near] == home)
        def _():
            for at in range(chunks):
                part_copy(home, at).wait_recv()
                x_out[at].wait_recv()
                summed = parts[at, home].astype(jnp.float32) + beside[at, 0].astype(jnp.float32)
                total[at] = (summed + arrived[at].astype(jnp.float32)).astype(jnp.bfloat16)

                @pl.when(stays)
                def _(at=at):
                    kept[at].start()

                @pl.when(jnp.logical_not(stays))
                def _(at=at):
                    finals[at].start()

    begin(0)
    backs[slabs - 1].wait_recv()
    far = other * slabs + slabs - 1
    far_out = spread(gathered.at[v, far], far)
    launch(far_out)
    z_out += far_out
    owns[-1].wait()
    finish(0)
    if slabs > 1:
        relay(far - 1)
    relay(c * slabs + slabs - 1)
    for near in range(1, count):
        begin(near)
    relay(far)
    for near in range(1, count):
        finish(near)
        cross(near - 1)
    cross(count - 1)
    for near in range(count):
        arrive(near)

    @pl.when(jnp.logical_not(stays))
    def _():
        for final in finals:
            final.wait_recv()
            final.wait_send()

    @pl.when(stays)
    def _():
        for copy in kept:
            copy.wait()

    rows_sent = [copy for copies in i_out + a_out for copy in copies]
    for copy in [rate_out] + rows_sent + backs + x_out:
        copy.wait_send()
    for step, copy in z_out:

        @pl.when(reached(step))
        def _(copy=copy):
            copy.wait_send()

    for spot in range(2 * slabs):
        for place, _, copy in relays(spot):

            @pl.when(v == place)
            def _(copy=copy):
                copy.wait_send()

    for lane in range(2):
        for at in range(chunks):
            part_copy(owned(lane, 1 - core_of), at).wait_send()


def fused_on_device(
    attention_qkv,
    inner_qkv,
    learn_rate,
    segment_id,
    video_length,
    gate_alpha,
    inner_gain,
    inner_shift,
    first_weight,
    first_bias,
    second_weight,
    second_bias,
    out_weight,
):
    tok = attention_qkv.shape[2]
    width_dev = attention_qkv.shape[3]
    count = lax.axis_size("head")
    ctx_count = lax.axis_size("ctx")
    seq = tok * ctx_count
    slabs = width_dev // LANE // ctx_count
    heads = width_dev // HD
    hidden = first_weight.shape[2]
    columns = out_weight.shape[1]
    chunk = LANE
    chunks = columns // chunk
    half = jnp.bfloat16
    full = jnp.float32
    hbm = pl.BlockSpec(memory_space=pl.ANY)
    dma = pltpu.SemaphoreType.DMA
    return pl.pallas_call(
        fused_kernel,
        out_shape=jax.ShapeDtypeStruct((1, tok, columns), half),
        in_specs=[hbm] * 13,
        out_specs=hbm,
        scratch_shapes=[
            pltpu.VMEM(segment_id.shape, segment_id.dtype),
            pltpu.SMEM(video_length.shape, video_length.dtype),
            pltpu.VMEM(gate_alpha.shape, full),
            pltpu.VMEM(inner_gain.shape, full),
            pltpu.VMEM(inner_shift.shape, full),
            pltpu.VMEM(first_bias.shape, full),
            pltpu.VMEM(second_bias.shape, full),
            dma((7,)),
            pltpu.VMEM((slabs, 3, seq, LANE), half),
            pltpu.VMEM((slabs, 3, seq, LANE), half),
            pltpu.VMEM((ctx_count, heads, 1, tok), full),
            pltpu.VMEM((2 * slabs,) + first_weight.shape[1:], half),
            pltpu.VMEM((2 * slabs,) + second_weight.shape[:0:-1], half),
            pltpu.VMEM(out_weight.shape, half),
            pltpu.VMEM((slabs, 2, 2 * seq, seq), half),
            pltpu.VMEM((slabs, 2, seq, hidden), half),
            pltpu.VMEM((slabs, LANE, hidden), full),
            pltpu.VMEM((slabs, seq // MB, LANE, hidden), half),
            pltpu.VMEM((slabs, 2, 1, hidden), full),
            pltpu.VMEM((slabs, seq // MB, 1, LANE), full),
            pltpu.VMEM((1, width_dev), full),
            pltpu.VMEM((slabs, 1, LANE), full),
            pltpu.VMEM((slabs, 1, LANE), full),
            pltpu.VMEM((slabs, seq, LANE), full),
            pltpu.VMEM((LANE, LANE), half),
            pltpu.VMEM((LANE, LANE), half),
            pltpu.VMEM((LANE, LANE), full),
            pltpu.VMEM((seq, seq), full),
            pltpu.VMEM((slabs, seq, LANE), full),
            pltpu.VMEM((slabs, seq, LANE), full),
            pltpu.VMEM((slabs, LANE, LANE), half),
            pltpu.VMEM((slabs, seq // MB, LANE, hidden), half),
            pltpu.VMEM((slabs, seq // MB, LANE, LANE), half),
            pltpu.VMEM((slabs, seq, LANE), full),
            pltpu.VMEM((slabs, seq, LANE), half),
            pltpu.VMEM((count, 2 * slabs, tok, LANE), half),
            pltpu.VMEM((count, tok, columns), full),
            pltpu.VMEM((chunks, count, tok, chunk), half),
            pltpu.VMEM((chunks, 2, tok, chunk), half),
            pltpu.VMEM((chunks, tok, chunk), half),
            pltpu.VMEM((chunks, tok, chunk), half),
            pltpu.VMEM((chunks, tok, chunk), half),
            dma((2 * slabs + 4,)),
            dma((6 * slabs + 1,)),
            dma((6 * slabs + 1,)),
            dma((slabs,)),
            dma((slabs,)),
            dma((2 * slabs, count - 1)),
            dma((2 * slabs, count - 1)),
            dma((2 * slabs,)),
            dma((slabs,)),
            dma((chunks, 2)),
            dma((chunks, 2)),
            dma((chunks,)),
            dma((chunks,)),
            dma((chunks,)),
            dma((chunks,)),
            pltpu.SemaphoreType.REGULAR,
            pltpu.SemaphoreType.REGULAR,
        ],
        compiler_params=pltpu.CompilerParams(
            collective_id=0, has_side_effects=True, vmem_limit_bytes=60 * 1024 * 1024
        ),
    )(
        attention_qkv,
        inner_qkv,
        learn_rate.transpose(1, 0, 2),
        first_weight,
        second_weight.transpose(0, 2, 1),
        out_weight,
        segment_id,
        video_length,
        gate_alpha,
        inner_gain,
        inner_shift,
        first_bias,
        second_bias,
    )


def general_on_device(
    attention_qkv,
    inner_qkv,
    learn_rate,
    segment_id,
    video_length,
    gate_alpha,
    inner_gain,
    inner_shift,
    first_weight,
    first_bias,
    second_weight,
    second_bias,
    out_weight,
):
    tok_count = attention_qkv.shape[2]
    width_dev = attention_qkv.shape[3]
    heads_dev = width_dev // HD
    ctx_index = lax.axis_index("ctx")
    ctx_count = lax.axis_size("ctx")
    positions = ctx_index * tok_count + jnp.arange(tok_count, dtype=jnp.int32)
    length_val = video_length[0]
    live_rows = (positions < length_val).astype(jnp.float32)
    kv_pair = attention_qkv[1:, 0]
    kv_wide = with_halo(kv_pair, (("ctx", 1),), tok_count)
    key_pos = (ctx_index - 1) * tok_count + jnp.arange(3 * tok_count, dtype=jnp.int32)
    seg_row = segment_id[0]
    fill_ids = jnp.full((tok_count,), -1, jnp.int32)
    seg_pad = jnp.concatenate([fill_ids, seg_row, fill_ids])
    key_seg = lax.dynamic_slice_in_dim(seg_pad, ctx_index * tok_count, 3 * tok_count, 0)
    query_seg = lax.dynamic_slice_in_dim(seg_row, ctx_index * tok_count, tok_count, 0)
    allowed = (key_seg[None, :] == query_seg[:, None]) & (
        (key_pos[None, :] < length_val) | (key_pos[None, :] == positions[:, None])
    )
    query_heads = attention_qkv[0, 0].reshape(tok_count, heads_dev, HD)
    key_heads = kv_wide[0].reshape(3 * tok_count, heads_dev, HD)
    value_heads = kv_wide[1].reshape(3 * tok_count, heads_dev, HD)
    scores = jnp.einsum(
        "qhd,khd->hqk", query_heads, key_heads, preferred_element_type=jnp.float32
    ) * HD ** (-0.5)
    scores = jnp.where(allowed[None], scores, -1e30)
    row_max = jnp.max(scores, axis=-1, keepdims=True)
    exp_scores = jnp.exp(scores - row_max)
    soft_weights = (exp_scores / jnp.sum(exp_scores, axis=-1, keepdims=True)).astype(jnp.bfloat16)
    attended = jnp.einsum(
        "hqk,khd->qhd", soft_weights, value_heads, preferred_element_type=jnp.float32
    ).reshape(tok_count, width_dev)
    init_state = (
        first_weight.astype(jnp.float32),
        first_bias,
        second_weight.astype(jnp.float32),
        second_bias,
    )
    rate_rows = learn_rate[0] * live_rows[None, :]
    heads_each = -(-heads_dev // ctx_count)
    heads_padded = heads_each * ctx_count
    rows_heads = inner_qkv[:, 0].reshape(3, tok_count, heads_dev, HD)
    rows_padded = jnp.concatenate(
        [rows_heads, jnp.zeros((3, tok_count, heads_padded - heads_dev, HD), rows_heads.dtype)],
        axis=2,
    )
    rates_padded = pad_heads(rate_rows, heads_padded, 0.0)
    whole_rows = lax.all_to_all(rows_padded, "ctx", split_axis=2, concat_axis=1, tiled=True)
    whole_rates = lax.all_to_all(rates_padded, "ctx", split_axis=0, concat_axis=1, tiled=True)
    seq_count = whole_rows.shape[1]
    full_batches = seq_count // MB
    local_qkv = (
        whole_rows.astype(jnp.float32)
        .transpose(0, 2, 1, 3)
        .reshape(3, heads_each, full_batches, MB, HD)
    )
    local_rates = whole_rates.reshape(heads_each, full_batches, MB)
    first_head = ctx_index * heads_each
    local_gain = lax.dynamic_slice_in_dim(
        pad_heads(inner_gain, heads_padded, 1.0), first_head, heads_each, 0
    )
    local_shift = lax.dynamic_slice_in_dim(
        pad_heads(inner_shift, heads_padded, 0.0), first_head, heads_each, 0
    )
    local_state = tuple(
        (
            lax.dynamic_slice_in_dim(
                pad_heads(piece_arr, heads_padded, 0.0), first_head, heads_each, 0
            )
            for piece_arr in init_state
        )
    )
    unused_final, saved_local = jax.vmap(partial(chain_scan, True))(
        local_state, local_qkv[0], local_qkv[1], local_qkv[2], local_rates, local_gain, local_shift
    )
    out_rows = saved_local.reshape(heads_each, seq_count, HD).transpose(1, 0, 2)
    back_rows = lax.all_to_all(
        out_rows.astype(jnp.bfloat16), "ctx", split_axis=0, concat_axis=1, tiled=True
    ).astype(out_rows.dtype)
    inner_flat = back_rows[:, :heads_dev].reshape(tok_count, width_dev)
    combined = ((attended + jnp.tanh(gate_alpha) * inner_flat) * live_rows[:, None]).astype(
        jnp.bfloat16
    )
    terms = jnp.dot(
        combined,
        lax.all_gather(out_weight, "video", axis=1, tiled=True),
        preferred_element_type=jnp.float32,
    )
    mixed = lax.psum_scatter(terms.astype(jnp.bfloat16), "head", scatter_dimension=1, tiled=True)
    return mixed[None]


def solution(mesh):
    placed = (
        P(None, "video", "ctx", "head"),
        P(None, "video", "ctx", "head"),
        P("video", "head", "ctx"),
        P("video", None),
        P("video"),
        P("head"),
        P("head", None),
        P("head", None),
        P("head", None, None),
        P("head", None),
        P("head", None, None),
        P("head", None),
        P("head", "video"),
    )
    shape = mesh.shape
    fused = shape["ctx"] == 2 and shape["head"] == shape["video"] == 4

    def on_device(*args):
        heads_dev = args[0].shape[3] // HD
        if fused and heads_dev % (2 * shape["ctx"]) == 0 and args[0].shape[2] % 128 == 0:
            return fused_on_device(*args)
        return general_on_device(*args)

    return jax.shard_map(
        on_device, mesh=mesh, in_specs=placed, out_specs=P("video", "ctx", "head"), check_vma=False
    )
```

```python
from functools import partial

import jax
import jax.numpy as jnp
import numpy as np
from jax import lax
from jax.experimental import pallas as pl
from jax.experimental.pallas import tpu as pltpu
from jax.sharding import PartitionSpec as P

HD = 64
MB = 64


gelu_scale = 0.7978845608028654
gelu_cubic = 0.044715


def with_halo(cells, sides, width):
    for axis, dim in sides:
        count = lax.axis_size(axis)
        ends = count - 1
        head = lax.slice_in_dim(cells, 0, width, axis=dim)
        tail = lax.slice_in_dim(cells, cells.shape[dim] - width, cells.shape[dim], axis=dim)
        cells = jnp.concatenate(
            [
                lax.ppermute(tail, axis, [(i, (i + 1) % count) for i in range(ends)]),
                cells,
                lax.ppermute(head, axis, [((i + 1) % count, i) for i in range(ends)]),
            ],
            axis=dim,
        )
    return cells


def matmul_high(first_op, second_op):
    return jnp.matmul(first_op, second_op, precision=lax.Precision.HIGHEST)


def gelu_pair(entries):
    inner_arg = gelu_scale * (entries + gelu_cubic * entries * entries * entries)
    tanh_val = jnp.tanh(inner_arg)
    act_val = 0.5 * entries * (1.0 + tanh_val)
    slope_val = 0.5 * (1.0 + tanh_val) + 0.5 * entries * (
        1.0 - tanh_val * tanh_val
    ) * gelu_scale * (1.0 + 3.0 * gelu_cubic * entries * entries)
    return (act_val, slope_val)


def layer_stats(summed):
    center = summed - jnp.mean(summed, axis=-1, keepdims=True)
    variance = jnp.mean(center * center, axis=-1, keepdims=True)
    inv_std = lax.rsqrt(variance + 1e-06)
    return (center * inv_std, inv_std)


def lower_mask(row_count):
    row_ids = lax.broadcasted_iota(jnp.int32, (row_count, row_count), 0)
    col_ids = lax.broadcasted_iota(jnp.int32, (row_count, row_count), 1)
    return (row_ids >= col_ids).astype(jnp.float32)


def inner_update(inner_state, key_mb, value_mb, rate_mb, norm_gain, norm_shift):
    weight_one, bias_one, weight_two, bias_two = inner_state
    hidden_pre = matmul_high(key_mb, weight_one) + bias_one
    hidden_act, hidden_slope = gelu_pair(hidden_pre)
    output_pre = matmul_high(hidden_act, weight_two) + bias_two
    normed, inv_std = layer_stats(output_pre)
    residual_err = norm_gain * normed + norm_shift - (value_mb - key_mb)
    scaled_err = residual_err * norm_gain
    grad_two = inv_std * (
        scaled_err
        - jnp.mean(scaled_err, axis=-1, keepdims=True)
        - normed * jnp.mean(scaled_err * normed, axis=-1, keepdims=True)
    )
    grad_one = matmul_high(grad_two, weight_two.T) * hidden_slope
    grad_one = grad_one * rate_mb[:, None]
    grad_two = grad_two * rate_mb[:, None]
    new_state = (
        weight_one - matmul_high(key_mb.T, grad_one),
        bias_one - jnp.sum(grad_one, axis=0),
        weight_two - matmul_high(hidden_act.T, grad_two),
        bias_two - jnp.sum(grad_two, axis=0),
    )
    return ((grad_one, hidden_act, grad_two), new_state)


def query_side(inner_state, query_mb, key_mb, grad_pack, norm_gain, norm_shift):
    weight_one, bias_one, weight_two, bias_two = inner_state
    grad_one, hidden_act, grad_two = grad_pack
    causal = lower_mask(query_mb.shape[0])
    first_kernel = (matmul_high(query_mb, key_mb.T) + 1.0) * causal
    query_pre = matmul_high(query_mb, weight_one) + bias_one - matmul_high(first_kernel, grad_one)
    query_act, unused_slope = gelu_pair(query_pre)
    second_kernel = (matmul_high(query_act, hidden_act.T) + 1.0) * causal
    query_out = matmul_high(query_act, weight_two) + bias_two - matmul_high(second_kernel, grad_two)
    normed, unused_inv = layer_stats(query_out)
    return query_mb + norm_gain * normed + norm_shift


def chain_scan(
    keep_queries, inner_state, queries, key_rows, values, rate_vals, norm_gain, norm_shift
):

    def stepper(loop_state, inputs):
        query_mb, key_mb, value_mb, rate_mb = inputs
        grad_pack, new_state = inner_update(
            loop_state, key_mb, value_mb, rate_mb, norm_gain, norm_shift
        )
        return (
            new_state,
            query_side(loop_state, query_mb, key_mb, grad_pack, norm_gain, norm_shift),
        )

    return lax.scan(stepper, inner_state, (queries, key_rows, values, rate_vals))


def pad_heads(array_in, total_heads, fill_value):
    extra = total_heads - array_in.shape[0]
    filler = jnp.full((extra,) + array_in.shape[1:], fill_value, array_in.dtype)
    return jnp.concatenate([array_in, filler], axis=0)


LANE = 128
MESH_ID = pl.DeviceIdType.MESH


def dot_nn(left, right):
    return lax.dot_general(
        left, right, (((1,), (0,)), ((), ())), preferred_element_type=jnp.float32
    )


def dot_nt(left, right):
    return lax.dot_general(
        left, right, (((1,), (1,)), ((), ())), preferred_element_type=jnp.float32
    )


def dot_tn(left, right):
    return lax.dot_general(
        left, right, (((0,), (0,)), ((), ())), preferred_element_type=jnp.float32
    )


def gelu_parts(entries):
    square = entries * entries
    inner_arg = entries * (gelu_scale + gelu_scale * gelu_cubic * square)
    half = 0.5 + 0.5 * jnp.tanh(inner_arg)
    return (square, half, entries * half)


def gelu_only(entries):
    return gelu_parts(entries)[2]


def gelu_and_slope(entries):
    square, half, act_val = gelu_parts(entries)
    ramp = 2.0 * gelu_scale + 6.0 * gelu_scale * gelu_cubic * square
    return (act_val, half + act_val * (1.0 - half) * ramp)


def half_mean(cells, left):
    first = jnp.sum(jnp.where(left, cells, 0.0), axis=-1, keepdims=True)
    second = jnp.sum(jnp.where(left, 0.0, cells), axis=-1, keepdims=True)
    return jnp.where(left, first, second) * (1.0 / HD)


def split_heads(cells, left):
    wide = cells.astype(jnp.float32)
    return jnp.concatenate(
        [jnp.where(left, wide, 0.0), jnp.where(left, 0.0, wide)], axis=0
    ).astype(cells.dtype)


def fused_kernel(
    aqkv,
    iqkv,
    rate,
    first_w,
    second_w,
    out_w,
    seg_in,
    length_in,
    gate_in,
    gain_in,
    shift_in,
    first_b_in,
    second_b_in,
    out,
    seg,
    length,
    gate,
    gain,
    shift,
    first_b,
    second_b,
    small_sem,
    a_rows,
    i_rows,
    rates,
    fw,
    sw,
    ow,
    lefts,
    rights,
    w2m,
    w2b,
    b1,
    b2,
    gate_s,
    gain_s,
    shift_s,
    rate_s,
    averager,
    pickers,
    tri_pair,
    bias,
    pulls,
    pull_means,
    own_s,
    hiddens,
    twos,
    inner,
    comb,
    gathered,
    sums,
    parts,
    beside,
    crossing,
    arrived,
    total,
    load_sem,
    y_send,
    y_recv,
    back_send,
    back_recv,
    z_send,
    z_recv,
    relay_send,
    own_sem,
    s_send,
    s_recv,
    r_send,
    r_recv,
    t_send,
    t_recv,
    low_sem,
    high_sem,
):
    slabs, _, seq, _ = a_rows.shape
    tok = aqkv.shape[2]
    hidden = first_b.shape[1]
    count = lax.axis_size("head")
    c = lax.axis_index("ctx")
    h = lax.axis_index("head")
    v = lax.axis_index("video")
    other = 1 - c
    mine = pl.multiple_of(c * tok, tok)
    theirs = pl.multiple_of(other * tok, tok)
    pairs_heads = 2 * slabs

    def columns(owner, slab):
        return pl.ds(pl.multiple_of((owner * slabs + slab) * LANE, LANE), LANE)

    barrier = pltpu.get_barrier_semaphore()
    pl.semaphore_signal(
        barrier, inc=1, device_id={"ctx": other}, device_id_type=MESH_ID
    )
    below, above = v > 0, v < count - 1
    for step in range(1, count):
        pl.semaphore_signal(
            barrier,
            inc=1,
            device_id={"head": lax.rem(h + step, count)},
            device_id_type=MESH_ID,
        )

    def tell(semaphore, inside, video):
        @pl.when(inside)
        def _():
            pl.semaphore_signal(
                semaphore, inc=1, device_id={"video": video}, device_id_type=MESH_ID
            )

    tell(barrier, below, v - 1)
    tell(barrier, above, v + 1)
    loads = []
    for slab in range(slabs):
        loads.append(
            pltpu.make_async_copy(
                iqkv.at[:, 0, :, columns(c, slab)],
                i_rows.at[slab, :, pl.ds(mine, tok), :],
                load_sem.at[slab],
            )
        )
    loads.append(pltpu.make_async_copy(rate, rates.at[c], load_sem.at[2 * slabs]))
    loads.append(
        pltpu.make_async_copy(
            first_w.at[pl.ds(c * pairs_heads, pairs_heads)], fw, load_sem.at[2 * slabs + 1]
        )
    )
    loads.append(
        pltpu.make_async_copy(
            second_w.at[pl.ds(c * pairs_heads, pairs_heads)], sw, load_sem.at[2 * slabs + 2]
        )
    )
    a_loads = [
        pltpu.make_async_copy(
            aqkv.at[:, 0, :, columns(c, slab)],
            a_rows.at[slab, :, pl.ds(mine, tok), :],
            load_sem.at[slabs + slab],
        )
        for slab in range(slabs)
    ]
    ow_load = pltpu.make_async_copy(out_w, ow, load_sem.at[2 * slabs + 3])
    for copy in loads + a_loads + [ow_load]:
        copy.start()

    small_loads = [
        pltpu.make_async_copy(source, kept_in, small_sem.at[at])
        for at, (source, kept_in) in enumerate(
            (
                (seg_in, seg),
                (length_in, length),
                (gate_in, gate),
                (gain_in, gain),
                (shift_in, shift),
                (first_b_in, first_b),
                (second_b_in, second_b),
            )
        )
    ]
    for copy in small_loads:
        copy.start()
    pl.semaphore_wait(barrier, count + (v + count - 1) // count + (2 * count - 2 - v) // count)

    def to_partner(src, dst, send, recv):
        return pltpu.make_async_remote_copy(
            src_ref=src,
            dst_ref=dst,
            send_sem=send,
            recv_sem=recv,
            device_id={"ctx": other},
            device_id_type=MESH_ID,
        )

    rate_out = to_partner(
        rate, rates.at[c], y_send.at[6 * slabs], y_recv.at[6 * slabs]
    )
    rate_out.start()

    def rows_out(source, target, slab, base):
        return [
            to_partner(
                source.at[kind, 0, :, columns(other, slab)],
                target.at[slab, kind, pl.ds(mine, tok), :],
                y_send.at[base + 3 * slab + kind],
                y_recv.at[base + 3 * slab + kind],
            )
            for kind in range(3)
        ]

    i_out = [rows_out(iqkv, i_rows, slab, 0) for slab in range(slabs)]
    a_out = [rows_out(aqkv, a_rows, slab, 3 * slabs) for slab in range(slabs)]
    early = max(slabs - 1, 1)

    def start_rows(part):
        for copies in zip(i_out[part], a_out[part]):
            for copy in copies[0] + copies[1]:
                copy.start()

    start_rows(slice(0, early))

    tell(low_sem, v == 0, v + 1)
    tell(high_sem, v == count - 1, v - 1)

    def pass_on(stage):
        for semaphore, here, video, last in (
            (low_sem, v == stage, v + 1, above),
            (high_sem, v == count - 1 - stage, v - 1, below),
        ):

            @pl.when(here)
            def _(semaphore=semaphore):
                pl.semaphore_wait(semaphore, 1)

            tell(semaphore, jnp.logical_and(here, last), video)

    for copy in small_loads:
        copy.wait()
    seq_ids = lax.broadcasted_iota(jnp.int32, (seq, seq), 1)
    row_ids = lax.broadcasted_iota(jnp.int32, (seq, seq), 0)
    len_val = length[0]
    segs = jnp.broadcast_to(seg[...].astype(jnp.float32), (seq, seq))
    allowed = (segs == segs.T) & ((seq_ids < len_val) | (seq_ids == row_ids))
    bias[...] = jnp.where(allowed, 0.0, -1e30)
    live = (lax.broadcasted_iota(jnp.int32, (seq, LANE), 0) < len_val).astype(jnp.float32)
    left = lax.broadcasted_iota(jnp.int32, (MB, LANE), 1) < HD
    left_seq = lax.broadcasted_iota(jnp.int32, (seq, LANE), 1) < HD
    pair_row_ids = lax.broadcasted_iota(jnp.int32, (LANE, LANE), 0)
    pair_col_ids = lax.broadcasted_iota(jnp.int32, (LANE, LANE), 1)
    same = (pair_row_ids < HD) == (pair_col_ids < HD)
    tri_pair[...] = jnp.where(same & (pair_row_ids >= pair_col_ids), 1.0, 0.0)
    averager[...] = jnp.where(same, 1.0 / HD, 0.0).astype(jnp.bfloat16)
    pickers[...] = jnp.where(pair_row_ids == pair_col_ids, 1.0, 0.0).astype(jnp.bfloat16)
    batches = seq // MB
    before = seq - MB
    lane_ids = lax.broadcasted_iota(jnp.int32, (MB, LANE), 1)
    batch_row_ids = lax.broadcasted_iota(jnp.int32, (MB, LANE), 0)

    gate_s[...] = jnp.tanh(gate[...].reshape(1, gate.shape[0]))

    for copy in loads:
        copy.wait()

    def pair_row(ref, head):
        return jnp.concatenate([ref[pl.ds(head, 1), :], ref[pl.ds(head + 1, 1), :]], axis=1)

    for slab in range(slabs):
        head = c * pairs_heads + 2 * slab
        gain_s[slab] = pair_row(gain, head)
        shift_s[slab] = pair_row(shift, head)
        bias_two = pair_row(second_b, head)
        b2[slab, 0] = bias_two - half_mean(bias_two, left[:1])
        for half in range(2):
            b1[slab, half] = first_b[pl.ds(head + half, 1), :]
            rights[slab, half, 0:before] = jnp.zeros((before, hidden), jnp.bfloat16)
            rights[slab, half, before:seq] = fw[2 * slab + half]
            whole = sw[2 * slab + half].astype(jnp.float32)
            whole = whole - jnp.mean(whole, axis=0, keepdims=True)
            w2m[slab, half * HD : (half + 1) * HD] = whole
            w2b[slab, 0, half * HD : (half + 1) * HD] = whole.astype(jnp.bfloat16)

    def average(cells):
        return dot_nn(cells.astype(jnp.bfloat16), averager[...])

    def parted(cells):
        return jnp.concatenate(
            [jnp.where(left, cells, 0.0), jnp.where(left, 0.0, cells)], axis=0
        ).astype(jnp.bfloat16)

    def joined(cells):
        return jnp.where(left, cells[:MB], cells[MB:])

    def masked_tile(cells, base, limit, causal):
        cols = np.arange(LANE)[None, :] + base
        reach = limit + (np.arange(MB)[:, None] if causal else -1)
        allowed = np.broadcast_to((cols <= reach) & (cols < before), (MB, LANE))
        kept = allowed | (cols >= before)
        if not kept.any():
            return jnp.zeros((MB, LANE), jnp.bfloat16)
        col_ids = lane_ids + base
        if allowed.all():
            cells = cells + 1.0
        elif allowed.any():
            inside = col_ids <= (limit + batch_row_ids if causal else limit - 1)
            inside = inside & (col_ids < before)
            cells = cells + jnp.where(inside, 1.0, 0.0)
            if not kept.all():
                cells = jnp.where(inside | (col_ids >= before), cells, 0.0)
        elif not kept.all():
            cells = jnp.where(col_ids >= before, cells, 0.0)
        return cells.astype(jnp.bfloat16)

    def inner_setup(slab, part):
        rows = slice(part * tok, (part + 1) * tok)
        head = c * pairs_heads + 2 * slab
        upright = jnp.concatenate(
            [jnp.broadcast_to(rates[part, head + half], (HD, tok)) for half in range(2)], axis=0
        )
        rate_s[slab, rows] = -(upright.T * live[rows])
        known = min((part + 1) * tok, before)
        query, key, value = (i_rows[slab, kind, rows] for kind in range(3))
        both = jnp.concatenate([key, query], axis=0)
        keys = i_rows[slab, 1, 0 : (part + 1) * tok].astype(jnp.float32)
        left_keys = left_seq[0 : (part + 1) * tok]
        key_parts = (
            jnp.where(left_keys, keys, 0.0).astype(jnp.bfloat16),
            jnp.where(left_keys, 0.0, keys).astype(jnp.bfloat16),
        )
        spare = [jnp.zeros((before - known, LANE), jnp.bfloat16)] if known < before else []
        blocks = tok // MB
        for half in range(2):
            against = jnp.concatenate(
                [key_parts[half][:known]] + spare + [pickers[half * HD : (half + 1) * HD]], axis=0
            )
            product = dot_nt(both, against)
            for block in range(2 * blocks):
                batch = part * blocks + block % blocks
                causal = block >= blocks
                target = causal * seq + batch * MB
                for base in range(0, seq, LANE):
                    lefts[slab, half, target : target + MB, base : base + LANE] = masked_tile(
                        product[block * MB : (block + 1) * MB, base : base + LANE],
                        base,
                        batch * MB,
                        causal,
                    )
        key_f = key.astype(jnp.float32)
        pull = gain_s[slab] * (shift_s[slab] - (value.astype(jnp.float32) - key_f))
        pulls[slab, rows] = pull
        pull_means[slab, rows] = average(pull)
        if (part + 1) * tok == seq:
            last = slice(before, seq)
            own = dot_nt(
                query[before - part * tok :],
                jnp.concatenate([cells[last] for cells in key_parts], axis=0),
            )
            own = (jnp.concatenate([own, own], axis=0) + 1.0) * tri_pair[...]
            own_s[slab] = own.astype(jnp.bfloat16)

    def query_step(slab, batch, pre):
        hidden_b = hiddens[slab, batch]
        pair_two = twos[slab, batch]
        rows = slice(batch * MB, (batch + 1) * MB)
        query_act = gelu_only(pre).astype(jnp.bfloat16)
        second_kernel = (dot_nt(query_act, hidden_b) + 1.0) * tri_pair[...]
        query_out = dot_nt(query_act, w2b[slab, batch]) + dot_nn(
            second_kernel.astype(jnp.bfloat16), pair_two
        )
        query_out = joined(query_out) + b2[slab, batch]
        inv_std = lax.rsqrt(average(query_out * query_out) + 1e-06)
        query = i_rows[slab, 0, rows, :].astype(jnp.float32)
        inner[slab, rows, :] = query + gain_s[slab] * (query_out * inv_std) + shift_s[slab]

    def inner_step(slab, batch):
        rows = slice(batch * MB, (batch + 1) * MB)
        final = batch == batches - 1
        blocks = [batch] + ([batches + batch - 1] if batch else []) + (
            [batches + batch] if final else []
        )
        pres = []
        for half in range(2):
            used = jnp.concatenate(
                [lefts[slab, half, at * MB : (at + 1) * MB] for at in blocks], axis=0
            )
            pres.append(dot_nn(used, rights[slab, half]) + b1[slab, half])

        def picked(at):
            return jnp.concatenate([pre[at * MB : (at + 1) * MB] for pre in pres], axis=0)

        hidden_act, slope = gelu_and_slope(picked(0))
        hidden_b = hidden_act.astype(jnp.bfloat16)
        hiddens[slab, batch] = hidden_b
        norm_gain = gain_s[slab]
        squared_gain = norm_gain * norm_gain
        bias_two = b2[slab, batch]
        center = joined(dot_nt(hidden_b, w2b[slab, batch])) + bias_two
        square = center * center
        pulled = pulls[slab, rows]
        means = average(
            jnp.concatenate(
                [square, squared_gain * center, squared_gain * square, pulled * center], axis=0
            )
        )
        var, lin, quad, cross = (means[at * MB : (at + 1) * MB] for at in range(4))
        inv_std = lax.rsqrt(var + 1e-06)
        normed = center * inv_std
        scaled = squared_gain * normed + pulled
        along = inv_std * (inv_std * quad + cross)
        grad_two = inv_std * (scaled - (inv_std * lin + pull_means[slab, rows]) - normed * along)
        two = grad_two * rate_s[slab, rows]
        pair_two = parted(two)
        twos[slab, batch] = pair_two
        one = (dot_nn(pair_two, w2b[slab, batch]) * slope).astype(jnp.bfloat16)
        if not final:
            for half in range(2):
                rights[slab, half, rows] = one[half * MB : (half + 1) * MB]
            updated = w2m[slab] + dot_tn(pair_two, hidden_b)
            w2m[slab] = updated
            w2b[slab, batch + 1] = updated.astype(jnp.bfloat16)
            b2[slab, batch + 1] = bias_two + jnp.sum(two, axis=0, keepdims=True)
        if batch:
            query_step(slab, batch - 1, picked(1))
        if final:
            query_step(slab, batch, picked(len(blocks) - 1) + dot_nn(own_s[slab], one))

    def to_video(src, video, spot, step):
        return pltpu.make_async_remote_copy(
            src_ref=src,
            dst_ref=gathered.at[v, spot],
            send_sem=z_send.at[spot, step - 1],
            recv_sem=z_recv.at[spot, step - 1],
            device_id={"video": video},
            device_id_type=MESH_ID,
        )

    def reached(step):
        target = lax.rem(v + step, count)
        return jnp.abs(target - v) < count - 1

    def spread(src, spot):
        copies = []
        for step in (2, 1, 3):
            copy = to_video(src, lax.rem(v + step, count), spot, step)

            copies.append((step, copy))
        return copies

    def launch(copies):
        for step, copy in copies:

            @pl.when(reached(step))
            def _(copy=copy):
                copy.start()


    def relays(spot):
        found = []
        for place, origin in ((1, count - 1), (count - 2, 0)):
            end = count - 1 - origin
            step = (end - origin) % count
            found.append(
                (
                    place,
                    origin,
                    pltpu.make_async_remote_copy(
                        src_ref=gathered.at[origin, spot],
                        dst_ref=gathered.at[origin, spot],
                        send_sem=relay_send.at[spot],
                        recv_sem=z_recv.at[spot, step - 1],
                        device_id={"video": end},
                        device_id_type=MESH_ID,
                    ),
                )
            )
        return found

    def z_arrival(video, spot, step):
        return pltpu.make_async_remote_copy(
            src_ref=gathered.at[video, spot],
            dst_ref=gathered.at[video, spot],
            send_sem=z_send.at[spot, step - 1],
            recv_sem=z_recv.at[spot, step - 1],
            device_id={"video": video},
            device_id_type=MESH_ID,
        )

    def relay(spot):
        for place, origin, copy in relays(spot):

            @pl.when(v == place)
            def _(copy=copy, origin=origin, place=place):
                z_arrival(origin, spot, (place - origin) % count).wait_recv()
                copy.start()

    z_out = []
    backs = []
    owns = []
    half_batches = batches // 2

    def attend(slab):
        query, key, value = (a_rows[slab, kind] for kind in range(3))
        scores = dot_nt(split_heads(query, left_seq), key) * HD ** (-0.5)
        halves = []
        for part in range(2):
            mine_scores = scores[part * seq : (part + 1) * seq] + bias[...]
            top = jnp.max(mine_scores, axis=-1, keepdims=True)
            weights = jnp.exp(mine_scores - top)
            mass = jnp.sum(weights, axis=-1, keepdims=True)
            halves.append(dot_nn(weights.astype(jnp.bfloat16), value) / mass)
        return jnp.where(left_seq, halves[0], halves[1])

    def combine(slab, attended, part):
        rows = slice(part * tok, (part + 1) * tok)
        gate_row = gate_s[:, columns(c, slab)]
        whole = attended[rows] + gate_row * inner[slab, rows]
        comb[slab, rows] = (whole * live[rows]).astype(jnp.bfloat16)

    backs += [
        to_partner(
            comb.at[slab, pl.ds(theirs, tok), :],
            gathered.at[v, c * slabs + slab],
            back_send.at[slab],
            back_recv.at[slab],
        )
        for slab in range(slabs)
    ]

    @pl.when(c == 0)
    def _():
        for slab in range(slabs):
            inner_setup(slab, 0)
        for batch in range(half_batches):
            for slab in range(slabs):
                inner_step(slab, batch)

    pass_on(1)
    rate_out.wait_recv()
    for slab in range(slabs):
        for copy in i_out[slab]:
            copy.wait_recv()

        @pl.when(c == 1)
        def _(slab=slab):
            inner_setup(slab, 0)
            for batch in range(half_batches):
                inner_step(slab, batch)
            inner_setup(slab, 1)
            inner_step(slab, half_batches)

        @pl.when(c == 0)
        def _(slab=slab):
            inner_setup(slab, 1)
            for batch in range(half_batches, batches):
                inner_step(slab, batch)

        if slab == 0:
            pass_on(2)
        if slab:
            far = other * slabs + slab - 1
            far_out = spread(gathered.at[v, far], far)
            z_out += far_out

            def send_far(far_out=far_out, slab=slab):
                backs[slab - 1].wait_recv()
                launch(far_out)

            pl.when(c == 1)(send_far)
        a_loads[slab].wait()
        for copy in a_out[slab]:
            copy.wait_recv()
        @pl.when(c == 1)
        def _(slab=slab):
            attended = attend(slab)
            combine(slab, attended, 0)
            backs[slab].start()
            for batch in range(half_batches + 1, batches):
                inner_step(slab, batch)
            combine(slab, attended, 1)

        @pl.when(c == 0)
        def _(slab=slab):
            attended = attend(slab)
            combine(slab, attended, 1)
            backs[slab].start()
            combine(slab, attended, 0)

        if slab:
            pl.when(c == 0)(send_far)
        spot = c * slabs + slab
        if slab == 0:
            start_rows(slice(early, slabs))
        own = pltpu.make_async_copy(
            comb.at[slab, pl.ds(mine, tok), :], gathered.at[v, spot], own_sem.at[slab]
        )
        own.start()
        owns.append(own)
        if slab == 0:
            pass_on(3)
        near_out = spread(comb.at[slab, pl.ds(mine, tok), :], spot)
        launch(near_out)
        z_out += near_out
        if slab:
            relay(spot - 1)
        if slab > 1:
            relay(other * slabs + slab - 2)
    ow_load.wait()
    for own in owns[:-1]:
        own.wait()

    chunks, _, _, chunk = parts.shape
    toward = 1 - 2 * (v // (count // 2))
    videos = [lax.rem(v + toward * near + count, count) for near in range(count)]

    def z_wait(video, spots):
        step = lax.rem(v - video + count, count)
        passed = ((v == 1) & (video == count - 1)) | ((v == count - 2) & (video == 0))

        @pl.when(jnp.logical_not(passed))
        def _():
            for spot in spots:
                z_arrival(video, spot, step).wait_recv()

    def rows_of(video, spots):
        return jnp.concatenate([gathered[video, spot] for spot in spots], axis=1)

    first_half = list(range(slabs - 1))
    second_half = list(range(slabs, 2 * slabs - 1))
    last_spots = [slabs - 1, 2 * slabs - 1]

    def begin(near):
        if slabs == 1:
            return
        video = videos[near]
        if near:
            z_wait(video, first_half + second_half)
        sums[near] = dot_nn(
            rows_of(video, first_half), ow[0 : (slabs - 1) * LANE]
        ) + dot_nn(
            rows_of(video, second_half), ow[slabs * LANE : (2 * slabs - 1) * LANE]
        )

    lane_of, core_of = h // 2, lax.rem(h, 2)
    sibling = 2 * lane_of + 1 - core_of
    across = 2 * (1 - lane_of) + core_of

    def owner_lane(video):
        return lax.rem(video + v, 2)

    def owner_core(video):
        return lax.rem(video // 2 + v // 2, 2)

    def owned(lane, core):
        return 2 * lax.rem(core + v // 2, 2) + lax.rem(lane + v, 2)

    def to_head_copy(src, dst, send, recv, head):
        return pltpu.make_async_remote_copy(
            src_ref=src,
            dst_ref=dst,
            send_sem=send,
            recv_sem=recv,
            device_id={"head": head},
            device_id_type=MESH_ID,
        )

    def part_copy(video, at):
        slot = lax.rem(owner_lane(video) + lane_of, 2)
        return to_head_copy(
            parts.at[at, video],
            beside.at[at, slot],
            s_send.at[at, slot],
            s_recv.at[at, slot],
            sibling,
        )

    def finish(near):
        video = videos[near]
        if near:
            z_wait(video, last_spots)
        rest = jnp.concatenate(
            [ow[spot * LANE : (spot + 1) * LANE] for spot in last_spots], axis=0
        )
        piece = dot_nn(rows_of(video, last_spots), rest)
        if slabs > 1:
            piece = piece + sums[near]
        piece = piece.astype(jnp.bfloat16)
        for at in range(chunks):
            parts[at, video] = piece[:, at * chunk : (at + 1) * chunk]
            copy = part_copy(video, at)

            @pl.when(owner_core(video) != core_of)
            def _(copy=copy):
                copy.start()

    home, away = owned(lane_of, core_of), owned(1 - lane_of, core_of)
    to_head, to_v = v, home
    stays = (to_head == h) & (to_v == v)
    x_out = [
        to_head_copy(crossing.at[at], arrived.at[at], r_send.at[at], r_recv.at[at], across)
        for at in range(chunks)
    ]
    finals = [
        pltpu.make_async_remote_copy(
            src_ref=total.at[at],
            dst_ref=out.at[0, :, at * chunk : (at + 1) * chunk],
            send_sem=t_send.at[at],
            recv_sem=t_recv.at[at],
            device_id={"head": to_head, "video": to_v},
            device_id_type=MESH_ID,
        )
        for at in range(chunks)
    ]

    kept = [
        pltpu.make_async_copy(
            total.at[at], out.at[0, :, at * chunk : (at + 1) * chunk], t_send.at[at]
        )
        for at in range(chunks)
    ]

    def cross(near):
        @pl.when(videos[near] == away)
        def _():
            for at in range(chunks):
                part_copy(away, at).wait_recv()
                crossing[at] = (
                    parts[at, away].astype(jnp.float32) + beside[at, 1].astype(jnp.float32)
                ).astype(jnp.bfloat16)
                x_out[at].start()

    def arrive(near):
        @pl.when(videos[near] == home)
        def _():
            for at in range(chunks):
                part_copy(home, at).wait_recv()
                x_out[at].wait_recv()
                summed = parts[at, home].astype(jnp.float32) + beside[at, 0].astype(jnp.float32)
                total[at] = (summed + arrived[at].astype(jnp.float32)).astype(jnp.bfloat16)

                @pl.when(stays)
                def _(at=at):
                    kept[at].start()

                @pl.when(jnp.logical_not(stays))
                def _(at=at):
                    finals[at].start()

    begin(0)
    backs[slabs - 1].wait_recv()
    far = other * slabs + slabs - 1
    far_out = spread(gathered.at[v, far], far)
    launch(far_out)
    z_out += far_out
    owns[-1].wait()
    finish(0)
    if slabs > 1:
        relay(far - 1)
    relay(c * slabs + slabs - 1)
    for near in range(1, count):
        begin(near)
    relay(far)
    for near in range(1, count):
        finish(near)
        cross(near - 1)
    cross(count - 1)
    for near in range(count):
        arrive(near)

    rows_sent = [copy for copies in i_out + a_out for copy in copies]
    for copy in [rate_out] + rows_sent + backs + x_out:
        copy.wait_send()
    for step, copy in z_out:

        @pl.when(reached(step))
        def _(copy=copy):
            copy.wait_send()

    for spot in range(2 * slabs):
        for place, _, copy in relays(spot):

            @pl.when(v == place)
            def _(copy=copy):
                copy.wait_send()

    for lane in range(2):
        for at in range(chunks):
            part_copy(owned(lane, 1 - core_of), at).wait_send()

    @pl.when(jnp.logical_not(stays))
    def _():
        for final in finals:
            final.wait_recv()
            final.wait_send()

    @pl.when(stays)
    def _():
        for copy in kept:
            copy.wait()


def fused_on_device(
    attention_qkv,
    inner_qkv,
    learn_rate,
    segment_id,
    video_length,
    gate_alpha,
    inner_gain,
    inner_shift,
    first_weight,
    first_bias,
    second_weight,
    second_bias,
    out_weight,
):
    tok = attention_qkv.shape[2]
    width_dev = attention_qkv.shape[3]
    count = lax.axis_size("head")
    ctx_count = lax.axis_size("ctx")
    seq = tok * ctx_count
    slabs = width_dev // LANE // ctx_count
    heads = width_dev // HD
    hidden = first_weight.shape[2]
    columns = out_weight.shape[1]
    chunk = LANE
    chunks = columns // chunk
    half = jnp.bfloat16
    full = jnp.float32
    hbm = pl.BlockSpec(memory_space=pl.ANY)
    dma = pltpu.SemaphoreType.DMA
    return pl.pallas_call(
        fused_kernel,
        out_shape=pltpu.VMEM((1, tok, columns), half),
        in_specs=[hbm] * 13,
        out_specs=hbm,
        scratch_shapes=[
            pltpu.VMEM(segment_id.shape, segment_id.dtype),
            pltpu.SMEM(video_length.shape, video_length.dtype),
            pltpu.VMEM(gate_alpha.shape, full),
            pltpu.VMEM(inner_gain.shape, full),
            pltpu.VMEM(inner_shift.shape, full),
            pltpu.VMEM(first_bias.shape, full),
            pltpu.VMEM(second_bias.shape, full),
            dma((7,)),
            pltpu.VMEM((slabs, 3, seq, LANE), half),
            pltpu.VMEM((slabs, 3, seq, LANE), half),
            pltpu.VMEM((ctx_count, heads, 1, tok), full),
            pltpu.VMEM((2 * slabs,) + first_weight.shape[1:], half),
            pltpu.VMEM((2 * slabs,) + second_weight.shape[:0:-1], half),
            pltpu.VMEM(out_weight.shape, half),
            pltpu.VMEM((slabs, 2, 2 * seq, seq), half),
            pltpu.VMEM((slabs, 2, seq, hidden), half),
            pltpu.VMEM((slabs, LANE, hidden), full),
            pltpu.VMEM((slabs, seq // MB, LANE, hidden), half),
            pltpu.VMEM((slabs, 2, 1, hidden), full),
            pltpu.VMEM((slabs, seq // MB, 1, LANE), full),
            pltpu.VMEM((1, width_dev), full),
            pltpu.VMEM((slabs, 1, LANE), full),
            pltpu.VMEM((slabs, 1, LANE), full),
            pltpu.VMEM((slabs, seq, LANE), full),
            pltpu.VMEM((LANE, LANE), half),
            pltpu.VMEM((LANE, LANE), half),
            pltpu.VMEM((LANE, LANE), full),
            pltpu.VMEM((seq, seq), full),
            pltpu.VMEM((slabs, seq, LANE), full),
            pltpu.VMEM((slabs, seq, LANE), full),
            pltpu.VMEM((slabs, LANE, LANE), half),
            pltpu.VMEM((slabs, seq // MB, LANE, hidden), half),
            pltpu.VMEM((slabs, seq // MB, LANE, LANE), half),
            pltpu.VMEM((slabs, seq, LANE), full),
            pltpu.VMEM((slabs, seq, LANE), half),
            pltpu.VMEM((count, 2 * slabs, tok, LANE), half),
            pltpu.VMEM((count, tok, columns), full),
            pltpu.VMEM((chunks, count, tok, chunk), half),
            pltpu.VMEM((chunks, 2, tok, chunk), half),
            pltpu.VMEM((chunks, tok, chunk), half),
            pltpu.VMEM((chunks, tok, chunk), half),
            pltpu.VMEM((chunks, tok, chunk), half),
            dma((2 * slabs + 4,)),
            dma((6 * slabs + 1,)),
            dma((6 * slabs + 1,)),
            dma((slabs,)),
            dma((slabs,)),
            dma((2 * slabs, count - 1)),
            dma((2 * slabs, count - 1)),
            dma((2 * slabs,)),
            dma((slabs,)),
            dma((chunks, 2)),
            dma((chunks, 2)),
            dma((chunks,)),
            dma((chunks,)),
            dma((chunks,)),
            dma((chunks,)),
            pltpu.SemaphoreType.REGULAR,
            pltpu.SemaphoreType.REGULAR,
        ],
        compiler_params=pltpu.CompilerParams(
            collective_id=0, has_side_effects=True, vmem_limit_bytes=60 * 1024 * 1024
        ),
    )(
        attention_qkv,
        inner_qkv,
        learn_rate.transpose(1, 0, 2),
        first_weight,
        second_weight.transpose(0, 2, 1),
        out_weight,
        segment_id,
        video_length,
        gate_alpha,
        inner_gain,
        inner_shift,
        first_bias,
        second_bias,
    )


def general_on_device(
    attention_qkv,
    inner_qkv,
    learn_rate,
    segment_id,
    video_length,
    gate_alpha,
    inner_gain,
    inner_shift,
    first_weight,
    first_bias,
    second_weight,
    second_bias,
    out_weight,
):
    tok_count = attention_qkv.shape[2]
    width_dev = attention_qkv.shape[3]
    heads_dev = width_dev // HD
    ctx_index = lax.axis_index("ctx")
    ctx_count = lax.axis_size("ctx")
    positions = ctx_index * tok_count + jnp.arange(tok_count, dtype=jnp.int32)
    length_val = video_length[0]
    live_rows = (positions < length_val).astype(jnp.float32)
    kv_pair = attention_qkv[1:, 0]
    kv_wide = with_halo(kv_pair, (("ctx", 1),), tok_count)
    key_pos = (ctx_index - 1) * tok_count + jnp.arange(3 * tok_count, dtype=jnp.int32)
    seg_row = segment_id[0]
    fill_ids = jnp.full((tok_count,), -1, jnp.int32)
    seg_pad = jnp.concatenate([fill_ids, seg_row, fill_ids])
    key_seg = lax.dynamic_slice_in_dim(seg_pad, ctx_index * tok_count, 3 * tok_count, 0)
    query_seg = lax.dynamic_slice_in_dim(seg_row, ctx_index * tok_count, tok_count, 0)
    allowed = (key_seg[None, :] == query_seg[:, None]) & (
        (key_pos[None, :] < length_val) | (key_pos[None, :] == positions[:, None])
    )
    query_heads = attention_qkv[0, 0].reshape(tok_count, heads_dev, HD)
    key_heads = kv_wide[0].reshape(3 * tok_count, heads_dev, HD)
    value_heads = kv_wide[1].reshape(3 * tok_count, heads_dev, HD)
    scores = jnp.einsum(
        "qhd,khd->hqk", query_heads, key_heads, preferred_element_type=jnp.float32
    ) * HD ** (-0.5)
    scores = jnp.where(allowed[None], scores, -1e30)
    row_max = jnp.max(scores, axis=-1, keepdims=True)
    exp_scores = jnp.exp(scores - row_max)
    soft_weights = (exp_scores / jnp.sum(exp_scores, axis=-1, keepdims=True)).astype(jnp.bfloat16)
    attended = jnp.einsum(
        "hqk,khd->qhd", soft_weights, value_heads, preferred_element_type=jnp.float32
    ).reshape(tok_count, width_dev)
    init_state = (
        first_weight.astype(jnp.float32),
        first_bias,
        second_weight.astype(jnp.float32),
        second_bias,
    )
    rate_rows = learn_rate[0] * live_rows[None, :]
    heads_each = -(-heads_dev // ctx_count)
    heads_padded = heads_each * ctx_count
    rows_heads = inner_qkv[:, 0].reshape(3, tok_count, heads_dev, HD)
    rows_padded = jnp.concatenate(
        [rows_heads, jnp.zeros((3, tok_count, heads_padded - heads_dev, HD), rows_heads.dtype)],
        axis=2,
    )
    rates_padded = pad_heads(rate_rows, heads_padded, 0.0)
    whole_rows = lax.all_to_all(rows_padded, "ctx", split_axis=2, concat_axis=1, tiled=True)
    whole_rates = lax.all_to_all(rates_padded, "ctx", split_axis=0, concat_axis=1, tiled=True)
    seq_count = whole_rows.shape[1]
    full_batches = seq_count // MB
    local_qkv = (
        whole_rows.astype(jnp.float32)
        .transpose(0, 2, 1, 3)
        .reshape(3, heads_each, full_batches, MB, HD)
    )
    local_rates = whole_rates.reshape(heads_each, full_batches, MB)
    first_head = ctx_index * heads_each
    local_gain = lax.dynamic_slice_in_dim(
        pad_heads(inner_gain, heads_padded, 1.0), first_head, heads_each, 0
    )
    local_shift = lax.dynamic_slice_in_dim(
        pad_heads(inner_shift, heads_padded, 0.0), first_head, heads_each, 0
    )
    local_state = tuple(
        (
            lax.dynamic_slice_in_dim(
                pad_heads(piece_arr, heads_padded, 0.0), first_head, heads_each, 0
            )
            for piece_arr in init_state
        )
    )
    unused_final, saved_local = jax.vmap(partial(chain_scan, True))(
        local_state, local_qkv[0], local_qkv[1], local_qkv[2], local_rates, local_gain, local_shift
    )
    out_rows = saved_local.reshape(heads_each, seq_count, HD).transpose(1, 0, 2)
    back_rows = lax.all_to_all(
        out_rows.astype(jnp.bfloat16), "ctx", split_axis=0, concat_axis=1, tiled=True
    ).astype(out_rows.dtype)
    inner_flat = back_rows[:, :heads_dev].reshape(tok_count, width_dev)
    combined = ((attended + jnp.tanh(gate_alpha) * inner_flat) * live_rows[:, None]).astype(
        jnp.bfloat16
    )
    terms = jnp.dot(
        combined,
        lax.all_gather(out_weight, "video", axis=1, tiled=True),
        preferred_element_type=jnp.float32,
    )
    mixed = lax.psum_scatter(terms.astype(jnp.bfloat16), "head", scatter_dimension=1, tiled=True)
    return mixed[None]


def solution(mesh):
    placed = (
        P(None, "video", "ctx", "head"),
        P(None, "video", "ctx", "head"),
        P("video", "head", "ctx"),
        P("video", None),
        P("video"),
        P("head"),
        P("head", None),
        P("head", None),
        P("head", None, None),
        P("head", None),
        P("head", None, None),
        P("head", None),
        P("head", "video"),
    )
    shape = mesh.shape
    fused = shape["ctx"] == 2 and shape["head"] == shape["video"] == 4

    def on_device(*args):
        heads_dev = args[0].shape[3] // HD
        if fused and heads_dev % (2 * shape["ctx"]) == 0 and args[0].shape[2] % 128 == 0:
            return fused_on_device(*args)
        return general_on_device(*args)

    return jax.shard_map(
        on_device, mesh=mesh, in_specs=placed, out_specs=P("video", "ctx", "head"), check_vma=False
    )
```

```python
from functools import partial

import jax
import jax.numpy as jnp
import numpy as np
from jax import lax
from jax.experimental import pallas as pl
from jax.experimental.pallas import tpu as pltpu
from jax.sharding import PartitionSpec as P

HD = 64
MB = 64


gelu_scale = 0.7978845608028654
gelu_cubic = 0.044715


def with_halo(cells, sides, width):
    for axis, dim in sides:
        count = lax.axis_size(axis)
        ends = count - 1
        head = lax.slice_in_dim(cells, 0, width, axis=dim)
        tail = lax.slice_in_dim(cells, cells.shape[dim] - width, cells.shape[dim], axis=dim)
        cells = jnp.concatenate(
            [
                lax.ppermute(tail, axis, [(i, (i + 1) % count) for i in range(ends)]),
                cells,
                lax.ppermute(head, axis, [((i + 1) % count, i) for i in range(ends)]),
            ],
            axis=dim,
        )
    return cells


def matmul_high(first_op, second_op):
    return jnp.matmul(first_op, second_op, precision=lax.Precision.HIGHEST)


def gelu_pair(entries):
    inner_arg = gelu_scale * (entries + gelu_cubic * entries * entries * entries)
    tanh_val = jnp.tanh(inner_arg)
    act_val = 0.5 * entries * (1.0 + tanh_val)
    slope_val = 0.5 * (1.0 + tanh_val) + 0.5 * entries * (
        1.0 - tanh_val * tanh_val
    ) * gelu_scale * (1.0 + 3.0 * gelu_cubic * entries * entries)
    return (act_val, slope_val)


def layer_stats(summed):
    center = summed - jnp.mean(summed, axis=-1, keepdims=True)
    variance = jnp.mean(center * center, axis=-1, keepdims=True)
    inv_std = lax.rsqrt(variance + 1e-06)
    return (center * inv_std, inv_std)


def lower_mask(row_count):
    row_ids = lax.broadcasted_iota(jnp.int32, (row_count, row_count), 0)
    col_ids = lax.broadcasted_iota(jnp.int32, (row_count, row_count), 1)
    return (row_ids >= col_ids).astype(jnp.float32)


def inner_update(inner_state, key_mb, value_mb, rate_mb, norm_gain, norm_shift):
    weight_one, bias_one, weight_two, bias_two = inner_state
    hidden_pre = matmul_high(key_mb, weight_one) + bias_one
    hidden_act, hidden_slope = gelu_pair(hidden_pre)
    output_pre = matmul_high(hidden_act, weight_two) + bias_two
    normed, inv_std = layer_stats(output_pre)
    residual_err = norm_gain * normed + norm_shift - (value_mb - key_mb)
    scaled_err = residual_err * norm_gain
    grad_two = inv_std * (
        scaled_err
        - jnp.mean(scaled_err, axis=-1, keepdims=True)
        - normed * jnp.mean(scaled_err * normed, axis=-1, keepdims=True)
    )
    grad_one = matmul_high(grad_two, weight_two.T) * hidden_slope
    grad_one = grad_one * rate_mb[:, None]
    grad_two = grad_two * rate_mb[:, None]
    new_state = (
        weight_one - matmul_high(key_mb.T, grad_one),
        bias_one - jnp.sum(grad_one, axis=0),
        weight_two - matmul_high(hidden_act.T, grad_two),
        bias_two - jnp.sum(grad_two, axis=0),
    )
    return ((grad_one, hidden_act, grad_two), new_state)


def query_side(inner_state, query_mb, key_mb, grad_pack, norm_gain, norm_shift):
    weight_one, bias_one, weight_two, bias_two = inner_state
    grad_one, hidden_act, grad_two = grad_pack
    causal = lower_mask(query_mb.shape[0])
    first_kernel = (matmul_high(query_mb, key_mb.T) + 1.0) * causal
    query_pre = matmul_high(query_mb, weight_one) + bias_one - matmul_high(first_kernel, grad_one)
    query_act, unused_slope = gelu_pair(query_pre)
    second_kernel = (matmul_high(query_act, hidden_act.T) + 1.0) * causal
    query_out = matmul_high(query_act, weight_two) + bias_two - matmul_high(second_kernel, grad_two)
    normed, unused_inv = layer_stats(query_out)
    return query_mb + norm_gain * normed + norm_shift


def chain_scan(
    keep_queries, inner_state, queries, key_rows, values, rate_vals, norm_gain, norm_shift
):

    def stepper(loop_state, inputs):
        query_mb, key_mb, value_mb, rate_mb = inputs
        grad_pack, new_state = inner_update(
            loop_state, key_mb, value_mb, rate_mb, norm_gain, norm_shift
        )
        return (
            new_state,
            query_side(loop_state, query_mb, key_mb, grad_pack, norm_gain, norm_shift),
        )

    return lax.scan(stepper, inner_state, (queries, key_rows, values, rate_vals))


def pad_heads(array_in, total_heads, fill_value):
    extra = total_heads - array_in.shape[0]
    filler = jnp.full((extra,) + array_in.shape[1:], fill_value, array_in.dtype)
    return jnp.concatenate([array_in, filler], axis=0)


LANE = 128
MESH_ID = pl.DeviceIdType.MESH


def dot_nn(left, right):
    return lax.dot_general(
        left, right, (((1,), (0,)), ((), ())), preferred_element_type=jnp.float32
    )


def dot_nt(left, right):
    return lax.dot_general(
        left, right, (((1,), (1,)), ((), ())), preferred_element_type=jnp.float32
    )


def dot_tn(left, right):
    return lax.dot_general(
        left, right, (((0,), (0,)), ((), ())), preferred_element_type=jnp.float32
    )


def gelu_parts(entries):
    square = entries * entries
    inner_arg = entries * (gelu_scale + gelu_scale * gelu_cubic * square)
    half = 0.5 + 0.5 * jnp.tanh(inner_arg)
    return (square, half, entries * half)


def gelu_only(entries):
    return gelu_parts(entries)[2]


def gelu_and_slope(entries):
    square, half, act_val = gelu_parts(entries)
    ramp = 2.0 * gelu_scale + 6.0 * gelu_scale * gelu_cubic * square
    return (act_val, half + act_val * (1.0 - half) * ramp)


def half_mean(cells, left):
    first = jnp.sum(jnp.where(left, cells, 0.0), axis=-1, keepdims=True)
    second = jnp.sum(jnp.where(left, 0.0, cells), axis=-1, keepdims=True)
    return jnp.where(left, first, second) * (1.0 / HD)


def split_heads(cells, left):
    wide = cells.astype(jnp.float32)
    return jnp.concatenate(
        [jnp.where(left, wide, 0.0), jnp.where(left, 0.0, wide)], axis=0
    ).astype(cells.dtype)


def fused_kernel(
    aqkv,
    iqkv,
    rate,
    first_w,
    second_w,
    out_w,
    seg_in,
    length_in,
    gate_in,
    gain_in,
    shift_in,
    first_b_in,
    second_b_in,
    out,
    seg,
    length,
    gate,
    gain,
    shift,
    first_b,
    second_b,
    small_sem,
    a_rows,
    i_rows,
    rates,
    fw,
    sw,
    ow,
    lefts,
    rights,
    w2m,
    w2b,
    b1,
    b2,
    gate_s,
    gain_s,
    shift_s,
    rate_s,
    averager,
    pickers,
    tri_pair,
    bias,
    pulls,
    pull_means,
    own_s,
    hiddens,
    twos,
    inner,
    comb,
    gathered,
    sums,
    parts,
    beside,
    crossing,
    arrived,
    total,
    load_sem,
    y_send,
    y_recv,
    back_send,
    back_recv,
    z_send,
    z_recv,
    relay_send,
    own_sem,
    s_send,
    s_recv,
    r_send,
    r_recv,
    t_send,
    t_recv,
    low_sem,
    high_sem,
):
    slabs, _, seq, _ = a_rows.shape
    tok = aqkv.shape[2]
    hidden = first_b.shape[1]
    count = lax.axis_size("head")
    c = lax.axis_index("ctx")
    h = lax.axis_index("head")
    v = lax.axis_index("video")
    other = 1 - c
    mine = pl.multiple_of(c * tok, tok)
    theirs = pl.multiple_of(other * tok, tok)
    pairs_heads = 2 * slabs

    def columns(owner, slab):
        return pl.ds(pl.multiple_of((owner * slabs + slab) * LANE, LANE), LANE)

    barrier = pltpu.get_barrier_semaphore()
    pl.semaphore_signal(
        barrier, inc=1, device_id={"ctx": other}, device_id_type=MESH_ID
    )
    below, above = v > 0, v < count - 1
    for step in range(1, count):
        pl.semaphore_signal(
            barrier,
            inc=1,
            device_id={"head": lax.rem(h + step, count)},
            device_id_type=MESH_ID,
        )

    def tell(semaphore, inside, video):
        @pl.when(inside)
        def _():
            pl.semaphore_signal(
                semaphore, inc=1, device_id={"video": video}, device_id_type=MESH_ID
            )

    tell(barrier, below, v - 1)
    tell(barrier, above, v + 1)
    loads = []
    for slab in range(slabs):
        loads.append(
            pltpu.make_async_copy(
                iqkv.at[:, 0, :, columns(c, slab)],
                i_rows.at[slab, :, pl.ds(mine, tok), :],
                load_sem.at[slab],
            )
        )
    loads.append(pltpu.make_async_copy(rate, rates.at[c], load_sem.at[2 * slabs]))
    loads.append(
        pltpu.make_async_copy(
            first_w.at[pl.ds(c * pairs_heads, pairs_heads)], fw, load_sem.at[2 * slabs + 1]
        )
    )
    loads.append(
        pltpu.make_async_copy(
            second_w.at[pl.ds(c * pairs_heads, pairs_heads)], sw, load_sem.at[2 * slabs + 2]
        )
    )
    a_loads = [
        pltpu.make_async_copy(
            aqkv.at[:, 0, :, columns(c, slab)],
            a_rows.at[slab, :, pl.ds(mine, tok), :],
            load_sem.at[slabs + slab],
        )
        for slab in range(slabs)
    ]
    ow_load = pltpu.make_async_copy(out_w, ow, load_sem.at[2 * slabs + 3])
    for copy in loads + a_loads + [ow_load]:
        copy.start()

    small_loads = [
        pltpu.make_async_copy(source, kept_in, small_sem.at[at])
        for at, (source, kept_in) in enumerate(
            (
                (seg_in, seg),
                (length_in, length),
                (gate_in, gate),
                (gain_in, gain),
                (shift_in, shift),
                (first_b_in, first_b),
                (second_b_in, second_b),
            )
        )
    ]
    for copy in small_loads:
        copy.start()
    pl.semaphore_wait(barrier, count + (v + count - 1) // count + (2 * count - 2 - v) // count)

    def to_partner(src, dst, send, recv):
        return pltpu.make_async_remote_copy(
            src_ref=src,
            dst_ref=dst,
            send_sem=send,
            recv_sem=recv,
            device_id={"ctx": other},
            device_id_type=MESH_ID,
        )

    rate_out = to_partner(
        rate, rates.at[c], y_send.at[1], y_recv.at[2 * slabs]
    )
    rate_out.start()

    def rows_out(source, target, slab, base):
        return [
            to_partner(
                source.at[kind, 0, :, columns(other, slab)],
                target.at[slab, kind, pl.ds(mine, tok), :],
                y_send.at[0],
                y_recv.at[base + slab],
            )
            for kind in range(3)
        ]

    i_out = [rows_out(iqkv, i_rows, slab, 0) for slab in range(slabs)]
    a_out = [rows_out(aqkv, a_rows, slab, slabs) for slab in range(slabs)]
    early = max(slabs - 1, 1)

    def in_place(ref, send, recv):
        return to_partner(ref, ref, send, recv)

    def rows_in(target, slab, base):
        in_place(
            target.at[slab, :, pl.ds(theirs, tok), :], y_send.at[0], y_recv.at[base + slab]
        ).wait_recv()

    def start_rows(part):
        for copies in zip(i_out[part], a_out[part]):
            for copy in copies[0] + copies[1]:
                copy.start()

    start_rows(slice(0, early))

    tell(low_sem, v == 0, v + 1)
    tell(high_sem, v == count - 1, v - 1)

    def pass_on(stage):
        for semaphore, here, video, last in (
            (low_sem, v == stage, v + 1, above),
            (high_sem, v == count - 1 - stage, v - 1, below),
        ):

            @pl.when(here)
            def _(semaphore=semaphore):
                pl.semaphore_wait(semaphore, 1)

            tell(semaphore, jnp.logical_and(here, last), video)

    for copy in small_loads:
        copy.wait()
    seq_ids = lax.broadcasted_iota(jnp.int32, (seq, seq), 1)
    row_ids = lax.broadcasted_iota(jnp.int32, (seq, seq), 0)
    len_val = length[0]
    segs = jnp.broadcast_to(seg[...].astype(jnp.float32), (seq, seq))
    allowed = (segs == segs.T) & ((seq_ids < len_val) | (seq_ids == row_ids))
    bias[...] = jnp.where(allowed, 0.0, -1e30)
    live = (lax.broadcasted_iota(jnp.int32, (seq, LANE), 0) < len_val).astype(jnp.float32)
    left = lax.broadcasted_iota(jnp.int32, (MB, LANE), 1) < HD
    left_seq = lax.broadcasted_iota(jnp.int32, (seq, LANE), 1) < HD
    pair_row_ids = lax.broadcasted_iota(jnp.int32, (LANE, LANE), 0)
    pair_col_ids = lax.broadcasted_iota(jnp.int32, (LANE, LANE), 1)
    same = (pair_row_ids < HD) == (pair_col_ids < HD)
    tri_pair[...] = jnp.where(same & (pair_row_ids >= pair_col_ids), 1.0, 0.0)
    averager[...] = jnp.where(same, 1.0 / HD, 0.0).astype(jnp.bfloat16)
    pickers[...] = jnp.where(pair_row_ids == pair_col_ids, 1.0, 0.0).astype(jnp.bfloat16)
    batches = seq // MB
    before = seq - MB
    lane_ids = lax.broadcasted_iota(jnp.int32, (MB, LANE), 1)
    batch_row_ids = lax.broadcasted_iota(jnp.int32, (MB, LANE), 0)

    gate_s[...] = jnp.tanh(gate[...].reshape(1, gate.shape[0]))

    for copy in loads:
        copy.wait()

    def pair_row(ref, head):
        return jnp.concatenate([ref[pl.ds(head, 1), :], ref[pl.ds(head + 1, 1), :]], axis=1)

    for slab in range(slabs):
        head = c * pairs_heads + 2 * slab
        gain_s[slab] = pair_row(gain, head)
        shift_s[slab] = pair_row(shift, head)
        bias_two = pair_row(second_b, head)
        b2[slab, 0] = bias_two - half_mean(bias_two, left[:1])
        for half in range(2):
            b1[slab, half] = first_b[pl.ds(head + half, 1), :]
            rights[slab, half, 0:before] = jnp.zeros((before, hidden), jnp.bfloat16)
            rights[slab, half, before:seq] = fw[2 * slab + half]
            whole = sw[2 * slab + half].astype(jnp.float32)
            whole = whole - jnp.mean(whole, axis=0, keepdims=True)
            w2m[slab, half * HD : (half + 1) * HD] = whole
            w2b[slab, 0, half * HD : (half + 1) * HD] = whole.astype(jnp.bfloat16)

    def average(cells):
        return dot_nn(cells.astype(jnp.bfloat16), averager[...])

    def parted(cells):
        return jnp.concatenate(
            [jnp.where(left, cells, 0.0), jnp.where(left, 0.0, cells)], axis=0
        ).astype(jnp.bfloat16)

    def joined(cells):
        return jnp.where(left, cells[:MB], cells[MB:])

    def masked_tile(cells, base, limit, causal):
        cols = np.arange(LANE)[None, :] + base
        reach = limit + (np.arange(MB)[:, None] if causal else -1)
        allowed = np.broadcast_to((cols <= reach) & (cols < before), (MB, LANE))
        kept = allowed | (cols >= before)
        if not kept.any():
            return jnp.zeros((MB, LANE), jnp.bfloat16)
        col_ids = lane_ids + base
        if allowed.all():
            cells = cells + 1.0
        elif allowed.any():
            inside = col_ids <= (limit + batch_row_ids if causal else limit - 1)
            inside = inside & (col_ids < before)
            cells = cells + jnp.where(inside, 1.0, 0.0)
            if not kept.all():
                cells = jnp.where(inside | (col_ids >= before), cells, 0.0)
        elif not kept.all():
            cells = jnp.where(col_ids >= before, cells, 0.0)
        return cells.astype(jnp.bfloat16)

    def inner_setup(slab, part):
        rows = slice(part * tok, (part + 1) * tok)
        head = c * pairs_heads + 2 * slab
        upright = jnp.concatenate(
            [jnp.broadcast_to(rates[part, head + half], (HD, tok)) for half in range(2)], axis=0
        )
        rate_s[slab, rows] = -(upright.T * live[rows])
        known = min((part + 1) * tok, before)
        query, key, value = (i_rows[slab, kind, rows] for kind in range(3))
        both = jnp.concatenate([key, query], axis=0)
        keys = i_rows[slab, 1, 0 : (part + 1) * tok].astype(jnp.float32)
        left_keys = left_seq[0 : (part + 1) * tok]
        key_parts = (
            jnp.where(left_keys, keys, 0.0).astype(jnp.bfloat16),
            jnp.where(left_keys, 0.0, keys).astype(jnp.bfloat16),
        )
        spare = [jnp.zeros((before - known, LANE), jnp.bfloat16)] if known < before else []
        blocks = tok // MB
        for half in range(2):
            against = jnp.concatenate(
                [key_parts[half][:known]] + spare + [pickers[half * HD : (half + 1) * HD]], axis=0
            )
            product = dot_nt(both, against)
            for block in range(2 * blocks):
                batch = part * blocks + block % blocks
                causal = block >= blocks
                target = causal * seq + batch * MB
                for base in range(0, seq, LANE):
                    lefts[slab, half, target : target + MB, base : base + LANE] = masked_tile(
                        product[block * MB : (block + 1) * MB, base : base + LANE],
                        base,
                        batch * MB,
                        causal,
                    )
        key_f = key.astype(jnp.float32)
        pull = gain_s[slab] * (shift_s[slab] - (value.astype(jnp.float32) - key_f))
        pulls[slab, rows] = pull
        pull_means[slab, rows] = average(pull)
        if (part + 1) * tok == seq:
            last = slice(before, seq)
            own = dot_nt(
                query[before - part * tok :],
                jnp.concatenate([cells[last] for cells in key_parts], axis=0),
            )
            own = (jnp.concatenate([own, own], axis=0) + 1.0) * tri_pair[...]
            own_s[slab] = own.astype(jnp.bfloat16)

    def query_step(slab, batch, pre):
        hidden_b = hiddens[slab, batch]
        pair_two = twos[slab, batch]
        rows = slice(batch * MB, (batch + 1) * MB)
        query_act = gelu_only(pre).astype(jnp.bfloat16)
        second_kernel = (dot_nt(query_act, hidden_b) + 1.0) * tri_pair[...]
        query_out = dot_nt(query_act, w2b[slab, batch]) + dot_nn(
            second_kernel.astype(jnp.bfloat16), pair_two
        )
        query_out = joined(query_out) + b2[slab, batch]
        inv_std = lax.rsqrt(average(query_out * query_out) + 1e-06)
        query = i_rows[slab, 0, rows, :].astype(jnp.float32)
        inner[slab, rows, :] = query + gain_s[slab] * (query_out * inv_std) + shift_s[slab]

    def inner_step(slab, batch):
        rows = slice(batch * MB, (batch + 1) * MB)
        final = batch == batches - 1
        blocks = [batch] + ([batches + batch - 1] if batch else []) + (
            [batches + batch] if final else []
        )
        pres = []
        for half in range(2):
            used = jnp.concatenate(
                [lefts[slab, half, at * MB : (at + 1) * MB] for at in blocks], axis=0
            )
            pres.append(dot_nn(used, rights[slab, half]) + b1[slab, half])

        def picked(at):
            return jnp.concatenate([pre[at * MB : (at + 1) * MB] for pre in pres], axis=0)

        hidden_act, slope = gelu_and_slope(picked(0))
        hidden_b = hidden_act.astype(jnp.bfloat16)
        hiddens[slab, batch] = hidden_b
        norm_gain = gain_s[slab]
        squared_gain = norm_gain * norm_gain
        bias_two = b2[slab, batch]
        center = joined(dot_nt(hidden_b, w2b[slab, batch])) + bias_two
        square = center * center
        pulled = pulls[slab, rows]
        means = average(
            jnp.concatenate(
                [square, squared_gain * center, squared_gain * square, pulled * center], axis=0
            )
        )
        var, lin, quad, cross = (means[at * MB : (at + 1) * MB] for at in range(4))
        inv_std = lax.rsqrt(var + 1e-06)
        normed = center * inv_std
        scaled = squared_gain * normed + pulled
        along = inv_std * (inv_std * quad + cross)
        grad_two = inv_std * (scaled - (inv_std * lin + pull_means[slab, rows]) - normed * along)
        two = grad_two * rate_s[slab, rows]
        pair_two = parted(two)
        twos[slab, batch] = pair_two
        one = (dot_nn(pair_two, w2b[slab, batch]) * slope).astype(jnp.bfloat16)
        if not final:
            for half in range(2):
                rights[slab, half, rows] = one[half * MB : (half + 1) * MB]
            updated = w2m[slab] + dot_tn(pair_two, hidden_b)
            w2m[slab] = updated
            w2b[slab, batch + 1] = updated.astype(jnp.bfloat16)
            b2[slab, batch + 1] = bias_two + jnp.sum(two, axis=0, keepdims=True)
        if batch:
            query_step(slab, batch - 1, picked(1))
        if final:
            query_step(slab, batch, picked(len(blocks) - 1) + dot_nn(own_s[slab], one))

    def to_video(src, video, spot, step):
        return pltpu.make_async_remote_copy(
            src_ref=src,
            dst_ref=gathered.at[v, spot],
            send_sem=z_send.at[0],
            recv_sem=z_recv.at[spot, step - 1],
            device_id={"video": video},
            device_id_type=MESH_ID,
        )

    def reached(step):
        target = lax.rem(v + step, count)
        return jnp.abs(target - v) < count - 1

    def spread(src, spot):
        copies = []
        for step in (2, 1, 3):
            copy = to_video(src, lax.rem(v + step, count), spot, step)

            copies.append((step, copy))
        return copies

    def launch(copies):
        for step, copy in copies:

            @pl.when(reached(step))
            def _(copy=copy):
                copy.start()


    def relays(spot):
        found = []
        for place, origin in ((1, count - 1), (count - 2, 0)):
            end = count - 1 - origin
            step = (end - origin) % count
            found.append(
                (
                    place,
                    origin,
                    pltpu.make_async_remote_copy(
                        src_ref=gathered.at[origin, spot],
                        dst_ref=gathered.at[origin, spot],
                        send_sem=relay_send.at[0],
                        recv_sem=z_recv.at[spot, step - 1],
                        device_id={"video": end},
                        device_id_type=MESH_ID,
                    ),
                )
            )
        return found

    def z_arrival(video, spot, step):
        return pltpu.make_async_remote_copy(
            src_ref=gathered.at[video, spot],
            dst_ref=gathered.at[video, spot],
            send_sem=z_send.at[0],
            recv_sem=z_recv.at[spot, step - 1],
            device_id={"video": video},
            device_id_type=MESH_ID,
        )

    def relay(spot):
        for place, origin, copy in relays(spot):

            @pl.when(v == place)
            def _(copy=copy, origin=origin, place=place):
                z_arrival(origin, spot, (place - origin) % count).wait_recv()
                copy.start()

    backs = []
    owns = []
    half_batches = batches // 2

    def attend(slab):
        query, key, value = (a_rows[slab, kind] for kind in range(3))
        scores = dot_nt(split_heads(query, left_seq), key) * HD ** (-0.5)
        halves = []
        for part in range(2):
            mine_scores = scores[part * seq : (part + 1) * seq] + bias[...]
            top = jnp.max(mine_scores, axis=-1, keepdims=True)
            weights = jnp.exp(mine_scores - top)
            mass = jnp.sum(weights, axis=-1, keepdims=True)
            halves.append(dot_nn(weights.astype(jnp.bfloat16), value) / mass)
        return jnp.where(left_seq, halves[0], halves[1])

    def combine(slab, attended, part):
        rows = slice(part * tok, (part + 1) * tok)
        gate_row = gate_s[:, columns(c, slab)]
        whole = attended[rows] + gate_row * inner[slab, rows]
        comb[slab, rows] = (whole * live[rows]).astype(jnp.bfloat16)

    backs += [
        to_partner(
            comb.at[slab, pl.ds(theirs, tok), :],
            gathered.at[v, c * slabs + slab],
            back_send.at[0],
            back_recv.at[slab],
        )
        for slab in range(slabs)
    ]

    @pl.when(c == 0)
    def _():
        for slab in range(slabs):
            inner_setup(slab, 0)
        for batch in range(half_batches):
            for slab in range(slabs):
                inner_step(slab, batch)

    pass_on(1)
    rate_out.wait_recv()
    for slab in range(slabs):
        rows_in(i_rows, slab, 0)

        @pl.when(c == 1)
        def _(slab=slab):
            inner_setup(slab, 0)
            for batch in range(half_batches):
                inner_step(slab, batch)
            inner_setup(slab, 1)
            inner_step(slab, half_batches)

        @pl.when(c == 0)
        def _(slab=slab):
            inner_setup(slab, 1)
            for batch in range(half_batches, batches):
                inner_step(slab, batch)

        if slab == 0:
            pass_on(2)
        if slab:
            far = other * slabs + slab - 1
            far_out = spread(gathered.at[v, far], far)

            def send_far(far_out=far_out, slab=slab):
                backs[slab - 1].wait_recv()
                launch(far_out)

            pl.when(c == 1)(send_far)
        a_loads[slab].wait()
        rows_in(a_rows, slab, slabs)
        @pl.when(c == 1)
        def _(slab=slab):
            attended = attend(slab)
            combine(slab, attended, 0)
            backs[slab].start()
            for batch in range(half_batches + 1, batches):
                inner_step(slab, batch)
            combine(slab, attended, 1)

        @pl.when(c == 0)
        def _(slab=slab):
            attended = attend(slab)
            combine(slab, attended, 1)
            backs[slab].start()
            combine(slab, attended, 0)

        if slab:
            pl.when(c == 0)(send_far)
        spot = c * slabs + slab
        if slab == 0:
            start_rows(slice(early, slabs))
        own = pltpu.make_async_copy(
            comb.at[slab, pl.ds(mine, tok), :], gathered.at[v, spot], own_sem.at[slab]
        )
        own.start()
        owns.append(own)
        if slab == 0:
            pass_on(3)
        near_out = spread(comb.at[slab, pl.ds(mine, tok), :], spot)
        launch(near_out)
        if slab:
            relay(spot - 1)
        if slab > 1:
            relay(other * slabs + slab - 2)
    ow_load.wait()
    for own in owns[:-1]:
        own.wait()

    chunks, _, _, chunk = parts.shape
    toward = 1 - 2 * (v // (count // 2))
    videos = [lax.rem(v + toward * near + count, count) for near in range(count)]

    def z_wait(video, spots):
        step = lax.rem(v - video + count, count)
        passed = ((v == 1) & (video == count - 1)) | ((v == count - 2) & (video == 0))

        @pl.when(jnp.logical_not(passed))
        def _():
            for spot in spots:
                z_arrival(video, spot, step).wait_recv()

    def rows_of(video, spots):
        return jnp.concatenate([gathered[video, spot] for spot in spots], axis=1)

    first_half = list(range(slabs - 1))
    second_half = list(range(slabs, 2 * slabs - 1))
    last_spots = [slabs - 1, 2 * slabs - 1]

    def begin(near):
        if slabs == 1:
            return
        video = videos[near]
        if near:
            z_wait(video, first_half + second_half)
        sums[near] = dot_nn(
            rows_of(video, first_half), ow[0 : (slabs - 1) * LANE]
        ) + dot_nn(
            rows_of(video, second_half), ow[slabs * LANE : (2 * slabs - 1) * LANE]
        )

    lane_of, core_of = h // 2, lax.rem(h, 2)
    sibling = 2 * lane_of + 1 - core_of
    across = 2 * (1 - lane_of) + core_of

    def owner_lane(video):
        return lax.rem(video + v, 2)

    def owner_core(video):
        return lax.rem(video // 2 + v // 2, 2)

    def owned(lane, core):
        return 2 * lax.rem(core + v // 2, 2) + lax.rem(lane + v, 2)

    def to_head_copy(src, dst, send, recv, head):
        return pltpu.make_async_remote_copy(
            src_ref=src,
            dst_ref=dst,
            send_sem=send,
            recv_sem=recv,
            device_id={"head": head},
            device_id_type=MESH_ID,
        )

    def part_copy(video, at):
        slot = lax.rem(owner_lane(video) + lane_of, 2)
        return to_head_copy(
            parts.at[at, video],
            beside.at[at, slot],
            s_send.at[0],
            s_recv.at[at, slot],
            sibling,
        )

    def finish(near):
        video = videos[near]
        if near:
            z_wait(video, last_spots)
        rest = jnp.concatenate(
            [ow[spot * LANE : (spot + 1) * LANE] for spot in last_spots], axis=0
        )
        piece = dot_nn(rows_of(video, last_spots), rest)
        if slabs > 1:
            piece = piece + sums[near]
        piece = piece.astype(jnp.bfloat16)
        for at in range(chunks):
            parts[at, video] = piece[:, at * chunk : (at + 1) * chunk]
            copy = part_copy(video, at)

            @pl.when(owner_core(video) != core_of)
            def _(copy=copy):
                copy.start()

    home, away = owned(lane_of, core_of), owned(1 - lane_of, core_of)
    to_head, to_v = v, home
    stays = (to_head == h) & (to_v == v)
    x_out = [
        to_head_copy(crossing.at[at], arrived.at[at], r_send.at[0], r_recv.at[at], across)
        for at in range(chunks)
    ]
    finals = [
        pltpu.make_async_remote_copy(
            src_ref=total.at[at],
            dst_ref=out.at[0, :, at * chunk : (at + 1) * chunk],
            send_sem=t_send.at[0],
            recv_sem=t_recv.at[0],
            device_id={"head": to_head, "video": to_v},
            device_id_type=MESH_ID,
        )
        for at in range(chunks)
    ]

    kept = [
        pltpu.make_async_copy(
            total.at[at], out.at[0, :, at * chunk : (at + 1) * chunk], t_send.at[0]
        )
        for at in range(chunks)
    ]

    def cross(near):
        @pl.when(videos[near] == away)
        def _():
            for at in range(chunks):
                part_copy(away, at).wait_recv()
                crossing[at] = (
                    parts[at, away].astype(jnp.float32) + beside[at, 1].astype(jnp.float32)
                ).astype(jnp.bfloat16)
                x_out[at].start()

    def arrive(near):
        @pl.when(videos[near] == home)
        def _():
            for at in range(chunks):
                part_copy(home, at).wait_recv()
                x_out[at].wait_recv()
                summed = parts[at, home].astype(jnp.float32) + beside[at, 0].astype(jnp.float32)
                total[at] = (summed + arrived[at].astype(jnp.float32)).astype(jnp.bfloat16)

                @pl.when(stays)
                def _(at=at):
                    kept[at].start()

                @pl.when(jnp.logical_not(stays))
                def _(at=at):
                    finals[at].start()

    begin(0)
    backs[slabs - 1].wait_recv()
    far = other * slabs + slabs - 1
    far_out = spread(gathered.at[v, far], far)
    launch(far_out)
    owns[-1].wait()
    finish(0)
    if slabs > 1:
        relay(far - 1)
    relay(c * slabs + slabs - 1)
    for near in range(1, count):
        begin(near)
    relay(far)
    for near in range(1, count):
        finish(near)
        cross(near - 1)
    cross(count - 1)
    for near in range(count):
        arrive(near)

    rate_out.wait_send()
    in_place(i_rows, y_send.at[0], y_recv.at[0]).wait_send()
    in_place(comb.at[:, 0:tok], back_send.at[0], y_recv.at[0]).wait_send()
    in_place(parts.at[:, 0:2], s_send.at[0], y_recv.at[0]).wait_send()
    in_place(crossing, r_send.at[0], y_recv.at[0]).wait_send()
    at_end = (v == 0) | (v == count - 1)

    @pl.when(at_end)
    def _():
        in_place(gathered.at[0:2], z_send.at[0], y_recv.at[0]).wait_send()

    @pl.when(jnp.logical_not(at_end))
    def _():
        in_place(gathered.at[0:3], z_send.at[0], y_recv.at[0]).wait_send()
        in_place(gathered.at[0], relay_send.at[0], y_recv.at[0]).wait_send()

    finished = in_place(total, t_send.at[0], t_recv.at[0])

    @pl.when(jnp.logical_not(stays))
    def _():
        finished.wait_recv()

    finished.wait_send()


def fused_on_device(
    attention_qkv,
    inner_qkv,
    learn_rate,
    segment_id,
    video_length,
    gate_alpha,
    inner_gain,
    inner_shift,
    first_weight,
    first_bias,
    second_weight,
    second_bias,
    out_weight,
):
    tok = attention_qkv.shape[2]
    width_dev = attention_qkv.shape[3]
    count = lax.axis_size("head")
    ctx_count = lax.axis_size("ctx")
    seq = tok * ctx_count
    slabs = width_dev // LANE // ctx_count
    heads = width_dev // HD
    hidden = first_weight.shape[2]
    columns = out_weight.shape[1]
    chunk = LANE
    chunks = columns // chunk
    half = jnp.bfloat16
    full = jnp.float32
    hbm = pl.BlockSpec(memory_space=pl.ANY)
    dma = pltpu.SemaphoreType.DMA
    return pl.pallas_call(
        fused_kernel,
        out_shape=pltpu.VMEM((1, tok, columns), half),
        in_specs=[hbm] * 13,
        out_specs=hbm,
        scratch_shapes=[
            pltpu.VMEM(segment_id.shape, segment_id.dtype),
            pltpu.SMEM(video_length.shape, video_length.dtype),
            pltpu.VMEM(gate_alpha.shape, full),
            pltpu.VMEM(inner_gain.shape, full),
            pltpu.VMEM(inner_shift.shape, full),
            pltpu.VMEM(first_bias.shape, full),
            pltpu.VMEM(second_bias.shape, full),
            dma((7,)),
            pltpu.VMEM((slabs, 3, seq, LANE), half),
            pltpu.VMEM((slabs, 3, seq, LANE), half),
            pltpu.VMEM((ctx_count, heads, 1, tok), full),
            pltpu.VMEM((2 * slabs,) + first_weight.shape[1:], half),
            pltpu.VMEM((2 * slabs,) + second_weight.shape[:0:-1], half),
            pltpu.VMEM(out_weight.shape, half),
            pltpu.VMEM((slabs, 2, 2 * seq, seq), half),
            pltpu.VMEM((slabs, 2, seq, hidden), half),
            pltpu.VMEM((slabs, LANE, hidden), full),
            pltpu.VMEM((slabs, seq // MB, LANE, hidden), half),
            pltpu.VMEM((slabs, 2, 1, hidden), full),
            pltpu.VMEM((slabs, seq // MB, 1, LANE), full),
            pltpu.VMEM((1, width_dev), full),
            pltpu.VMEM((slabs, 1, LANE), full),
            pltpu.VMEM((slabs, 1, LANE), full),
            pltpu.VMEM((slabs, seq, LANE), full),
            pltpu.VMEM((LANE, LANE), half),
            pltpu.VMEM((LANE, LANE), half),
            pltpu.VMEM((LANE, LANE), full),
            pltpu.VMEM((seq, seq), full),
            pltpu.VMEM((slabs, seq, LANE), full),
            pltpu.VMEM((slabs, seq, LANE), full),
            pltpu.VMEM((slabs, LANE, LANE), half),
            pltpu.VMEM((slabs, seq // MB, LANE, hidden), half),
            pltpu.VMEM((slabs, seq // MB, LANE, LANE), half),
            pltpu.VMEM((slabs, seq, LANE), full),
            pltpu.VMEM((slabs, seq, LANE), half),
            pltpu.VMEM((count, 2 * slabs, tok, LANE), half),
            pltpu.VMEM((count, tok, columns), full),
            pltpu.VMEM((chunks, count, tok, chunk), half),
            pltpu.VMEM((chunks, 2, tok, chunk), half),
            pltpu.VMEM((chunks, tok, chunk), half),
            pltpu.VMEM((chunks, tok, chunk), half),
            pltpu.VMEM((chunks, tok, chunk), half),
            dma((2 * slabs + 4,)),
            dma((2,)),
            dma((2 * slabs + 1,)),
            dma((1,)),
            dma((slabs,)),
            dma((1,)),
            dma((2 * slabs, count - 1)),
            dma((1,)),
            dma((slabs,)),
            dma((1,)),
            dma((chunks, 2)),
            dma((1,)),
            dma((chunks,)),
            dma((1,)),
            dma((1,)),
            pltpu.SemaphoreType.REGULAR,
            pltpu.SemaphoreType.REGULAR,
        ],
        compiler_params=pltpu.CompilerParams(
            collective_id=0, has_side_effects=True, vmem_limit_bytes=60 * 1024 * 1024
        ),
    )(
        attention_qkv,
        inner_qkv,
        learn_rate.transpose(1, 0, 2),
        first_weight,
        second_weight.transpose(0, 2, 1),
        out_weight,
        segment_id,
        video_length,
        gate_alpha,
        inner_gain,
        inner_shift,
        first_bias,
        second_bias,
    )


def general_on_device(
    attention_qkv,
    inner_qkv,
    learn_rate,
    segment_id,
    video_length,
    gate_alpha,
    inner_gain,
    inner_shift,
    first_weight,
    first_bias,
    second_weight,
    second_bias,
    out_weight,
):
    tok_count = attention_qkv.shape[2]
    width_dev = attention_qkv.shape[3]
    heads_dev = width_dev // HD
    ctx_index = lax.axis_index("ctx")
    ctx_count = lax.axis_size("ctx")
    positions = ctx_index * tok_count + jnp.arange(tok_count, dtype=jnp.int32)
    length_val = video_length[0]
    live_rows = (positions < length_val).astype(jnp.float32)
    kv_pair = attention_qkv[1:, 0]
    kv_wide = with_halo(kv_pair, (("ctx", 1),), tok_count)
    key_pos = (ctx_index - 1) * tok_count + jnp.arange(3 * tok_count, dtype=jnp.int32)
    seg_row = segment_id[0]
    fill_ids = jnp.full((tok_count,), -1, jnp.int32)
    seg_pad = jnp.concatenate([fill_ids, seg_row, fill_ids])
    key_seg = lax.dynamic_slice_in_dim(seg_pad, ctx_index * tok_count, 3 * tok_count, 0)
    query_seg = lax.dynamic_slice_in_dim(seg_row, ctx_index * tok_count, tok_count, 0)
    allowed = (key_seg[None, :] == query_seg[:, None]) & (
        (key_pos[None, :] < length_val) | (key_pos[None, :] == positions[:, None])
    )
    query_heads = attention_qkv[0, 0].reshape(tok_count, heads_dev, HD)
    key_heads = kv_wide[0].reshape(3 * tok_count, heads_dev, HD)
    value_heads = kv_wide[1].reshape(3 * tok_count, heads_dev, HD)
    scores = jnp.einsum(
        "qhd,khd->hqk", query_heads, key_heads, preferred_element_type=jnp.float32
    ) * HD ** (-0.5)
    scores = jnp.where(allowed[None], scores, -1e30)
    row_max = jnp.max(scores, axis=-1, keepdims=True)
    exp_scores = jnp.exp(scores - row_max)
    soft_weights = (exp_scores / jnp.sum(exp_scores, axis=-1, keepdims=True)).astype(jnp.bfloat16)
    attended = jnp.einsum(
        "hqk,khd->qhd", soft_weights, value_heads, preferred_element_type=jnp.float32
    ).reshape(tok_count, width_dev)
    init_state = (
        first_weight.astype(jnp.float32),
        first_bias,
        second_weight.astype(jnp.float32),
        second_bias,
    )
    rate_rows = learn_rate[0] * live_rows[None, :]
    heads_each = -(-heads_dev // ctx_count)
    heads_padded = heads_each * ctx_count
    rows_heads = inner_qkv[:, 0].reshape(3, tok_count, heads_dev, HD)
    rows_padded = jnp.concatenate(
        [rows_heads, jnp.zeros((3, tok_count, heads_padded - heads_dev, HD), rows_heads.dtype)],
        axis=2,
    )
    rates_padded = pad_heads(rate_rows, heads_padded, 0.0)
    whole_rows = lax.all_to_all(rows_padded, "ctx", split_axis=2, concat_axis=1, tiled=True)
    whole_rates = lax.all_to_all(rates_padded, "ctx", split_axis=0, concat_axis=1, tiled=True)
    seq_count = whole_rows.shape[1]
    full_batches = seq_count // MB
    local_qkv = (
        whole_rows.astype(jnp.float32)
        .transpose(0, 2, 1, 3)
        .reshape(3, heads_each, full_batches, MB, HD)
    )
    local_rates = whole_rates.reshape(heads_each, full_batches, MB)
    first_head = ctx_index * heads_each
    local_gain = lax.dynamic_slice_in_dim(
        pad_heads(inner_gain, heads_padded, 1.0), first_head, heads_each, 0
    )
    local_shift = lax.dynamic_slice_in_dim(
        pad_heads(inner_shift, heads_padded, 0.0), first_head, heads_each, 0
    )
    local_state = tuple(
        (
            lax.dynamic_slice_in_dim(
                pad_heads(piece_arr, heads_padded, 0.0), first_head, heads_each, 0
            )
            for piece_arr in init_state
        )
    )
    unused_final, saved_local = jax.vmap(partial(chain_scan, True))(
        local_state, local_qkv[0], local_qkv[1], local_qkv[2], local_rates, local_gain, local_shift
    )
    out_rows = saved_local.reshape(heads_each, seq_count, HD).transpose(1, 0, 2)
    back_rows = lax.all_to_all(
        out_rows.astype(jnp.bfloat16), "ctx", split_axis=0, concat_axis=1, tiled=True
    ).astype(out_rows.dtype)
    inner_flat = back_rows[:, :heads_dev].reshape(tok_count, width_dev)
    combined = ((attended + jnp.tanh(gate_alpha) * inner_flat) * live_rows[:, None]).astype(
        jnp.bfloat16
    )
    terms = jnp.dot(
        combined,
        lax.all_gather(out_weight, "video", axis=1, tiled=True),
        preferred_element_type=jnp.float32,
    )
    mixed = lax.psum_scatter(terms.astype(jnp.bfloat16), "head", scatter_dimension=1, tiled=True)
    return mixed[None]


def solution(mesh):
    placed = (
        P(None, "video", "ctx", "head"),
        P(None, "video", "ctx", "head"),
        P("video", "head", "ctx"),
        P("video", None),
        P("video"),
        P("head"),
        P("head", None),
        P("head", None),
        P("head", None, None),
        P("head", None),
        P("head", None, None),
        P("head", None),
        P("head", "video"),
    )
    shape = mesh.shape
    fused = shape["ctx"] == 2 and shape["head"] == shape["video"] == 4

    def on_device(*args):
        heads_dev = args[0].shape[3] // HD
        if fused and heads_dev % (2 * shape["ctx"]) == 0 and args[0].shape[2] % 128 == 0:
            return fused_on_device(*args)
        return general_on_device(*args)

    return jax.shard_map(
        on_device, mesh=mesh, in_specs=placed, out_specs=P("video", "ctx", "head"), check_vma=False
    )
```

```python
from functools import partial

import jax
import jax.numpy as jnp
import numpy as np
from jax import lax
from jax.experimental import pallas as pl
from jax.experimental.pallas import tpu as pltpu
from jax.sharding import PartitionSpec as P

HD = 64
MB = 64


gelu_scale = 0.7978845608028654
gelu_cubic = 0.044715


def with_halo(cells, sides, width):
    for axis, dim in sides:
        count = lax.axis_size(axis)
        ends = count - 1
        head = lax.slice_in_dim(cells, 0, width, axis=dim)
        tail = lax.slice_in_dim(cells, cells.shape[dim] - width, cells.shape[dim], axis=dim)
        cells = jnp.concatenate(
            [
                lax.ppermute(tail, axis, [(i, (i + 1) % count) for i in range(ends)]),
                cells,
                lax.ppermute(head, axis, [((i + 1) % count, i) for i in range(ends)]),
            ],
            axis=dim,
        )
    return cells


def matmul_high(first_op, second_op):
    return jnp.matmul(first_op, second_op, precision=lax.Precision.HIGHEST)


def gelu_pair(entries):
    inner_arg = gelu_scale * (entries + gelu_cubic * entries * entries * entries)
    tanh_val = jnp.tanh(inner_arg)
    act_val = 0.5 * entries * (1.0 + tanh_val)
    slope_val = 0.5 * (1.0 + tanh_val) + 0.5 * entries * (
        1.0 - tanh_val * tanh_val
    ) * gelu_scale * (1.0 + 3.0 * gelu_cubic * entries * entries)
    return (act_val, slope_val)


def layer_stats(summed):
    center = summed - jnp.mean(summed, axis=-1, keepdims=True)
    variance = jnp.mean(center * center, axis=-1, keepdims=True)
    inv_std = lax.rsqrt(variance + 1e-06)
    return (center * inv_std, inv_std)


def lower_mask(row_count):
    row_ids = lax.broadcasted_iota(jnp.int32, (row_count, row_count), 0)
    col_ids = lax.broadcasted_iota(jnp.int32, (row_count, row_count), 1)
    return (row_ids >= col_ids).astype(jnp.float32)


def inner_update(inner_state, key_mb, value_mb, rate_mb, norm_gain, norm_shift):
    weight_one, bias_one, weight_two, bias_two = inner_state
    hidden_pre = matmul_high(key_mb, weight_one) + bias_one
    hidden_act, hidden_slope = gelu_pair(hidden_pre)
    output_pre = matmul_high(hidden_act, weight_two) + bias_two
    normed, inv_std = layer_stats(output_pre)
    residual_err = norm_gain * normed + norm_shift - (value_mb - key_mb)
    scaled_err = residual_err * norm_gain
    grad_two = inv_std * (
        scaled_err
        - jnp.mean(scaled_err, axis=-1, keepdims=True)
        - normed * jnp.mean(scaled_err * normed, axis=-1, keepdims=True)
    )
    grad_one = matmul_high(grad_two, weight_two.T) * hidden_slope
    grad_one = grad_one * rate_mb[:, None]
    grad_two = grad_two * rate_mb[:, None]
    new_state = (
        weight_one - matmul_high(key_mb.T, grad_one),
        bias_one - jnp.sum(grad_one, axis=0),
        weight_two - matmul_high(hidden_act.T, grad_two),
        bias_two - jnp.sum(grad_two, axis=0),
    )
    return ((grad_one, hidden_act, grad_two), new_state)


def query_side(inner_state, query_mb, key_mb, grad_pack, norm_gain, norm_shift):
    weight_one, bias_one, weight_two, bias_two = inner_state
    grad_one, hidden_act, grad_two = grad_pack
    causal = lower_mask(query_mb.shape[0])
    first_kernel = (matmul_high(query_mb, key_mb.T) + 1.0) * causal
    query_pre = matmul_high(query_mb, weight_one) + bias_one - matmul_high(first_kernel, grad_one)
    query_act, unused_slope = gelu_pair(query_pre)
    second_kernel = (matmul_high(query_act, hidden_act.T) + 1.0) * causal
    query_out = matmul_high(query_act, weight_two) + bias_two - matmul_high(second_kernel, grad_two)
    normed, unused_inv = layer_stats(query_out)
    return query_mb + norm_gain * normed + norm_shift


def chain_scan(
    keep_queries, inner_state, queries, key_rows, values, rate_vals, norm_gain, norm_shift
):

    def stepper(loop_state, inputs):
        query_mb, key_mb, value_mb, rate_mb = inputs
        grad_pack, new_state = inner_update(
            loop_state, key_mb, value_mb, rate_mb, norm_gain, norm_shift
        )
        return (
            new_state,
            query_side(loop_state, query_mb, key_mb, grad_pack, norm_gain, norm_shift),
        )

    return lax.scan(stepper, inner_state, (queries, key_rows, values, rate_vals))


def pad_heads(array_in, total_heads, fill_value):
    extra = total_heads - array_in.shape[0]
    filler = jnp.full((extra,) + array_in.shape[1:], fill_value, array_in.dtype)
    return jnp.concatenate([array_in, filler], axis=0)


LANE = 128
MESH_ID = pl.DeviceIdType.MESH


def dot_nn(left, right):
    return lax.dot_general(
        left, right, (((1,), (0,)), ((), ())), preferred_element_type=jnp.float32
    )


def dot_nt(left, right):
    return lax.dot_general(
        left, right, (((1,), (1,)), ((), ())), preferred_element_type=jnp.float32
    )


def dot_tn(left, right):
    return lax.dot_general(
        left, right, (((0,), (0,)), ((), ())), preferred_element_type=jnp.float32
    )


def gelu_parts(entries):
    square = entries * entries
    inner_arg = entries * (gelu_scale + gelu_scale * gelu_cubic * square)
    half = 0.5 + 0.5 * jnp.tanh(inner_arg)
    return (square, half, entries * half)


def gelu_only(entries):
    return gelu_parts(entries)[2]


def gelu_and_slope(entries):
    square, half, act_val = gelu_parts(entries)
    ramp = 2.0 * gelu_scale + 6.0 * gelu_scale * gelu_cubic * square
    return (act_val, half + act_val * (1.0 - half) * ramp)


def half_mean(cells, left):
    first = jnp.sum(jnp.where(left, cells, 0.0), axis=-1, keepdims=True)
    second = jnp.sum(jnp.where(left, 0.0, cells), axis=-1, keepdims=True)
    return jnp.where(left, first, second) * (1.0 / HD)


def split_heads(cells, left):
    wide = cells.astype(jnp.float32)
    return jnp.concatenate(
        [jnp.where(left, wide, 0.0), jnp.where(left, 0.0, wide)], axis=0
    ).astype(cells.dtype)


def fused_kernel(
    aqkv,
    iqkv,
    rate,
    first_w,
    second_w,
    out_w,
    seg_in,
    length_in,
    gate_in,
    gain_in,
    shift_in,
    first_b_in,
    second_b_in,
    out,
    seg,
    length,
    gate,
    gain,
    shift,
    first_b,
    second_b,
    small_sem,
    a_rows,
    i_rows,
    rates,
    fw,
    sw,
    ow,
    lefts,
    rights,
    w2m,
    w2b,
    b1,
    b2,
    gate_s,
    gain_s,
    shift_s,
    rate_s,
    averager,
    pickers,
    tri_pair,
    bias,
    pulls,
    pull_means,
    own_s,
    hiddens,
    twos,
    inner,
    comb,
    gathered,
    sums,
    parts,
    beside,
    crossing,
    arrived,
    total,
    load_sem,
    y_send,
    y_recv,
    back_send,
    back_recv,
    z_send,
    z_recv,
    relay_send,
    own_sem,
    s_send,
    s_recv,
    r_send,
    r_recv,
    t_send,
    t_recv,
    low_sem,
    high_sem,
):
    slabs, _, seq, _ = a_rows.shape
    tok = aqkv.shape[2]
    hidden = first_b.shape[1]
    count = lax.axis_size("head")
    c = lax.axis_index("ctx")
    h = lax.axis_index("head")
    v = lax.axis_index("video")
    other = 1 - c
    mine = pl.multiple_of(c * tok, tok)
    theirs = pl.multiple_of(other * tok, tok)
    pairs_heads = 2 * slabs

    def columns(owner, slab):
        return pl.ds(pl.multiple_of((owner * slabs + slab) * LANE, LANE), LANE)

    barrier = pltpu.get_barrier_semaphore()
    pl.semaphore_signal(
        barrier, inc=1, device_id={"ctx": other}, device_id_type=MESH_ID
    )
    below, above = v > 0, v < count - 1
    for step in range(1, count):
        pl.semaphore_signal(
            barrier,
            inc=1,
            device_id={"head": lax.rem(h + step, count)},
            device_id_type=MESH_ID,
        )

    def tell(semaphore, inside, video):
        @pl.when(inside)
        def _():
            pl.semaphore_signal(
                semaphore, inc=1, device_id={"video": video}, device_id_type=MESH_ID
            )

    tell(barrier, below, v - 1)
    tell(barrier, above, v + 1)
    loads = []
    for slab in range(slabs):
        loads.append(
            pltpu.make_async_copy(
                iqkv.at[:, 0, :, columns(c, slab)],
                i_rows.at[slab, :, pl.ds(mine, tok), :],
                load_sem.at[slab],
            )
        )
    loads.append(pltpu.make_async_copy(rate, rates.at[c], load_sem.at[2 * slabs]))
    loads.append(
        pltpu.make_async_copy(
            first_w.at[pl.ds(c * pairs_heads, pairs_heads)], fw, load_sem.at[2 * slabs + 1]
        )
    )
    loads.append(
        pltpu.make_async_copy(
            second_w.at[pl.ds(c * pairs_heads, pairs_heads)], sw, load_sem.at[2 * slabs + 2]
        )
    )
    a_loads = [
        pltpu.make_async_copy(
            aqkv.at[:, 0, :, columns(c, slab)],
            a_rows.at[slab, :, pl.ds(mine, tok), :],
            load_sem.at[slabs + slab],
        )
        for slab in range(slabs)
    ]
    ow_load = pltpu.make_async_copy(out_w, ow, load_sem.at[2 * slabs + 3])
    for copy in loads + a_loads + [ow_load]:
        copy.start()

    small_loads = [
        pltpu.make_async_copy(source, kept_in, small_sem.at[at])
        for at, (source, kept_in) in enumerate(
            (
                (seg_in, seg),
                (length_in, length),
                (gate_in, gate),
                (gain_in, gain),
                (shift_in, shift),
                (first_b_in, first_b),
                (second_b_in, second_b),
            )
        )
    ]
    for copy in small_loads:
        copy.start()
    pl.semaphore_wait(barrier, count + (v + count - 1) // count + (2 * count - 2 - v) // count)

    def to_partner(src, dst, send, recv):
        return pltpu.make_async_remote_copy(
            src_ref=src,
            dst_ref=dst,
            send_sem=send,
            recv_sem=recv,
            device_id={"ctx": other},
            device_id_type=MESH_ID,
        )

    rate_out = to_partner(
        rate, rates.at[c], y_send.at[1], y_recv.at[2 * slabs]
    )
    rate_out.start()

    def rows_out(source, target, slab, base):
        return [
            to_partner(
                source.at[kind, 0, :, columns(other, slab)],
                target.at[slab, kind, pl.ds(mine, tok), :],
                y_send.at[0],
                y_recv.at[base + slab],
            )
            for kind in range(3)
        ]

    i_out = [rows_out(iqkv, i_rows, slab, 0) for slab in range(slabs)]
    a_out = [rows_out(aqkv, a_rows, slab, slabs) for slab in range(slabs)]
    early = max(slabs - 1, 1)

    def in_place(ref, send, recv):
        return to_partner(ref, ref, send, recv)

    def rows_in(target, slab, base):
        in_place(
            target.at[slab, :, pl.ds(theirs, tok), :], y_send.at[0], y_recv.at[base + slab]
        ).wait_recv()

    def start_rows(part):
        for copies in zip(i_out[part], a_out[part]):
            for copy in copies[0] + copies[1]:
                copy.start()

    start_rows(slice(0, early))

    tell(low_sem, v == 0, v + 1)
    tell(high_sem, v == count - 1, v - 1)

    def pass_on(stage):
        for semaphore, here, video, last in (
            (low_sem, v == stage, v + 1, above),
            (high_sem, v == count - 1 - stage, v - 1, below),
        ):

            @pl.when(here)
            def _(semaphore=semaphore):
                pl.semaphore_wait(semaphore, 1)

            tell(semaphore, jnp.logical_and(here, last), video)

    for copy in small_loads:
        copy.wait()
    seq_ids = lax.broadcasted_iota(jnp.int32, (seq, seq), 1)
    row_ids = lax.broadcasted_iota(jnp.int32, (seq, seq), 0)
    len_val = length[0]
    segs = jnp.broadcast_to(seg[...].astype(jnp.float32), (seq, seq))
    allowed = (segs == segs.T) & ((seq_ids < len_val) | (seq_ids == row_ids))
    bias[...] = jnp.where(allowed, 0.0, -1e30)
    live = (lax.broadcasted_iota(jnp.int32, (seq, LANE), 0) < len_val).astype(jnp.float32)
    left = lax.broadcasted_iota(jnp.int32, (MB, LANE), 1) < HD
    left_seq = lax.broadcasted_iota(jnp.int32, (seq, LANE), 1) < HD
    pair_row_ids = lax.broadcasted_iota(jnp.int32, (LANE, LANE), 0)
    pair_col_ids = lax.broadcasted_iota(jnp.int32, (LANE, LANE), 1)
    same = (pair_row_ids < HD) == (pair_col_ids < HD)
    tri_pair[...] = jnp.where(same & (pair_row_ids >= pair_col_ids), 1.0, 0.0)
    averager[...] = jnp.where(same, 1.0 / HD, 0.0).astype(jnp.bfloat16)
    pickers[...] = jnp.where(pair_row_ids == pair_col_ids, 1.0, 0.0).astype(jnp.bfloat16)
    batches = seq // MB
    before = seq - MB
    lane_ids = lax.broadcasted_iota(jnp.int32, (MB, LANE), 1)
    batch_row_ids = lax.broadcasted_iota(jnp.int32, (MB, LANE), 0)

    gate_s[...] = jnp.tanh(gate[...].reshape(1, gate.shape[0]))

    for copy in loads:
        copy.wait()

    def pair_row(ref, head):
        return jnp.concatenate([ref[pl.ds(head, 1), :], ref[pl.ds(head + 1, 1), :]], axis=1)

    for slab in range(slabs):
        head = c * pairs_heads + 2 * slab
        gain_s[slab] = pair_row(gain, head)
        shift_s[slab] = pair_row(shift, head)
        bias_two = pair_row(second_b, head)
        b2[slab, 0] = bias_two - half_mean(bias_two, left[:1])
        for half in range(2):
            b1[slab, half] = first_b[pl.ds(head + half, 1), :]
            rights[slab, half, 0:before] = jnp.zeros((before, hidden), jnp.bfloat16)
            rights[slab, half, before:seq] = fw[2 * slab + half]
            whole = sw[2 * slab + half].astype(jnp.float32)
            whole = whole - jnp.mean(whole, axis=0, keepdims=True)
            w2m[slab, half * HD : (half + 1) * HD] = whole
            w2b[slab, 0, half * HD : (half + 1) * HD] = whole.astype(jnp.bfloat16)

    def average(cells):
        return dot_nn(cells.astype(jnp.bfloat16), averager[...])

    def parted(cells):
        return jnp.concatenate(
            [jnp.where(left, cells, 0.0), jnp.where(left, 0.0, cells)], axis=0
        ).astype(jnp.bfloat16)

    def joined(cells):
        return jnp.where(left, cells[:MB], cells[MB:])

    def masked_tile(cells, base, limit, causal):
        cols = np.arange(LANE)[None, :] + base
        reach = limit + (np.arange(MB)[:, None] if causal else -1)
        allowed = np.broadcast_to((cols <= reach) & (cols < before), (MB, LANE))
        kept = allowed | (cols >= before)
        if not kept.any():
            return jnp.zeros((MB, LANE), jnp.bfloat16)
        col_ids = lane_ids + base
        if allowed.all():
            cells = cells + 1.0
        elif allowed.any():
            inside = col_ids <= (limit + batch_row_ids if causal else limit - 1)
            inside = inside & (col_ids < before)
            cells = cells + jnp.where(inside, 1.0, 0.0)
            if not kept.all():
                cells = jnp.where(inside | (col_ids >= before), cells, 0.0)
        elif not kept.all():
            cells = jnp.where(col_ids >= before, cells, 0.0)
        return cells.astype(jnp.bfloat16)

    def inner_setup(slab, part):
        rows = slice(part * tok, (part + 1) * tok)
        head = c * pairs_heads + 2 * slab
        upright = jnp.concatenate(
            [jnp.broadcast_to(rates[part, head + half], (HD, tok)) for half in range(2)], axis=0
        )
        rate_s[slab, rows] = -(upright.T * live[rows])
        known = min((part + 1) * tok, before)
        query, key, value = (i_rows[slab, kind, rows] for kind in range(3))
        both = jnp.concatenate([key, query], axis=0)
        keys = i_rows[slab, 1, 0 : (part + 1) * tok].astype(jnp.float32)
        left_keys = left_seq[0 : (part + 1) * tok]
        key_parts = (
            jnp.where(left_keys, keys, 0.0).astype(jnp.bfloat16),
            jnp.where(left_keys, 0.0, keys).astype(jnp.bfloat16),
        )
        spare = [jnp.zeros((before - known, LANE), jnp.bfloat16)] if known < before else []
        blocks = tok // MB
        for half in range(2):
            against = jnp.concatenate(
                [key_parts[half][:known]] + spare + [pickers[half * HD : (half + 1) * HD]], axis=0
            )
            product = dot_nt(both, against)
            for block in range(2 * blocks):
                batch = part * blocks + block % blocks
                causal = block >= blocks
                target = causal * seq + batch * MB
                for base in range(0, seq, LANE):
                    lefts[slab, half, target : target + MB, base : base + LANE] = masked_tile(
                        product[block * MB : (block + 1) * MB, base : base + LANE],
                        base,
                        batch * MB,
                        causal,
                    )
        key_f = key.astype(jnp.float32)
        pull = gain_s[slab] * (shift_s[slab] - (value.astype(jnp.float32) - key_f))
        pulls[slab, rows] = pull
        pull_means[slab, rows] = average(pull)
        if (part + 1) * tok == seq:
            last = slice(before, seq)
            own = dot_nt(
                query[before - part * tok :],
                jnp.concatenate([cells[last] for cells in key_parts], axis=0),
            )
            own = (jnp.concatenate([own, own], axis=0) + 1.0) * tri_pair[...]
            own_s[slab] = own.astype(jnp.bfloat16)

    def query_step(slab, batch, pre):
        hidden_b = hiddens[slab, batch]
        pair_two = twos[slab, batch]
        rows = slice(batch * MB, (batch + 1) * MB)
        query_act = gelu_only(pre).astype(jnp.bfloat16)
        second_kernel = (dot_nt(query_act, hidden_b) + 1.0) * tri_pair[...]
        query_out = dot_nt(query_act, w2b[slab, batch]) + dot_nn(
            second_kernel.astype(jnp.bfloat16), pair_two
        )
        query_out = joined(query_out) + b2[slab, batch]
        inv_std = lax.rsqrt(average(query_out * query_out) + 1e-06)
        query = i_rows[slab, 0, rows, :].astype(jnp.float32)
        inner[slab, rows, :] = query + gain_s[slab] * (query_out * inv_std) + shift_s[slab]

    def inner_step(slab, batch):
        rows = slice(batch * MB, (batch + 1) * MB)
        final = batch == batches - 1
        blocks = [batch] + ([batches + batch - 1] if batch else []) + (
            [batches + batch] if final else []
        )
        pres = []
        for half in range(2):
            used = jnp.concatenate(
                [lefts[slab, half, at * MB : (at + 1) * MB] for at in blocks], axis=0
            )
            pres.append(dot_nn(used, rights[slab, half]) + b1[slab, half])

        def picked(at):
            return jnp.concatenate([pre[at * MB : (at + 1) * MB] for pre in pres], axis=0)

        hidden_act, slope = gelu_and_slope(picked(0))
        hidden_b = hidden_act.astype(jnp.bfloat16)
        hiddens[slab, batch] = hidden_b
        norm_gain = gain_s[slab]
        squared_gain = norm_gain * norm_gain
        bias_two = b2[slab, batch]
        center = joined(dot_nt(hidden_b, w2b[slab, batch])) + bias_two
        square = center * center
        pulled = pulls[slab, rows]
        means = average(
            jnp.concatenate(
                [square, squared_gain * center, squared_gain * square, pulled * center], axis=0
            )
        )
        var, lin, quad, cross = (means[at * MB : (at + 1) * MB] for at in range(4))
        inv_std = lax.rsqrt(var + 1e-06)
        normed = center * inv_std
        scaled = squared_gain * normed + pulled
        along = inv_std * (inv_std * quad + cross)
        grad_two = inv_std * (scaled - (inv_std * lin + pull_means[slab, rows]) - normed * along)
        two = grad_two * rate_s[slab, rows]
        pair_two = parted(two)
        twos[slab, batch] = pair_two
        one = (dot_nn(pair_two, w2b[slab, batch]) * slope).astype(jnp.bfloat16)
        if not final:
            for half in range(2):
                rights[slab, half, rows] = one[half * MB : (half + 1) * MB]
            updated = w2m[slab] + dot_tn(pair_two, hidden_b)
            w2m[slab] = updated
            w2b[slab, batch + 1] = updated.astype(jnp.bfloat16)
            b2[slab, batch + 1] = bias_two + jnp.sum(two, axis=0, keepdims=True)
        if batch:
            query_step(slab, batch - 1, picked(1))
        if final:
            query_step(slab, batch, picked(len(blocks) - 1) + dot_nn(own_s[slab], one))

    def to_video(src, video, spot, step):
        return pltpu.make_async_remote_copy(
            src_ref=src,
            dst_ref=gathered.at[v, spot],
            send_sem=z_send.at[0],
            recv_sem=z_recv.at[spot, step - 1],
            device_id={"video": video},
            device_id_type=MESH_ID,
        )

    def reached(step):
        target = lax.rem(v + step, count)
        return jnp.abs(target - v) < count - 1

    def spread(src, spot):
        copies = []
        for step in (2, 1, 3):
            copy = to_video(src, lax.rem(v + step, count), spot, step)

            copies.append((step, copy))
        return copies

    def launch(copies):
        for step, copy in copies:

            @pl.when(reached(step))
            def _(copy=copy):
                copy.start()


    def relays(spot):
        found = []
        for place, origin in ((1, count - 1), (count - 2, 0)):
            end = count - 1 - origin
            step = (end - origin) % count
            found.append(
                (
                    place,
                    origin,
                    pltpu.make_async_remote_copy(
                        src_ref=gathered.at[origin, spot],
                        dst_ref=gathered.at[origin, spot],
                        send_sem=relay_send.at[0],
                        recv_sem=z_recv.at[spot, step - 1],
                        device_id={"video": end},
                        device_id_type=MESH_ID,
                    ),
                )
            )
        return found

    def z_arrival(video, spot, step):
        return pltpu.make_async_remote_copy(
            src_ref=gathered.at[video, spot],
            dst_ref=gathered.at[video, spot],
            send_sem=z_send.at[0],
            recv_sem=z_recv.at[spot, step - 1],
            device_id={"video": video},
            device_id_type=MESH_ID,
        )

    def relay(spot):
        for place, origin, copy in relays(spot):

            @pl.when(v == place)
            def _(copy=copy, origin=origin, place=place):
                z_arrival(origin, spot, (place - origin) % count).wait_recv()
                copy.start()

    backs = []
    owns = []
    half_batches = batches // 2

    def attend(slab):
        query, key, value = (a_rows[slab, kind] for kind in range(3))
        scores = dot_nt(split_heads(query, left_seq), key) * HD ** (-0.5)
        halves = []
        for part in range(2):
            mine_scores = scores[part * seq : (part + 1) * seq] + bias[...]
            top = jnp.max(mine_scores, axis=-1, keepdims=True)
            weights = jnp.exp(mine_scores - top)
            mass = jnp.sum(weights, axis=-1, keepdims=True)
            halves.append(dot_nn(weights.astype(jnp.bfloat16), value) / mass)
        return jnp.where(left_seq, halves[0], halves[1])

    def combine(slab, attended, part):
        rows = slice(part * tok, (part + 1) * tok)
        gate_row = gate_s[:, columns(c, slab)]
        whole = attended[rows] + gate_row * inner[slab, rows]
        comb[slab, rows] = (whole * live[rows]).astype(jnp.bfloat16)

    backs += [
        to_partner(
            comb.at[slab, pl.ds(theirs, tok), :],
            gathered.at[v, c * slabs + slab],
            back_send.at[0],
            back_recv.at[slab],
        )
        for slab in range(slabs)
    ]

    @pl.when(c == 0)
    def _():
        for slab in range(slabs):
            inner_setup(slab, 0)
        for batch in range(half_batches):
            for slab in range(slabs):
                inner_step(slab, batch)

    pass_on(1)
    rate_out.wait_recv()
    for slab in range(slabs):
        rows_in(i_rows, slab, 0)

        @pl.when(c == 1)
        def _(slab=slab):
            inner_setup(slab, 0)
            for batch in range(half_batches):
                inner_step(slab, batch)
            inner_setup(slab, 1)
            inner_step(slab, half_batches)

        @pl.when(c == 0)
        def _(slab=slab):
            inner_setup(slab, 1)
            for batch in range(half_batches, batches):
                inner_step(slab, batch)

        if slab == 0:
            pass_on(2)
        if slab:
            far = other * slabs + slab - 1
            far_out = spread(gathered.at[v, far], far)

            def send_far(far_out=far_out, slab=slab):
                backs[slab - 1].wait_recv()
                launch(far_out)

            pl.when(c == 1)(send_far)
        a_loads[slab].wait()
        rows_in(a_rows, slab, slabs)
        @pl.when(c == 1)
        def _(slab=slab):
            attended = attend(slab)
            combine(slab, attended, 0)
            backs[slab].start()
            for batch in range(half_batches + 1, batches):
                inner_step(slab, batch)
            combine(slab, attended, 1)

        @pl.when(c == 0)
        def _(slab=slab):
            attended = attend(slab)
            combine(slab, attended, 1)
            backs[slab].start()
            combine(slab, attended, 0)

        if slab:
            pl.when(c == 0)(send_far)
        spot = c * slabs + slab
        if slab == 0:
            start_rows(slice(early, slabs))
        own = pltpu.make_async_copy(
            comb.at[slab, pl.ds(mine, tok), :], gathered.at[v, spot], own_sem.at[slab]
        )
        own.start()
        owns.append(own)
        if slab == 0:
            pass_on(3)
        near_out = spread(comb.at[slab, pl.ds(mine, tok), :], spot)
        launch(near_out)
        if slab:
            relay(spot - 1)
        if slab > 1:
            relay(other * slabs + slab - 2)
    ow_load.wait()
    for own in owns[:-1]:
        own.wait()

    chunks, _, _, chunk = parts.shape
    toward = 1 - 2 * (v // (count // 2))
    videos = [lax.rem(v + toward * near + count, count) for near in range(count)]

    def z_wait(video, spots):
        step = lax.rem(v - video + count, count)
        passed = ((v == 1) & (video == count - 1)) | ((v == count - 2) & (video == 0))

        @pl.when(jnp.logical_not(passed))
        def _():
            for spot in spots:
                z_arrival(video, spot, step).wait_recv()

    def rows_of(video, spots):
        return jnp.concatenate([gathered[video, spot] for spot in spots], axis=1)

    first_half = list(range(slabs - 1))
    second_half = list(range(slabs, 2 * slabs - 1))
    last_spots = [slabs - 1, 2 * slabs - 1]

    def begin(near):
        if slabs == 1:
            return
        video = videos[near]
        if near:
            z_wait(video, first_half + second_half)
        sums[near] = dot_nn(
            rows_of(video, first_half), ow[0 : (slabs - 1) * LANE]
        ) + dot_nn(
            rows_of(video, second_half), ow[slabs * LANE : (2 * slabs - 1) * LANE]
        )

    lane_of, core_of = h // 2, lax.rem(h, 2)
    sibling = 2 * lane_of + 1 - core_of
    across = 2 * (1 - lane_of) + core_of

    swapped = lax.rem(v // 2 + v, 2)

    def owner_lane(video):
        return lax.rem(video + v + (1 - video // 2) * swapped, 2)

    def owner_core(video):
        return lax.rem(video // 2 + v // 2, 2)

    def owned(lane, core):
        upper = lax.rem(core + v // 2, 2)
        return 2 * upper + lax.rem(lane + v + (1 - upper) * swapped, 2)

    def to_head_copy(src, dst, send, recv, head):
        return pltpu.make_async_remote_copy(
            src_ref=src,
            dst_ref=dst,
            send_sem=send,
            recv_sem=recv,
            device_id={"head": head},
            device_id_type=MESH_ID,
        )

    def part_copy(video, at):
        slot = lax.rem(owner_lane(video) + lane_of, 2)
        return to_head_copy(
            parts.at[at, video],
            beside.at[at, slot],
            s_send.at[0],
            s_recv.at[at, slot],
            sibling,
        )

    def finish(near):
        video = videos[near]
        if near:
            z_wait(video, last_spots)
        rest = jnp.concatenate(
            [ow[spot * LANE : (spot + 1) * LANE] for spot in last_spots], axis=0
        )
        piece = dot_nn(rows_of(video, last_spots), rest)
        if slabs > 1:
            piece = piece + sums[near]
        piece = piece.astype(jnp.bfloat16)
        for at in range(chunks):
            parts[at, video] = piece[:, at * chunk : (at + 1) * chunk]
            copy = part_copy(video, at)

            @pl.when(owner_core(video) != core_of)
            def _(copy=copy):
                copy.start()

    home, away = owned(lane_of, core_of), owned(1 - lane_of, core_of)
    to_head, to_v = v, home
    stays = (to_head == h) & (to_v == v)
    x_out = [
        to_head_copy(crossing.at[at], arrived.at[at], r_send.at[0], r_recv.at[at], across)
        for at in range(chunks)
    ]
    finals = [
        pltpu.make_async_remote_copy(
            src_ref=total.at[at],
            dst_ref=out.at[0, :, at * chunk : (at + 1) * chunk],
            send_sem=t_send.at[0],
            recv_sem=t_recv.at[0],
            device_id={"head": to_head, "video": to_v},
            device_id_type=MESH_ID,
        )
        for at in range(chunks)
    ]

    kept = [
        pltpu.make_async_copy(
            total.at[at], out.at[0, :, at * chunk : (at + 1) * chunk], t_send.at[0]
        )
        for at in range(chunks)
    ]

    def cross(near):
        @pl.when(videos[near] == away)
        def _():
            for at in range(chunks):
                part_copy(away, at).wait_recv()
                crossing[at] = (
                    parts[at, away].astype(jnp.float32) + beside[at, 1].astype(jnp.float32)
                ).astype(jnp.bfloat16)
                x_out[at].start()

    def arrive(near):
        @pl.when(videos[near] == home)
        def _():
            for at in range(chunks):
                part_copy(home, at).wait_recv()
                x_out[at].wait_recv()
                summed = parts[at, home].astype(jnp.float32) + beside[at, 0].astype(jnp.float32)
                total[at] = (summed + arrived[at].astype(jnp.float32)).astype(jnp.bfloat16)

                @pl.when(stays)
                def _(at=at):
                    kept[at].start()

                @pl.when(jnp.logical_not(stays))
                def _(at=at):
                    finals[at].start()

    begin(0)
    backs[slabs - 1].wait_recv()
    far = other * slabs + slabs - 1
    far_out = spread(gathered.at[v, far], far)
    launch(far_out)
    owns[-1].wait()
    finish(0)
    if slabs > 1:
        relay(far - 1)
    relay(c * slabs + slabs - 1)
    for near in range(1, count):
        begin(near)
    relay(far)
    for near in range(1, count):
        finish(near)
        cross(near - 1)
    cross(count - 1)
    for near in range(count):
        arrive(near)

    rate_out.wait_send()
    in_place(i_rows, y_send.at[0], y_recv.at[0]).wait_send()
    in_place(comb.at[:, 0:tok], back_send.at[0], y_recv.at[0]).wait_send()
    in_place(parts.at[:, 0:2], s_send.at[0], y_recv.at[0]).wait_send()
    in_place(crossing, r_send.at[0], y_recv.at[0]).wait_send()
    at_end = (v == 0) | (v == count - 1)

    @pl.when(at_end)
    def _():
        in_place(gathered.at[0:2], z_send.at[0], y_recv.at[0]).wait_send()

    @pl.when(jnp.logical_not(at_end))
    def _():
        in_place(gathered.at[0:3], z_send.at[0], y_recv.at[0]).wait_send()
        in_place(gathered.at[0], relay_send.at[0], y_recv.at[0]).wait_send()

    finished = in_place(total, t_send.at[0], t_recv.at[0])

    @pl.when(jnp.logical_not(stays))
    def _():
        finished.wait_recv()

    finished.wait_send()


def fused_on_device(
    attention_qkv,
    inner_qkv,
    learn_rate,
    segment_id,
    video_length,
    gate_alpha,
    inner_gain,
    inner_shift,
    first_weight,
    first_bias,
    second_weight,
    second_bias,
    out_weight,
):
    tok = attention_qkv.shape[2]
    width_dev = attention_qkv.shape[3]
    count = lax.axis_size("head")
    ctx_count = lax.axis_size("ctx")
    seq = tok * ctx_count
    slabs = width_dev // LANE // ctx_count
    heads = width_dev // HD
    hidden = first_weight.shape[2]
    columns = out_weight.shape[1]
    chunk = LANE
    chunks = columns // chunk
    half = jnp.bfloat16
    full = jnp.float32
    hbm = pl.BlockSpec(memory_space=pl.ANY)
    dma = pltpu.SemaphoreType.DMA
    return pl.pallas_call(
        fused_kernel,
        out_shape=pltpu.VMEM((1, tok, columns), half),
        in_specs=[hbm] * 13,
        out_specs=hbm,
        scratch_shapes=[
            pltpu.VMEM(segment_id.shape, segment_id.dtype),
            pltpu.SMEM(video_length.shape, video_length.dtype),
            pltpu.VMEM(gate_alpha.shape, full),
            pltpu.VMEM(inner_gain.shape, full),
            pltpu.VMEM(inner_shift.shape, full),
            pltpu.VMEM(first_bias.shape, full),
            pltpu.VMEM(second_bias.shape, full),
            dma((7,)),
            pltpu.VMEM((slabs, 3, seq, LANE), half),
            pltpu.VMEM((slabs, 3, seq, LANE), half),
            pltpu.VMEM((ctx_count, heads, 1, tok), full),
            pltpu.VMEM((2 * slabs,) + first_weight.shape[1:], half),
            pltpu.VMEM((2 * slabs,) + second_weight.shape[:0:-1], half),
            pltpu.VMEM(out_weight.shape, half),
            pltpu.VMEM((slabs, 2, 2 * seq, seq), half),
            pltpu.VMEM((slabs, 2, seq, hidden), half),
            pltpu.VMEM((slabs, LANE, hidden), full),
            pltpu.VMEM((slabs, seq // MB, LANE, hidden), half),
            pltpu.VMEM((slabs, 2, 1, hidden), full),
            pltpu.VMEM((slabs, seq // MB, 1, LANE), full),
            pltpu.VMEM((1, width_dev), full),
            pltpu.VMEM((slabs, 1, LANE), full),
            pltpu.VMEM((slabs, 1, LANE), full),
            pltpu.VMEM((slabs, seq, LANE), full),
            pltpu.VMEM((LANE, LANE), half),
            pltpu.VMEM((LANE, LANE), half),
            pltpu.VMEM((LANE, LANE), full),
            pltpu.VMEM((seq, seq), full),
            pltpu.VMEM((slabs, seq, LANE), full),
            pltpu.VMEM((slabs, seq, LANE), full),
            pltpu.VMEM((slabs, LANE, LANE), half),
            pltpu.VMEM((slabs, seq // MB, LANE, hidden), half),
            pltpu.VMEM((slabs, seq // MB, LANE, LANE), half),
            pltpu.VMEM((slabs, seq, LANE), full),
            pltpu.VMEM((slabs, seq, LANE), half),
            pltpu.VMEM((count, 2 * slabs, tok, LANE), half),
            pltpu.VMEM((count, tok, columns), full),
            pltpu.VMEM((chunks, count, tok, chunk), half),
            pltpu.VMEM((chunks, 2, tok, chunk), half),
            pltpu.VMEM((chunks, tok, chunk), half),
            pltpu.VMEM((chunks, tok, chunk), half),
            pltpu.VMEM((chunks, tok, chunk), half),
            dma((2 * slabs + 4,)),
            dma((2,)),
            dma((2 * slabs + 1,)),
            dma((1,)),
            dma((slabs,)),
            dma((1,)),
            dma((2 * slabs, count - 1)),
            dma((1,)),
            dma((slabs,)),
            dma((1,)),
            dma((chunks, 2)),
            dma((1,)),
            dma((chunks,)),
            dma((1,)),
            dma((1,)),
            pltpu.SemaphoreType.REGULAR,
            pltpu.SemaphoreType.REGULAR,
        ],
        compiler_params=pltpu.CompilerParams(
            collective_id=0, has_side_effects=True, vmem_limit_bytes=60 * 1024 * 1024
        ),
    )(
        attention_qkv,
        inner_qkv,
        learn_rate.transpose(1, 0, 2),
        first_weight,
        second_weight.transpose(0, 2, 1),
        out_weight,
        segment_id,
        video_length,
        gate_alpha,
        inner_gain,
        inner_shift,
        first_bias,
        second_bias,
    )


def general_on_device(
    attention_qkv,
    inner_qkv,
    learn_rate,
    segment_id,
    video_length,
    gate_alpha,
    inner_gain,
    inner_shift,
    first_weight,
    first_bias,
    second_weight,
    second_bias,
    out_weight,
):
    tok_count = attention_qkv.shape[2]
    width_dev = attention_qkv.shape[3]
    heads_dev = width_dev // HD
    ctx_index = lax.axis_index("ctx")
    ctx_count = lax.axis_size("ctx")
    positions = ctx_index * tok_count + jnp.arange(tok_count, dtype=jnp.int32)
    length_val = video_length[0]
    live_rows = (positions < length_val).astype(jnp.float32)
    kv_pair = attention_qkv[1:, 0]
    kv_wide = with_halo(kv_pair, (("ctx", 1),), tok_count)
    key_pos = (ctx_index - 1) * tok_count + jnp.arange(3 * tok_count, dtype=jnp.int32)
    seg_row = segment_id[0]
    fill_ids = jnp.full((tok_count,), -1, jnp.int32)
    seg_pad = jnp.concatenate([fill_ids, seg_row, fill_ids])
    key_seg = lax.dynamic_slice_in_dim(seg_pad, ctx_index * tok_count, 3 * tok_count, 0)
    query_seg = lax.dynamic_slice_in_dim(seg_row, ctx_index * tok_count, tok_count, 0)
    allowed = (key_seg[None, :] == query_seg[:, None]) & (
        (key_pos[None, :] < length_val) | (key_pos[None, :] == positions[:, None])
    )
    query_heads = attention_qkv[0, 0].reshape(tok_count, heads_dev, HD)
    key_heads = kv_wide[0].reshape(3 * tok_count, heads_dev, HD)
    value_heads = kv_wide[1].reshape(3 * tok_count, heads_dev, HD)
    scores = jnp.einsum(
        "qhd,khd->hqk", query_heads, key_heads, preferred_element_type=jnp.float32
    ) * HD ** (-0.5)
    scores = jnp.where(allowed[None], scores, -1e30)
    row_max = jnp.max(scores, axis=-1, keepdims=True)
    exp_scores = jnp.exp(scores - row_max)
    soft_weights = (exp_scores / jnp.sum(exp_scores, axis=-1, keepdims=True)).astype(jnp.bfloat16)
    attended = jnp.einsum(
        "hqk,khd->qhd", soft_weights, value_heads, preferred_element_type=jnp.float32
    ).reshape(tok_count, width_dev)
    init_state = (
        first_weight.astype(jnp.float32),
        first_bias,
        second_weight.astype(jnp.float32),
        second_bias,
    )
    rate_rows = learn_rate[0] * live_rows[None, :]
    heads_each = -(-heads_dev // ctx_count)
    heads_padded = heads_each * ctx_count
    rows_heads = inner_qkv[:, 0].reshape(3, tok_count, heads_dev, HD)
    rows_padded = jnp.concatenate(
        [rows_heads, jnp.zeros((3, tok_count, heads_padded - heads_dev, HD), rows_heads.dtype)],
        axis=2,
    )
    rates_padded = pad_heads(rate_rows, heads_padded, 0.0)
    whole_rows = lax.all_to_all(rows_padded, "ctx", split_axis=2, concat_axis=1, tiled=True)
    whole_rates = lax.all_to_all(rates_padded, "ctx", split_axis=0, concat_axis=1, tiled=True)
    seq_count = whole_rows.shape[1]
    full_batches = seq_count // MB
    local_qkv = (
        whole_rows.astype(jnp.float32)
        .transpose(0, 2, 1, 3)
        .reshape(3, heads_each, full_batches, MB, HD)
    )
    local_rates = whole_rates.reshape(heads_each, full_batches, MB)
    first_head = ctx_index * heads_each
    local_gain = lax.dynamic_slice_in_dim(
        pad_heads(inner_gain, heads_padded, 1.0), first_head, heads_each, 0
    )
    local_shift = lax.dynamic_slice_in_dim(
        pad_heads(inner_shift, heads_padded, 0.0), first_head, heads_each, 0
    )
    local_state = tuple(
        (
            lax.dynamic_slice_in_dim(
                pad_heads(piece_arr, heads_padded, 0.0), first_head, heads_each, 0
            )
            for piece_arr in init_state
        )
    )
    unused_final, saved_local = jax.vmap(partial(chain_scan, True))(
        local_state, local_qkv[0], local_qkv[1], local_qkv[2], local_rates, local_gain, local_shift
    )
    out_rows = saved_local.reshape(heads_each, seq_count, HD).transpose(1, 0, 2)
    back_rows = lax.all_to_all(
        out_rows.astype(jnp.bfloat16), "ctx", split_axis=0, concat_axis=1, tiled=True
    ).astype(out_rows.dtype)
    inner_flat = back_rows[:, :heads_dev].reshape(tok_count, width_dev)
    combined = ((attended + jnp.tanh(gate_alpha) * inner_flat) * live_rows[:, None]).astype(
        jnp.bfloat16
    )
    terms = jnp.dot(
        combined,
        lax.all_gather(out_weight, "video", axis=1, tiled=True),
        preferred_element_type=jnp.float32,
    )
    mixed = lax.psum_scatter(terms.astype(jnp.bfloat16), "head", scatter_dimension=1, tiled=True)
    return mixed[None]


def solution(mesh):
    placed = (
        P(None, "video", "ctx", "head"),
        P(None, "video", "ctx", "head"),
        P("video", "head", "ctx"),
        P("video", None),
        P("video"),
        P("head"),
        P("head", None),
        P("head", None),
        P("head", None, None),
        P("head", None),
        P("head", None, None),
        P("head", None),
        P("head", "video"),
    )
    shape = mesh.shape
    fused = shape["ctx"] == 2 and shape["head"] == shape["video"] == 4

    def on_device(*args):
        heads_dev = args[0].shape[3] // HD
        if fused and heads_dev % (2 * shape["ctx"]) == 0 and args[0].shape[2] % 128 == 0:
            return fused_on_device(*args)
        return general_on_device(*args)

    return jax.shard_map(
        on_device, mesh=mesh, in_specs=placed, out_specs=P("video", "ctx", "head"), check_vma=False
    )
```

```python
from functools import partial

import jax
import jax.numpy as jnp
import numpy as np
from jax import lax
from jax.experimental import pallas as pl
from jax.experimental.pallas import tpu as pltpu
from jax.sharding import PartitionSpec as P

HD = 64
MB = 64


gelu_scale = 0.7978845608028654
gelu_cubic = 0.044715


def with_halo(cells, sides, width):
    for axis, dim in sides:
        count = lax.axis_size(axis)
        ends = count - 1
        head = lax.slice_in_dim(cells, 0, width, axis=dim)
        tail = lax.slice_in_dim(cells, cells.shape[dim] - width, cells.shape[dim], axis=dim)
        cells = jnp.concatenate(
            [
                lax.ppermute(tail, axis, [(i, (i + 1) % count) for i in range(ends)]),
                cells,
                lax.ppermute(head, axis, [((i + 1) % count, i) for i in range(ends)]),
            ],
            axis=dim,
        )
    return cells


def matmul_high(first_op, second_op):
    return jnp.matmul(first_op, second_op, precision=lax.Precision.HIGHEST)


def gelu_pair(entries):
    inner_arg = gelu_scale * (entries + gelu_cubic * entries * entries * entries)
    tanh_val = jnp.tanh(inner_arg)
    act_val = 0.5 * entries * (1.0 + tanh_val)
    slope_val = 0.5 * (1.0 + tanh_val) + 0.5 * entries * (
        1.0 - tanh_val * tanh_val
    ) * gelu_scale * (1.0 + 3.0 * gelu_cubic * entries * entries)
    return (act_val, slope_val)


def layer_stats(summed):
    center = summed - jnp.mean(summed, axis=-1, keepdims=True)
    variance = jnp.mean(center * center, axis=-1, keepdims=True)
    inv_std = lax.rsqrt(variance + 1e-06)
    return (center * inv_std, inv_std)


def lower_mask(row_count):
    row_ids = lax.broadcasted_iota(jnp.int32, (row_count, row_count), 0)
    col_ids = lax.broadcasted_iota(jnp.int32, (row_count, row_count), 1)
    return (row_ids >= col_ids).astype(jnp.float32)


def inner_update(inner_state, key_mb, value_mb, rate_mb, norm_gain, norm_shift):
    weight_one, bias_one, weight_two, bias_two = inner_state
    hidden_pre = matmul_high(key_mb, weight_one) + bias_one
    hidden_act, hidden_slope = gelu_pair(hidden_pre)
    output_pre = matmul_high(hidden_act, weight_two) + bias_two
    normed, inv_std = layer_stats(output_pre)
    residual_err = norm_gain * normed + norm_shift - (value_mb - key_mb)
    scaled_err = residual_err * norm_gain
    grad_two = inv_std * (
        scaled_err
        - jnp.mean(scaled_err, axis=-1, keepdims=True)
        - normed * jnp.mean(scaled_err * normed, axis=-1, keepdims=True)
    )
    grad_one = matmul_high(grad_two, weight_two.T) * hidden_slope
    grad_one = grad_one * rate_mb[:, None]
    grad_two = grad_two * rate_mb[:, None]
    new_state = (
        weight_one - matmul_high(key_mb.T, grad_one),
        bias_one - jnp.sum(grad_one, axis=0),
        weight_two - matmul_high(hidden_act.T, grad_two),
        bias_two - jnp.sum(grad_two, axis=0),
    )
    return ((grad_one, hidden_act, grad_two), new_state)


def query_side(inner_state, query_mb, key_mb, grad_pack, norm_gain, norm_shift):
    weight_one, bias_one, weight_two, bias_two = inner_state
    grad_one, hidden_act, grad_two = grad_pack
    causal = lower_mask(query_mb.shape[0])
    first_kernel = (matmul_high(query_mb, key_mb.T) + 1.0) * causal
    query_pre = matmul_high(query_mb, weight_one) + bias_one - matmul_high(first_kernel, grad_one)
    query_act, unused_slope = gelu_pair(query_pre)
    second_kernel = (matmul_high(query_act, hidden_act.T) + 1.0) * causal
    query_out = matmul_high(query_act, weight_two) + bias_two - matmul_high(second_kernel, grad_two)
    normed, unused_inv = layer_stats(query_out)
    return query_mb + norm_gain * normed + norm_shift


def chain_scan(
    keep_queries, inner_state, queries, key_rows, values, rate_vals, norm_gain, norm_shift
):

    def stepper(loop_state, inputs):
        query_mb, key_mb, value_mb, rate_mb = inputs
        grad_pack, new_state = inner_update(
            loop_state, key_mb, value_mb, rate_mb, norm_gain, norm_shift
        )
        return (
            new_state,
            query_side(loop_state, query_mb, key_mb, grad_pack, norm_gain, norm_shift),
        )

    return lax.scan(stepper, inner_state, (queries, key_rows, values, rate_vals))


def pad_heads(array_in, total_heads, fill_value):
    extra = total_heads - array_in.shape[0]
    filler = jnp.full((extra,) + array_in.shape[1:], fill_value, array_in.dtype)
    return jnp.concatenate([array_in, filler], axis=0)


LANE = 128
MESH_ID = pl.DeviceIdType.MESH


def dot_nn(left, right):
    return lax.dot_general(
        left, right, (((1,), (0,)), ((), ())), preferred_element_type=jnp.float32
    )


def dot_nt(left, right):
    return lax.dot_general(
        left, right, (((1,), (1,)), ((), ())), preferred_element_type=jnp.float32
    )


def dot_tn(left, right):
    return lax.dot_general(
        left, right, (((0,), (0,)), ((), ())), preferred_element_type=jnp.float32
    )


def gelu_parts(entries):
    square = entries * entries
    inner_arg = entries * (gelu_scale + gelu_scale * gelu_cubic * square)
    half = 0.5 + 0.5 * jnp.tanh(inner_arg)
    return (square, half, entries * half)


def gelu_only(entries):
    return gelu_parts(entries)[2]


def gelu_and_slope(entries):
    square, half, act_val = gelu_parts(entries)
    ramp = 2.0 * gelu_scale + 6.0 * gelu_scale * gelu_cubic * square
    return (act_val, half + act_val * (1.0 - half) * ramp)


def half_mean(cells, left):
    first = jnp.sum(jnp.where(left, cells, 0.0), axis=-1, keepdims=True)
    second = jnp.sum(jnp.where(left, 0.0, cells), axis=-1, keepdims=True)
    return jnp.where(left, first, second) * (1.0 / HD)


def split_heads(cells, left):
    wide = cells.astype(jnp.float32)
    return jnp.concatenate(
        [jnp.where(left, wide, 0.0), jnp.where(left, 0.0, wide)], axis=0
    ).astype(cells.dtype)


def fused_kernel(
    aqkv,
    iqkv,
    rate,
    first_w,
    second_w,
    out_w,
    seg_in,
    length_in,
    gate_in,
    gain_in,
    shift_in,
    first_b_in,
    second_b_in,
    out,
    seg,
    length,
    gate,
    gain,
    shift,
    first_b,
    second_b,
    small_sem,
    a_rows,
    i_rows,
    rates,
    fw,
    sw,
    ow,
    lefts,
    rights,
    w2m,
    w2b,
    b1,
    b2,
    gate_s,
    gain_s,
    shift_s,
    rate_s,
    averager,
    pickers,
    tri_pair,
    bias,
    pulls,
    pull_means,
    own_s,
    hiddens,
    twos,
    inner,
    comb,
    gathered,
    sums,
    parts,
    beside,
    crossing,
    arrived,
    total,
    load_sem,
    y_send,
    y_recv,
    back_send,
    back_recv,
    z_send,
    z_recv,
    relay_send,
    own_sem,
    s_send,
    s_recv,
    r_send,
    r_recv,
    t_send,
    t_recv,
    low_sem,
    high_sem,
):
    slabs, _, seq, _ = a_rows.shape
    tok = aqkv.shape[2]
    hidden = first_b.shape[1]
    count = lax.axis_size("head")
    c = lax.axis_index("ctx")
    h = lax.axis_index("head")
    v = lax.axis_index("video")
    other = 1 - c
    mine = pl.multiple_of(c * tok, tok)
    theirs = pl.multiple_of(other * tok, tok)
    pairs_heads = 2 * slabs

    def columns(owner, slab):
        return pl.ds(pl.multiple_of((owner * slabs + slab) * LANE, LANE), LANE)

    barrier = pltpu.get_barrier_semaphore()
    pl.semaphore_signal(
        barrier, inc=1, device_id={"ctx": other}, device_id_type=MESH_ID
    )
    below, above = v > 0, v < count - 1
    for step in range(1, count):
        pl.semaphore_signal(
            barrier,
            inc=1,
            device_id={"head": lax.rem(h + step, count)},
            device_id_type=MESH_ID,
        )

    def tell(semaphore, inside, video):
        @pl.when(inside)
        def _():
            pl.semaphore_signal(
                semaphore, inc=1, device_id={"video": video}, device_id_type=MESH_ID
            )

    tell(barrier, below, v - 1)
    tell(barrier, above, v + 1)
    loads = []
    for slab in range(slabs):
        loads.append(
            pltpu.make_async_copy(
                iqkv.at[:, 0, :, columns(c, slab)],
                i_rows.at[slab, :, pl.ds(mine, tok), :],
                load_sem.at[slab],
            )
        )
    loads.append(pltpu.make_async_copy(rate, rates.at[c], load_sem.at[2 * slabs]))
    loads.append(
        pltpu.make_async_copy(
            first_w.at[pl.ds(c * pairs_heads, pairs_heads)], fw, load_sem.at[2 * slabs + 1]
        )
    )
    loads.append(
        pltpu.make_async_copy(
            second_w.at[pl.ds(c * pairs_heads, pairs_heads)], sw, load_sem.at[2 * slabs + 2]
        )
    )
    a_loads = [
        pltpu.make_async_copy(
            aqkv.at[:, 0, :, columns(c, slab)],
            a_rows.at[slab, :, pl.ds(mine, tok), :],
            load_sem.at[slabs + slab],
        )
        for slab in range(slabs)
    ]
    ow_load = pltpu.make_async_copy(out_w, ow, load_sem.at[2 * slabs + 3])
    for copy in loads + a_loads + [ow_load]:
        copy.start()

    small_loads = [
        pltpu.make_async_copy(source, kept_in, small_sem.at[at])
        for at, (source, kept_in) in enumerate(
            (
                (seg_in, seg),
                (length_in, length),
                (gate_in, gate),
                (gain_in, gain),
                (shift_in, shift),
                (first_b_in, first_b),
                (second_b_in, second_b),
            )
        )
    ]
    for copy in small_loads:
        copy.start()
    pl.semaphore_wait(barrier, count + (v + count - 1) // count + (2 * count - 2 - v) // count)

    def to_partner(src, dst, send, recv):
        return pltpu.make_async_remote_copy(
            src_ref=src,
            dst_ref=dst,
            send_sem=send,
            recv_sem=recv,
            device_id={"ctx": other},
            device_id_type=MESH_ID,
        )

    rate_out = to_partner(
        rate, rates.at[c], y_send.at[1], y_recv.at[2 * slabs]
    )
    rate_out.start()

    def rows_out(source, target, slab, base):
        return [
            to_partner(
                source.at[kind, 0, :, columns(other, slab)],
                target.at[slab, kind, pl.ds(mine, tok), :],
                y_send.at[0],
                y_recv.at[base + slab],
            )
            for kind in range(3)
        ]

    i_out = [rows_out(iqkv, i_rows, slab, 0) for slab in range(slabs)]
    a_out = [rows_out(aqkv, a_rows, slab, slabs) for slab in range(slabs)]
    early = max(slabs - 1, 1)

    def in_place(ref, send, recv):
        return to_partner(ref, ref, send, recv)

    def rows_in(target, slab, base):
        in_place(
            target.at[slab, :, pl.ds(theirs, tok), :], y_send.at[0], y_recv.at[base + slab]
        ).wait_recv()

    def start_rows(part):
        for copies in zip(i_out[part], a_out[part]):
            for copy in copies[0] + copies[1]:
                copy.start()

    start_rows(slice(0, early))

    tell(low_sem, v == 0, v + 1)
    tell(high_sem, v == count - 1, v - 1)

    def pass_on(stage):
        for semaphore, here, video, last in (
            (low_sem, v == stage, v + 1, above),
            (high_sem, v == count - 1 - stage, v - 1, below),
        ):

            @pl.when(here)
            def _(semaphore=semaphore):
                pl.semaphore_wait(semaphore, 1)

            tell(semaphore, jnp.logical_and(here, last), video)

    for copy in small_loads:
        copy.wait()
    seq_ids = lax.broadcasted_iota(jnp.int32, (seq, seq), 1)
    row_ids = lax.broadcasted_iota(jnp.int32, (seq, seq), 0)
    len_val = length[0]
    segs = jnp.broadcast_to(seg[...].astype(jnp.float32), (seq, seq))
    allowed = (segs == segs.T) & ((seq_ids < len_val) | (seq_ids == row_ids))
    bias[...] = jnp.where(allowed, 0.0, -1e30)
    live = (lax.broadcasted_iota(jnp.int32, (seq, LANE), 0) < len_val).astype(jnp.float32)
    left = lax.broadcasted_iota(jnp.int32, (MB, LANE), 1) < HD
    left_seq = lax.broadcasted_iota(jnp.int32, (seq, LANE), 1) < HD
    pair_row_ids = lax.broadcasted_iota(jnp.int32, (LANE, LANE), 0)
    pair_col_ids = lax.broadcasted_iota(jnp.int32, (LANE, LANE), 1)
    same = (pair_row_ids < HD) == (pair_col_ids < HD)
    tri_pair[...] = jnp.where(same & (pair_row_ids >= pair_col_ids), 1.0, 0.0)
    averager[...] = jnp.where(same, 1.0 / HD, 0.0).astype(jnp.bfloat16)
    pickers[...] = jnp.where(pair_row_ids == pair_col_ids, 1.0, 0.0).astype(jnp.bfloat16)
    batches = seq // MB
    before = seq - MB
    lane_ids = lax.broadcasted_iota(jnp.int32, (MB, LANE), 1)
    batch_row_ids = lax.broadcasted_iota(jnp.int32, (MB, LANE), 0)

    gate_s[...] = jnp.tanh(gate[...].reshape(1, gate.shape[0]))

    for copy in loads:
        copy.wait()

    def pair_row(ref, head):
        return jnp.concatenate([ref[pl.ds(head, 1), :], ref[pl.ds(head + 1, 1), :]], axis=1)

    for slab in range(slabs):
        head = c * pairs_heads + 2 * slab
        gain_s[slab] = pair_row(gain, head)
        shift_s[slab] = pair_row(shift, head)
        bias_two = pair_row(second_b, head)
        b2[slab, 0] = bias_two - half_mean(bias_two, left[:1])
        for half in range(2):
            b1[slab, half] = first_b[pl.ds(head + half, 1), :]
            rights[slab, half, 0:before] = jnp.zeros((before, hidden), jnp.bfloat16)
            rights[slab, half, before:seq] = fw[2 * slab + half]
            whole = sw[2 * slab + half].astype(jnp.float32)
            whole = whole - jnp.mean(whole, axis=0, keepdims=True)
            w2m[slab, half * HD : (half + 1) * HD] = whole
            w2b[slab, 0, half * HD : (half + 1) * HD] = whole.astype(jnp.bfloat16)

    def average(cells):
        return dot_nn(cells.astype(jnp.bfloat16), averager[...])

    def parted(cells):
        return jnp.concatenate(
            [jnp.where(left, cells, 0.0), jnp.where(left, 0.0, cells)], axis=0
        ).astype(jnp.bfloat16)

    def joined(cells):
        return jnp.where(left, cells[:MB], cells[MB:])

    def masked_tile(cells, base, limit, causal):
        cols = np.arange(LANE)[None, :] + base
        reach = limit + (np.arange(MB)[:, None] if causal else -1)
        allowed = np.broadcast_to((cols <= reach) & (cols < before), (MB, LANE))
        kept = allowed | (cols >= before)
        if not kept.any():
            return jnp.zeros((MB, LANE), jnp.bfloat16)
        col_ids = lane_ids + base
        if allowed.all():
            cells = cells + 1.0
        elif allowed.any():
            inside = col_ids <= (limit + batch_row_ids if causal else limit - 1)
            inside = inside & (col_ids < before)
            cells = cells + jnp.where(inside, 1.0, 0.0)
            if not kept.all():
                cells = jnp.where(inside | (col_ids >= before), cells, 0.0)
        elif not kept.all():
            cells = jnp.where(col_ids >= before, cells, 0.0)
        return cells.astype(jnp.bfloat16)

    def inner_setup(slab, part):
        rows = slice(part * tok, (part + 1) * tok)
        head = c * pairs_heads + 2 * slab
        upright = jnp.concatenate(
            [jnp.broadcast_to(rates[part, head + half], (HD, tok)) for half in range(2)], axis=0
        )
        rate_s[slab, rows] = -(upright.T * live[rows])
        known = min((part + 1) * tok, before)
        query, key, value = (i_rows[slab, kind, rows] for kind in range(3))
        both = jnp.concatenate([key, query], axis=0)
        keys = i_rows[slab, 1, 0 : (part + 1) * tok].astype(jnp.float32)
        left_keys = left_seq[0 : (part + 1) * tok]
        key_parts = (
            jnp.where(left_keys, keys, 0.0).astype(jnp.bfloat16),
            jnp.where(left_keys, 0.0, keys).astype(jnp.bfloat16),
        )
        spare = [jnp.zeros((before - known, LANE), jnp.bfloat16)] if known < before else []
        blocks = tok // MB
        for half in range(2):
            against = jnp.concatenate(
                [key_parts[half][:known]] + spare + [pickers[half * HD : (half + 1) * HD]], axis=0
            )
            product = dot_nt(both, against)
            for block in range(2 * blocks):
                batch = part * blocks + block % blocks
                causal = block >= blocks
                target = causal * seq + batch * MB
                for base in range(0, seq, LANE):
                    lefts[slab, half, target : target + MB, base : base + LANE] = masked_tile(
                        product[block * MB : (block + 1) * MB, base : base + LANE],
                        base,
                        batch * MB,
                        causal,
                    )
        key_f = key.astype(jnp.float32)
        pull = gain_s[slab] * (shift_s[slab] - (value.astype(jnp.float32) - key_f))
        pulls[slab, rows] = pull
        pull_means[slab, rows] = average(pull)
        if (part + 1) * tok == seq:
            last = slice(before, seq)
            own = dot_nt(
                query[before - part * tok :],
                jnp.concatenate([cells[last] for cells in key_parts], axis=0),
            )
            own = (jnp.concatenate([own, own], axis=0) + 1.0) * tri_pair[...]
            own_s[slab] = own.astype(jnp.bfloat16)

    def query_step(slab, batch, pre):
        hidden_b = hiddens[slab, batch]
        pair_two = twos[slab, batch]
        rows = slice(batch * MB, (batch + 1) * MB)
        query_act = gelu_only(pre).astype(jnp.bfloat16)
        second_kernel = (dot_nt(query_act, hidden_b) + 1.0) * tri_pair[...]
        query_out = dot_nt(query_act, w2b[slab, batch]) + dot_nn(
            second_kernel.astype(jnp.bfloat16), pair_two
        )
        query_out = joined(query_out) + b2[slab, batch]
        inv_std = lax.rsqrt(average(query_out * query_out) + 1e-06)
        query = i_rows[slab, 0, rows, :].astype(jnp.float32)
        inner[slab, rows, :] = query + gain_s[slab] * (query_out * inv_std) + shift_s[slab]

    def inner_step(slab, batch):
        rows = slice(batch * MB, (batch + 1) * MB)
        final = batch == batches - 1
        blocks = [batch] + ([batches + batch - 1] if batch else []) + (
            [batches + batch] if final else []
        )
        pres = []
        for half in range(2):
            used = jnp.concatenate(
                [lefts[slab, half, at * MB : (at + 1) * MB] for at in blocks], axis=0
            )
            pres.append(dot_nn(used, rights[slab, half]) + b1[slab, half])

        def picked(at):
            return jnp.concatenate([pre[at * MB : (at + 1) * MB] for pre in pres], axis=0)

        hidden_act, slope = gelu_and_slope(picked(0))
        hidden_b = hidden_act.astype(jnp.bfloat16)
        hiddens[slab, batch] = hidden_b
        norm_gain = gain_s[slab]
        squared_gain = norm_gain * norm_gain
        bias_two = b2[slab, batch]
        center = joined(dot_nt(hidden_b, w2b[slab, batch])) + bias_two
        square = center * center
        pulled = pulls[slab, rows]
        means = average(
            jnp.concatenate(
                [square, squared_gain * center, squared_gain * square, pulled * center], axis=0
            )
        )
        var, lin, quad, cross = (means[at * MB : (at + 1) * MB] for at in range(4))
        inv_std = lax.rsqrt(var + 1e-06)
        normed = center * inv_std
        scaled = squared_gain * normed + pulled
        along = inv_std * (inv_std * quad + cross)
        grad_two = inv_std * (scaled - (inv_std * lin + pull_means[slab, rows]) - normed * along)
        two = grad_two * rate_s[slab, rows]
        pair_two = parted(two)
        twos[slab, batch] = pair_two
        one = (dot_nn(pair_two, w2b[slab, batch]) * slope).astype(jnp.bfloat16)
        if not final:
            for half in range(2):
                rights[slab, half, rows] = one[half * MB : (half + 1) * MB]
            updated = w2m[slab] + dot_tn(pair_two, hidden_b)
            w2m[slab] = updated
            w2b[slab, batch + 1] = updated.astype(jnp.bfloat16)
            b2[slab, batch + 1] = bias_two + jnp.sum(two, axis=0, keepdims=True)
        if batch:
            query_step(slab, batch - 1, picked(1))
        if final:
            query_step(slab, batch, picked(len(blocks) - 1) + dot_nn(own_s[slab], one))

    def to_video(src, video, spot, step):
        return pltpu.make_async_remote_copy(
            src_ref=src,
            dst_ref=gathered.at[v, spot],
            send_sem=z_send.at[0],
            recv_sem=z_recv.at[spot, step - 1],
            device_id={"video": video},
            device_id_type=MESH_ID,
        )

    def reached(step):
        target = lax.rem(v + step, count)
        return jnp.abs(target - v) < count - 1

    def spread(src, spot):
        copies = []
        for step in (2, 1, 3):
            copy = to_video(src, lax.rem(v + step, count), spot, step)

            copies.append((step, copy))
        return copies

    def launch(copies):
        for step, copy in copies:

            @pl.when(reached(step))
            def _(copy=copy):
                copy.start()


    def relays(spot):
        found = []
        for place, origin in ((1, count - 1), (count - 2, 0)):
            end = count - 1 - origin
            step = (end - origin) % count
            found.append(
                (
                    place,
                    origin,
                    pltpu.make_async_remote_copy(
                        src_ref=gathered.at[origin, spot],
                        dst_ref=gathered.at[origin, spot],
                        send_sem=relay_send.at[0],
                        recv_sem=z_recv.at[spot, step - 1],
                        device_id={"video": end},
                        device_id_type=MESH_ID,
                    ),
                )
            )
        return found

    def z_arrival(video, spot, step):
        return pltpu.make_async_remote_copy(
            src_ref=gathered.at[video, spot],
            dst_ref=gathered.at[video, spot],
            send_sem=z_send.at[0],
            recv_sem=z_recv.at[spot, step - 1],
            device_id={"video": video},
            device_id_type=MESH_ID,
        )

    def relay(spot):
        for place, origin, copy in relays(spot):

            @pl.when(v == place)
            def _(copy=copy, origin=origin, place=place):
                z_arrival(origin, spot, (place - origin) % count).wait_recv()
                copy.start()

    backs = []
    owns = []
    half_batches = batches // 2

    def attend(slab):
        query, key, value = (a_rows[slab, kind] for kind in range(3))
        scores = dot_nt(split_heads(query, left_seq), key) * HD ** (-0.5)
        halves = []
        for part in range(2):
            mine_scores = scores[part * seq : (part + 1) * seq] + bias[...]
            top = jnp.max(mine_scores, axis=-1, keepdims=True)
            weights = jnp.exp(mine_scores - top)
            mass = jnp.sum(weights, axis=-1, keepdims=True)
            halves.append(dot_nn(weights.astype(jnp.bfloat16), value) / mass)
        return jnp.where(left_seq, halves[0], halves[1])

    def combine(slab, attended, part):
        rows = slice(part * tok, (part + 1) * tok)
        gate_row = gate_s[:, columns(c, slab)]
        whole = attended[rows] + gate_row * inner[slab, rows]
        comb[slab, rows] = (whole * live[rows]).astype(jnp.bfloat16)

    backs += [
        to_partner(
            comb.at[slab, pl.ds(theirs, tok), :],
            gathered.at[v, c * slabs + slab],
            back_send.at[0],
            back_recv.at[slab],
        )
        for slab in range(slabs)
    ]

    @pl.when(c == 0)
    def _():
        for slab in range(slabs):
            inner_setup(slab, 0)
        for batch in range(half_batches):
            for slab in range(slabs):
                inner_step(slab, batch)

    pass_on(1)
    rate_out.wait_recv()
    for slab in range(slabs):
        rows_in(i_rows, slab, 0)
        if slab == 0:
            pass_on(2)

        @pl.when(c == 1)
        def _(slab=slab):
            inner_setup(slab, 0)
            for batch in range(half_batches):
                inner_step(slab, batch)
            inner_setup(slab, 1)
            inner_step(slab, half_batches)

        @pl.when(c == 0)
        def _(slab=slab):
            inner_setup(slab, 1)
            for batch in range(half_batches, batches):
                inner_step(slab, batch)

        if slab:
            far = other * slabs + slab - 1
            far_out = spread(gathered.at[v, far], far)

            def send_far(far_out=far_out, slab=slab):
                backs[slab - 1].wait_recv()
                launch(far_out)

            pl.when(c == 1)(send_far)
        a_loads[slab].wait()
        rows_in(a_rows, slab, slabs)
        @pl.when(c == 1)
        def _(slab=slab):
            attended = attend(slab)
            combine(slab, attended, 0)
            backs[slab].start()
            for batch in range(half_batches + 1, batches):
                inner_step(slab, batch)
            combine(slab, attended, 1)

        @pl.when(c == 0)
        def _(slab=slab):
            attended = attend(slab)
            combine(slab, attended, 1)
            backs[slab].start()
            combine(slab, attended, 0)

        if slab:
            pl.when(c == 0)(send_far)
        spot = c * slabs + slab
        if slab == 0:
            start_rows(slice(early, slabs))
        own = pltpu.make_async_copy(
            comb.at[slab, pl.ds(mine, tok), :], gathered.at[v, spot], own_sem.at[slab]
        )
        own.start()
        owns.append(own)
        if slab == 0:
            pass_on(3)
        near_out = spread(comb.at[slab, pl.ds(mine, tok), :], spot)
        launch(near_out)
        if slab:
            relay(spot - 1)
        if slab > 1:
            relay(other * slabs + slab - 2)
    ow_load.wait()
    for own in owns[:-1]:
        own.wait()

    chunks, _, _, chunk = parts.shape
    toward = 1 - 2 * (v // (count // 2))
    videos = [lax.rem(v + toward * near + count, count) for near in range(count)]

    def z_wait(video, spots):
        step = lax.rem(v - video + count, count)
        passed = ((v == 1) & (video == count - 1)) | ((v == count - 2) & (video == 0))

        @pl.when(jnp.logical_not(passed))
        def _():
            for spot in spots:
                z_arrival(video, spot, step).wait_recv()

    def rows_of(video, spots):
        return jnp.concatenate([gathered[video, spot] for spot in spots], axis=1)

    first_half = list(range(slabs - 1))
    second_half = list(range(slabs, 2 * slabs - 1))
    last_spots = [slabs - 1, 2 * slabs - 1]

    def begin(near):
        if slabs == 1:
            return
        video = videos[near]
        if near:
            z_wait(video, first_half + second_half)
        sums[near] = dot_nn(
            rows_of(video, first_half), ow[0 : (slabs - 1) * LANE]
        ) + dot_nn(
            rows_of(video, second_half), ow[slabs * LANE : (2 * slabs - 1) * LANE]
        )

    lane_of, core_of = h // 2, lax.rem(h, 2)
    sibling = 2 * lane_of + 1 - core_of
    across = 2 * (1 - lane_of) + core_of

    swapped = lax.rem(v // 2 + v, 2)

    def owner_lane(video):
        return lax.rem(video + v + (1 - video // 2) * swapped, 2)

    def owner_core(video):
        return lax.rem(video // 2 + v // 2, 2)

    def owned(lane, core):
        upper = lax.rem(core + v // 2, 2)
        return 2 * upper + lax.rem(lane + v + (1 - upper) * swapped, 2)

    def to_head_copy(src, dst, send, recv, head):
        return pltpu.make_async_remote_copy(
            src_ref=src,
            dst_ref=dst,
            send_sem=send,
            recv_sem=recv,
            device_id={"head": head},
            device_id_type=MESH_ID,
        )

    def part_copy(video, at):
        slot = lax.rem(owner_lane(video) + lane_of, 2)
        return to_head_copy(
            parts.at[at, video],
            beside.at[at, slot],
            s_send.at[0],
            s_recv.at[at, slot],
            sibling,
        )

    def finish(near):
        video = videos[near]
        if near:
            z_wait(video, last_spots)
        rest = jnp.concatenate(
            [ow[spot * LANE : (spot + 1) * LANE] for spot in last_spots], axis=0
        )
        piece = dot_nn(rows_of(video, last_spots), rest)
        if slabs > 1:
            piece = piece + sums[near]
        piece = piece.astype(jnp.bfloat16)
        for at in range(chunks):
            parts[at, video] = piece[:, at * chunk : (at + 1) * chunk]
            copy = part_copy(video, at)

            @pl.when(owner_core(video) != core_of)
            def _(copy=copy):
                copy.start()

    home, away = owned(lane_of, core_of), owned(1 - lane_of, core_of)
    to_head, to_v = v, home
    stays = (to_head == h) & (to_v == v)
    x_out = [
        to_head_copy(crossing.at[at], arrived.at[at], r_send.at[0], r_recv.at[at], across)
        for at in range(chunks)
    ]
    finals = [
        pltpu.make_async_remote_copy(
            src_ref=total.at[at],
            dst_ref=out.at[0, :, at * chunk : (at + 1) * chunk],
            send_sem=t_send.at[0],
            recv_sem=t_recv.at[0],
            device_id={"head": to_head, "video": to_v},
            device_id_type=MESH_ID,
        )
        for at in range(chunks)
    ]

    kept = [
        pltpu.make_async_copy(
            total.at[at], out.at[0, :, at * chunk : (at + 1) * chunk], t_send.at[0]
        )
        for at in range(chunks)
    ]

    def cross(near):
        @pl.when(videos[near] == away)
        def _():
            for at in range(chunks):
                part_copy(away, at).wait_recv()
                crossing[at] = (
                    parts[at, away].astype(jnp.float32) + beside[at, 1].astype(jnp.float32)
                ).astype(jnp.bfloat16)
                x_out[at].start()

    def arrive(near):
        @pl.when(videos[near] == home)
        def _():
            for at in range(chunks):
                part_copy(home, at).wait_recv()
                x_out[at].wait_recv()
                summed = parts[at, home].astype(jnp.float32) + beside[at, 0].astype(jnp.float32)
                total[at] = (summed + arrived[at].astype(jnp.float32)).astype(jnp.bfloat16)

                @pl.when(stays)
                def _(at=at):
                    kept[at].start()

                @pl.when(jnp.logical_not(stays))
                def _(at=at):
                    finals[at].start()

    begin(0)
    backs[slabs - 1].wait_recv()
    far = other * slabs + slabs - 1
    far_out = spread(gathered.at[v, far], far)
    launch(far_out)
    owns[-1].wait()
    finish(0)
    if slabs > 1:
        relay(far - 1)
    relay(c * slabs + slabs - 1)
    for near in range(1, count):
        begin(near)
    relay(far)
    for near in range(1, count):
        finish(near)
        cross(near - 1)
    cross(count - 1)
    for near in range(count):
        arrive(near)

    rate_out.wait_send()
    in_place(i_rows, y_send.at[0], y_recv.at[0]).wait_send()
    in_place(comb.at[:, 0:tok], back_send.at[0], y_recv.at[0]).wait_send()
    in_place(parts.at[:, 0:2], s_send.at[0], y_recv.at[0]).wait_send()
    in_place(crossing, r_send.at[0], y_recv.at[0]).wait_send()
    at_end = (v == 0) | (v == count - 1)

    @pl.when(at_end)
    def _():
        in_place(gathered.at[0:2], z_send.at[0], y_recv.at[0]).wait_send()

    @pl.when(jnp.logical_not(at_end))
    def _():
        in_place(gathered.at[0:3], z_send.at[0], y_recv.at[0]).wait_send()
        in_place(gathered.at[0], relay_send.at[0], y_recv.at[0]).wait_send()

    finished = in_place(total, t_send.at[0], t_recv.at[0])

    @pl.when(jnp.logical_not(stays))
    def _():
        finished.wait_recv()

    finished.wait_send()


def fused_on_device(
    attention_qkv,
    inner_qkv,
    learn_rate,
    segment_id,
    video_length,
    gate_alpha,
    inner_gain,
    inner_shift,
    first_weight,
    first_bias,
    second_weight,
    second_bias,
    out_weight,
):
    tok = attention_qkv.shape[2]
    width_dev = attention_qkv.shape[3]
    count = lax.axis_size("head")
    ctx_count = lax.axis_size("ctx")
    seq = tok * ctx_count
    slabs = width_dev // LANE // ctx_count
    heads = width_dev // HD
    hidden = first_weight.shape[2]
    columns = out_weight.shape[1]
    chunk = LANE
    chunks = columns // chunk
    half = jnp.bfloat16
    full = jnp.float32
    hbm = pl.BlockSpec(memory_space=pl.ANY)
    dma = pltpu.SemaphoreType.DMA
    return pl.pallas_call(
        fused_kernel,
        out_shape=pltpu.VMEM((1, tok, columns), half),
        in_specs=[hbm] * 13,
        out_specs=hbm,
        scratch_shapes=[
            pltpu.VMEM(segment_id.shape, segment_id.dtype),
            pltpu.SMEM(video_length.shape, video_length.dtype),
            pltpu.VMEM(gate_alpha.shape, full),
            pltpu.VMEM(inner_gain.shape, full),
            pltpu.VMEM(inner_shift.shape, full),
            pltpu.VMEM(first_bias.shape, full),
            pltpu.VMEM(second_bias.shape, full),
            dma((7,)),
            pltpu.VMEM((slabs, 3, seq, LANE), half),
            pltpu.VMEM((slabs, 3, seq, LANE), half),
            pltpu.VMEM((ctx_count, heads, 1, tok), full),
            pltpu.VMEM((2 * slabs,) + first_weight.shape[1:], half),
            pltpu.VMEM((2 * slabs,) + second_weight.shape[:0:-1], half),
            pltpu.VMEM(out_weight.shape, half),
            pltpu.VMEM((slabs, 2, 2 * seq, seq), half),
            pltpu.VMEM((slabs, 2, seq, hidden), half),
            pltpu.VMEM((slabs, LANE, hidden), full),
            pltpu.VMEM((slabs, seq // MB, LANE, hidden), half),
            pltpu.VMEM((slabs, 2, 1, hidden), full),
            pltpu.VMEM((slabs, seq // MB, 1, LANE), full),
            pltpu.VMEM((1, width_dev), full),
            pltpu.VMEM((slabs, 1, LANE), full),
            pltpu.VMEM((slabs, 1, LANE), full),
            pltpu.VMEM((slabs, seq, LANE), full),
            pltpu.VMEM((LANE, LANE), half),
            pltpu.VMEM((LANE, LANE), half),
            pltpu.VMEM((LANE, LANE), full),
            pltpu.VMEM((seq, seq), full),
            pltpu.VMEM((slabs, seq, LANE), full),
            pltpu.VMEM((slabs, seq, LANE), full),
            pltpu.VMEM((slabs, LANE, LANE), half),
            pltpu.VMEM((slabs, seq // MB, LANE, hidden), half),
            pltpu.VMEM((slabs, seq // MB, LANE, LANE), half),
            pltpu.VMEM((slabs, seq, LANE), full),
            pltpu.VMEM((slabs, seq, LANE), half),
            pltpu.VMEM((count, 2 * slabs, tok, LANE), half),
            pltpu.VMEM((count, tok, columns), full),
            pltpu.VMEM((chunks, count, tok, chunk), half),
            pltpu.VMEM((chunks, 2, tok, chunk), half),
            pltpu.VMEM((chunks, tok, chunk), half),
            pltpu.VMEM((chunks, tok, chunk), half),
            pltpu.VMEM((chunks, tok, chunk), half),
            dma((2 * slabs + 4,)),
            dma((2,)),
            dma((2 * slabs + 1,)),
            dma((1,)),
            dma((slabs,)),
            dma((1,)),
            dma((2 * slabs, count - 1)),
            dma((1,)),
            dma((slabs,)),
            dma((1,)),
            dma((chunks, 2)),
            dma((1,)),
            dma((chunks,)),
            dma((1,)),
            dma((1,)),
            pltpu.SemaphoreType.REGULAR,
            pltpu.SemaphoreType.REGULAR,
        ],
        compiler_params=pltpu.CompilerParams(
            collective_id=0, has_side_effects=True, vmem_limit_bytes=60 * 1024 * 1024
        ),
    )(
        attention_qkv,
        inner_qkv,
        learn_rate.transpose(1, 0, 2),
        first_weight,
        second_weight.transpose(0, 2, 1),
        out_weight,
        segment_id,
        video_length,
        gate_alpha,
        inner_gain,
        inner_shift,
        first_bias,
        second_bias,
    )


def general_on_device(
    attention_qkv,
    inner_qkv,
    learn_rate,
    segment_id,
    video_length,
    gate_alpha,
    inner_gain,
    inner_shift,
    first_weight,
    first_bias,
    second_weight,
    second_bias,
    out_weight,
):
    tok_count = attention_qkv.shape[2]
    width_dev = attention_qkv.shape[3]
    heads_dev = width_dev // HD
    ctx_index = lax.axis_index("ctx")
    ctx_count = lax.axis_size("ctx")
    positions = ctx_index * tok_count + jnp.arange(tok_count, dtype=jnp.int32)
    length_val = video_length[0]
    live_rows = (positions < length_val).astype(jnp.float32)
    kv_pair = attention_qkv[1:, 0]
    kv_wide = with_halo(kv_pair, (("ctx", 1),), tok_count)
    key_pos = (ctx_index - 1) * tok_count + jnp.arange(3 * tok_count, dtype=jnp.int32)
    seg_row = segment_id[0]
    fill_ids = jnp.full((tok_count,), -1, jnp.int32)
    seg_pad = jnp.concatenate([fill_ids, seg_row, fill_ids])
    key_seg = lax.dynamic_slice_in_dim(seg_pad, ctx_index * tok_count, 3 * tok_count, 0)
    query_seg = lax.dynamic_slice_in_dim(seg_row, ctx_index * tok_count, tok_count, 0)
    allowed = (key_seg[None, :] == query_seg[:, None]) & (
        (key_pos[None, :] < length_val) | (key_pos[None, :] == positions[:, None])
    )
    query_heads = attention_qkv[0, 0].reshape(tok_count, heads_dev, HD)
    key_heads = kv_wide[0].reshape(3 * tok_count, heads_dev, HD)
    value_heads = kv_wide[1].reshape(3 * tok_count, heads_dev, HD)
    scores = jnp.einsum(
        "qhd,khd->hqk", query_heads, key_heads, preferred_element_type=jnp.float32
    ) * HD ** (-0.5)
    scores = jnp.where(allowed[None], scores, -1e30)
    row_max = jnp.max(scores, axis=-1, keepdims=True)
    exp_scores = jnp.exp(scores - row_max)
    soft_weights = (exp_scores / jnp.sum(exp_scores, axis=-1, keepdims=True)).astype(jnp.bfloat16)
    attended = jnp.einsum(
        "hqk,khd->qhd", soft_weights, value_heads, preferred_element_type=jnp.float32
    ).reshape(tok_count, width_dev)
    init_state = (
        first_weight.astype(jnp.float32),
        first_bias,
        second_weight.astype(jnp.float32),
        second_bias,
    )
    rate_rows = learn_rate[0] * live_rows[None, :]
    heads_each = -(-heads_dev // ctx_count)
    heads_padded = heads_each * ctx_count
    rows_heads = inner_qkv[:, 0].reshape(3, tok_count, heads_dev, HD)
    rows_padded = jnp.concatenate(
        [rows_heads, jnp.zeros((3, tok_count, heads_padded - heads_dev, HD), rows_heads.dtype)],
        axis=2,
    )
    rates_padded = pad_heads(rate_rows, heads_padded, 0.0)
    whole_rows = lax.all_to_all(rows_padded, "ctx", split_axis=2, concat_axis=1, tiled=True)
    whole_rates = lax.all_to_all(rates_padded, "ctx", split_axis=0, concat_axis=1, tiled=True)
    seq_count = whole_rows.shape[1]
    full_batches = seq_count // MB
    local_qkv = (
        whole_rows.astype(jnp.float32)
        .transpose(0, 2, 1, 3)
        .reshape(3, heads_each, full_batches, MB, HD)
    )
    local_rates = whole_rates.reshape(heads_each, full_batches, MB)
    first_head = ctx_index * heads_each
    local_gain = lax.dynamic_slice_in_dim(
        pad_heads(inner_gain, heads_padded, 1.0), first_head, heads_each, 0
    )
    local_shift = lax.dynamic_slice_in_dim(
        pad_heads(inner_shift, heads_padded, 0.0), first_head, heads_each, 0
    )
    local_state = tuple(
        (
            lax.dynamic_slice_in_dim(
                pad_heads(piece_arr, heads_padded, 0.0), first_head, heads_each, 0
            )
            for piece_arr in init_state
        )
    )
    unused_final, saved_local = jax.vmap(partial(chain_scan, True))(
        local_state, local_qkv[0], local_qkv[1], local_qkv[2], local_rates, local_gain, local_shift
    )
    out_rows = saved_local.reshape(heads_each, seq_count, HD).transpose(1, 0, 2)
    back_rows = lax.all_to_all(
        out_rows.astype(jnp.bfloat16), "ctx", split_axis=0, concat_axis=1, tiled=True
    ).astype(out_rows.dtype)
    inner_flat = back_rows[:, :heads_dev].reshape(tok_count, width_dev)
    combined = ((attended + jnp.tanh(gate_alpha) * inner_flat) * live_rows[:, None]).astype(
        jnp.bfloat16
    )
    terms = jnp.dot(
        combined,
        lax.all_gather(out_weight, "video", axis=1, tiled=True),
        preferred_element_type=jnp.float32,
    )
    mixed = lax.psum_scatter(terms.astype(jnp.bfloat16), "head", scatter_dimension=1, tiled=True)
    return mixed[None]


def solution(mesh):
    placed = (
        P(None, "video", "ctx", "head"),
        P(None, "video", "ctx", "head"),
        P("video", "head", "ctx"),
        P("video", None),
        P("video"),
        P("head"),
        P("head", None),
        P("head", None),
        P("head", None, None),
        P("head", None),
        P("head", None, None),
        P("head", None),
        P("head", "video"),
    )
    shape = mesh.shape
    fused = shape["ctx"] == 2 and shape["head"] == shape["video"] == 4

    def on_device(*args):
        heads_dev = args[0].shape[3] // HD
        if fused and heads_dev % (2 * shape["ctx"]) == 0 and args[0].shape[2] % 128 == 0:
            return fused_on_device(*args)
        return general_on_device(*args)

    return jax.shard_map(
        on_device, mesh=mesh, in_specs=placed, out_specs=P("video", "ctx", "head"), check_vma=False
    )
```
